128 devices in a mesh: sy: 8 (over x, y_lo), sz: 16 (over z, y_hi, core).
Axes of the slice: x: 4, y: 4 (y_hi: 2, y_lo: 2; y = y_hi * 2 + y_lo), z: 4, core: 2. Of those that a mesh axis runs over, the one named last changes fastest.
Arguments:
- labels: int32 [16, 512, 512], P(None, 'sy', 'sz'), may hold values from 0 to 3
- wall_dist: bfloat16 [16, 512, 512], P(None, 'sy', 'sz'), may hold values from -5 to 5
- material_table: bfloat16 [4, 16], replicated, may hold values from -4 to 4
- dist_weight: bfloat16 [16], replicated, may hold values from -4 to 4
- conv_weight: bfloat16 [27, 16, 16], replicated, may hold values from -0.3125 to 0.3125
- down_weight: bfloat16 [8, 64, 16], replicated, may hold values from -0.5 to 0.5
- mix_weight: bfloat16 [64, 256, 256], P('sz'), may hold values from -0.375 to 0.375
- cotangent: bfloat16 [64, 8, 256, 256], P('sz', None, 'sy'), may hold values from -6 to 6
Outputs:
- mid_features: bfloat16 [64, 8, 256, 256], P('sz', None, 'sy')
- mix_grad: float32 [64, 256, 256], P('sz', 'sy')
- down_grad: float32 [8, 64, 16], replicated
- conv_grad: float32 [27, 16, 16], replicated
The draws below stay inside these ranges and needn't reach their ends.
All inputs are finite; a program needn't handle non-finite values.
Results may differ from the reference program's by a relative error of at most 0.0084.
Values may be sent and summed in bfloat16 or wider, within the bound.
No kernel may reach another device: no remote copies, remote signals or barrier semaphores. Data moves between devices by JAX's collectives and lax.ppermute only.
A program may use at most 192 MiB of HBM per device.

```python
import math
import jax
import jax.numpy as jnp
from jax import lax

C1 = 16
C2 = 64
NMAT = 4
XD = 16
NY = 512
NZ = 512
X2 = 8
NY2 = 256
NZ2 = 256


def touch_ends(values, stream_key, smallest, largest):
    dims = values.shape
    index_at = [jax.random.randint(jax.random.fold_in(stream_key, axis), (), 0, dims[axis]) for axis in range(len(dims))]
    values = values.at[tuple(index_at)].set(smallest)
    longest = dims.index(max(dims))
    index_at[longest] = (index_at[longest] + 1) % dims[longest]
    return values.at[tuple(index_at)].set(largest)


def steps_of(key, shape, cuts, least, top_value):
    def one(axis_at, parts):
        draws = jax.random.uniform(jax.random.fold_in(jax.random.fold_in(key, 6), axis_at), (parts,), jnp.float32, least / len(cuts), top_value / len(cuts))
        return jnp.repeat(jnp.exp(draws), shape[axis_at] // parts).reshape((-1,) + (1,) * (len(shape) - axis_at - 1))

    loudness = one(*cuts[0])
    for cut in cuts[1:]:
        loudness = loudness * one(*cut)
    return loudness


def gaussian(rng, extent, width, bound, pieces=(), kind=jnp.bfloat16):
    entries = jax.random.normal(rng, extent, jnp.float32) * width
    if len(pieces) > 0:
        entries = steps_of(rng, extent, pieces, -0.22, 0.18) * entries
    return jnp.clip(entries, min=-bound, max=bound).astype(kind)


def setup_inputs(seed: int = 0) -> dict:
    arg_keys = jax.random.split(jax.random.key(seed), 9)
    return {
        "labels": touch_ends(jax.random.randint(arg_keys[0], (XD, NY, NZ), 0, NMAT), jax.random.fold_in(arg_keys[0], 1), 0, NMAT - 1).astype(jnp.int32),
        "wall_dist": gaussian(arg_keys[1], (XD, NY, NZ), 1.0, 5.0, ((1, 8), (2, 16))),
        "material_table": gaussian(arg_keys[2], (NMAT, C1), 1.0, 4.0),
        "dist_weight": gaussian(arg_keys[3], (C1,), 1.0, 4.0),
        "conv_weight": gaussian(arg_keys[4], (27, C1, C1), (27 * C1) ** -0.5, 0.3125),
        "down_weight": gaussian(arg_keys[5], (8, C2, C1), (8 * C1) ** -0.5, 0.5),
        "mix_weight": gaussian(arg_keys[6], (C2, NZ2, NZ2), NZ2 ** -0.5, 0.375, ((0, 16),)),
        "cotangent": gaussian(arg_keys[7], (C2, X2, NY2, NZ2), 1.0, 6.0, ((0, 16), (2, 8))),
    }


def silu_slope(values):
    sigma = jax.nn.sigmoid(values)
    return sigma * (1.0 + values * (1.0 - sigma))

def conv_first(embedded_f, kernel_taps):
    kernel = jnp.transpose(kernel_taps.reshape(3, 3, 3, C1, C1), (3, 4, 0, 1, 2))
    result = lax.conv_general_dilated(embedded_f[None], kernel, (1, 1, 1), ((1, 1), (1, 1), (1, 1)), dimension_numbers=('NCDHW', 'OIDHW', 'NCDHW'), precision=lax.Precision.HIGHEST)
    return result[0]

def reference(labels, wall_dist, material_table, dist_weight, conv_weight, down_weight, mix_weight, cotangent):
    looked = jnp.transpose(material_table.astype(jnp.float32)[labels], (3, 0, 1, 2))
    embedded = (looked + dist_weight.astype(jnp.float32)[:, None, None, None] * wall_dist.astype(jnp.float32)[None]).astype(jnp.bfloat16)
    embedded_f = embedded.astype(jnp.float32)
    pre_act, pullback = jax.vjp(lambda kernel_taps: conv_first(embedded_f, kernel_taps), conv_weight.astype(jnp.float32))
    hidden = jax.nn.silu(pre_act).astype(jnp.bfloat16)
    hidden_r = hidden.astype(jnp.float32).reshape(C1, X2, 2, NY2, 2, NZ2, 2)
    down_r = down_weight.astype(jnp.float32).reshape(2, 2, 2, C2, C1)
    coarse = jnp.einsum('abcoi,ixaybzc->oxyz', down_r, hidden_r).astype(jnp.bfloat16)
    coarse_f = coarse.astype(jnp.float32)
    mix_f = mix_weight.astype(jnp.float32)
    mixed_pre = jnp.einsum('czw,cxyw->cxyz', mix_f, coarse_f)
    mid_features = jax.nn.silu(mixed_pre).astype(jnp.bfloat16)
    mixed_grad = (cotangent.astype(jnp.float32) * silu_slope(mixed_pre)).astype(jnp.bfloat16)
    mixed_grad_f = mixed_grad.astype(jnp.float32)
    mix_grad = jnp.einsum('cxyz,cxyw->czw', mixed_grad_f, coarse_f) / math.sqrt(X2 * NY2)
    coarse_grad = jnp.einsum('czw,cxyz->cxyw', mix_f, mixed_grad_f).astype(jnp.bfloat16)
    coarse_grad_f = coarse_grad.astype(jnp.float32)
    down_grad = jnp.einsum('oxyz,ixaybzc->abcoi', coarse_grad_f, hidden_r).reshape(8, C2, C1) / math.sqrt(X2 * NY2 * NZ2)
    hidden_grad = jnp.einsum('abcoi,oxyz->ixaybzc', down_r, coarse_grad_f).reshape(C1, XD, NY, NZ)
    pre_grad = (hidden_grad * silu_slope(pre_act)).astype(jnp.bfloat16)
    conv_grad = pullback(pre_grad.astype(jnp.float32))[0] / math.sqrt(XD * NY * NZ)
    return (mid_features, mix_grad, down_grad, conv_grad)
```

```python
import math

import jax
import jax.numpy as jnp
from jax import lax
from jax.experimental import pallas as pl
from jax.experimental.pallas import tpu as pltpu
from jax.sharding import PartitionSpec as P

F32 = jnp.float32
BF16 = jnp.bfloat16
VMEM = pl.BlockSpec(memory_space=pltpu.VMEM)


def dot(a, b, ca, cb):
    return lax.dot_general(a, b, (((ca,), (cb,)), ((), ())), preferred_element_type=F32)


def iota(shape, dim):
    return lax.broadcasted_iota(jnp.int32, shape, dim)


def feature_kernel(lab_ref, wd_ref, out_ref, lab_s, wd_s):
    lab_s[...] = lab_ref[...]
    wd_s[...] = wd_ref[...].astype(F32)
    row = iota((128, 64), 0)
    run, r = row // 32, row % 32
    y = jnp.where(run == 0, 2 * r, jnp.where(run == 1, 2 * r + 1, jnp.where(run == 2, 2 * r - 1, 2 * r + 2)))
    pick = (y == iota((128, 64), 1)).astype(BF16)
    for z in range(out_ref.shape[0]):
        lab = lab_s[:, z, :]
        parts = [(lab == m).astype(F32).astype(BF16) for m in range(4)]
        parts.append(wd_s[:, z, :].astype(BF16))
        out_ref[z] = dot(pick, jnp.concatenate(parts, axis=0), 1, 1).astype(BF16)


def weight_kernel(conv_ref, down_ref, emb_ref, band_ref, dband_ref, table_ref):
    spread = (iota((256, 16), 0) % 16 == iota((256, 16), 1)).astype(BF16)
    wide = dot(spread, conv_ref[...], 1, 0).astype(BF16)
    offset = iota((256, 256), 0) // 16 - iota((256, 256), 1) // 16 + 1
    for t in range(9):
        total = jnp.zeros((256, 256), F32)
        for tx in range(3):
            at = (tx * 9 + t) * 16
            tile = dot(wide[:, at : at + 16], spread, 1, 1)
            total = jnp.where(offset == tx, tile, total)
        band_ref[t] = total.astype(BF16)
    lane_x = iota((64, 256), 1) // 16
    for bc in range(4):
        tiles = [dot(down_ref[4 * a + bc], spread, 0, 1) for a in range(2)]
        both = jnp.where(lane_x % 2 == 0, tiles[0], tiles[1])
        for x2 in range(8):
            dband_ref[bc, 64 * x2 : 64 * x2 + 64, :] = jnp.where(lane_x // 2 == x2, both, 0.0).astype(BF16)
    lane_e = iota((16, 256), 1) // 16
    row_e = iota((16, 256), 0)
    rows = dot(emb_ref[...], spread, 1, 1)
    for m in range(5):
        line = jnp.broadcast_to(rows[m : m + 1, :], (16, 256))
        table_ref[16 * m : 16 * m + 16, :] = jnp.where(lane_e == row_e, line, 0.0).astype(BF16)


def forward_kernel(
    feat_ref, zlo_ref, zhi_ref, ylo_ref, yhi_ref, table_ref, band_ref, dband_ref,
    emb_ref, slope_ref, hidden_ref, coarse_ref, turn_a, turn_b,
):
    table = table_ref[...]
    row = iota((128, 80), 0)
    emb_ref[0] = dot(zlo_ref[...], table, 1, 0).astype(BF16)
    emb_ref[33] = dot(zhi_ref[...], table, 1, 0).astype(BF16)
    ylo = ylo_ref[...].astype(F32)
    yhi = yhi_ref[...].astype(F32)
    for z in range(32):
        f = feat_ref[z].astype(F32)
        f = jnp.where(row == 64, ylo[z : z + 1, :], f)
        f = jnp.where(row == 127, yhi[z : z + 1, :], f)
        emb_ref[z + 1] = dot(f.astype(BF16), table, 1, 0).astype(BF16)
    chunk = 8
    for b in range(2):
        runs = (2, 0, 1) if b == 0 else (0, 1, 3)
        for z0 in range(0, 32, chunk):
            acc = None
            for ty in range(3):
                for tz in range(3):
                    run = 32 * runs[ty]
                    rows = emb_ref[z0 + tz : z0 + tz + chunk, run : run + 32, :].reshape(32 * chunk, 256)
                    part = dot(rows, band_ref[3 * ty + tz], 1, 0)
                    acc = part if acc is None else acc + part
            sigma = jax.nn.sigmoid(acc)
            hid = (acc * sigma).astype(BF16).reshape(chunk, 32, 256)
            slope = (sigma * (1.0 + acc * (1.0 - sigma))).reshape(chunk, 32, 256)
            for k in range(chunk):
                z2, c = (z0 + k) // 2, k % 2
                hidden_ref[2 * b + c, 32 * z2 : 32 * z2 + 32, :] = hid[k]
                slope_ref[2 * b + c, 32 * z2 : 32 * z2 + 32, :] = slope[k]
    for x2 in range(8):
        at = slice(64 * x2, 64 * x2 + 64)
        acc = None
        for bc in range(4):
            part = dot(dband_ref[bc, at, :], hidden_ref[bc], 1, 1)
            acc = part if acc is None else acc + part
        turn_a[at, :] = acc
    for z2 in range(16):
        for half in range(2):
            pieces = [
                turn_a[64 * x2 : 64 * x2 + 64, 32 * z2 : 32 * z2 + 32]
                for x2 in range(4 * half, 4 * half + 4)
            ]
            turn_b[half, pl.ds(z2, 64, stride=16), :] = jnp.concatenate(pieces, axis=1)
    for half in range(2):
        coarse_ref[:, 128 * half : 128 * half + 128] = turn_b[half].astype(BF16)


def mix_kernel(scale, coarse_ref, mix_ref, cot_ref, mid_ref, mixg_ref, grad_ref):
    width = mix_ref.shape[1]
    coarse = coarse_ref[...].reshape(width, 256)
    mix = mix_ref[0]
    flat = coarse.T
    pre = dot(flat, mix, 1, 1)
    sigma = jax.nn.sigmoid(pre)
    mid_ref[0] = (pre * sigma).astype(BF16)
    grad = (cot_ref[0].astype(F32) * (sigma * (1.0 + pre * (1.0 - sigma)))).astype(BF16)
    turned = grad.T
    mixg_ref[0] = dot(turned, flat, 1, 0) * scale
    out = dot(mix.T, turned, 1, 0)
    grad_ref[...] = out.astype(BF16).reshape(grad_ref.shape)


def fold(value, step):
    lanes = value.shape[-1]
    if lanes == 256:
        value = value[:, :128] + value[:, 128:]
    shift = 64
    while shift >= step:
        value = value + pltpu.roll(value, shift, 1)
        shift //= 2
    return value


def backward_kernel(
    down_scale, conv_scale, cgrad_ref, emb_ref, slope_ref, hidden_ref, dband_ref,
    out_ref, turn_a, turn_b, turned_pg,
):
    for half in range(2):
        turn_b[half] = cgrad_ref[:, 128 * half : 128 * half + 128].astype(F32)
    for half in range(2):
        for quad in range(4):
            pieces = [turn_b[half, pl.ds(4 * quad + k, 64, stride=16), :] for k in range(4)]
            for k in range(4):
                x2 = 4 * half + k
                turn_a[64 * x2 : 64 * x2 + 64, 128 * quad : 128 * quad + 128] = jnp.concatenate(
                    [p[:, 32 * k : 32 * k + 32] for p in pieces], axis=1
                )
    cg_t = turn_a[...].astype(BF16)
    cg = cg_t.T
    lane = iota((64, 256), 1)
    low = iota((64, 128), 1)
    down = jnp.zeros((64, 128), F32)
    for bc in range(4):
        total = jnp.zeros((64, 256), F32)
        for x2 in range(8):
            part = dot(cg_t[64 * x2 : 64 * x2 + 64, :], hidden_ref[bc], 1, 0)
            total = jnp.where(lane // 32 == x2, part, total)
        down = jnp.where(low // 32 == bc, fold(total, 32), down)
    out_ref[0:64, :] = down * down_scale
    for bc in range(4):
        hgrad = dot(cg, dband_ref[bc], 1, 0)
        pgrad = (hgrad * slope_ref[bc]).astype(BF16)
        turned_pg[bc] = pgrad.T
    lane_x = iota((16, 256), 1) // 16
    group = iota((16, 128), 1) // 16
    blocks = [jnp.zeros((16, 128), F32) for _ in range(4)]
    for ty in range(3):
        for tz in range(3):
            acc = None
            for bc in range(4):
                b, c = bc // 2, bc % 2
                run = 32 * ((2, 0, 1) if b == 0 else (0, 1, 3))[ty]
                q, p = (c + tz) // 2, (c + tz) % 2
                rows = emb_ref[q : q + 16, p, run : run + 32, :].reshape(512, 256)
                part = dot(turned_pg[bc], rows, 1, 0)
                acc = part if acc is None else acc + part
            for tx in range(3):
                total = jnp.zeros((16, 256), F32)
                for x in range(16):
                    if 0 <= x + tx - 1 < 16:
                        total = jnp.where(lane_x == x + tx - 1, acc[16 * x : 16 * x + 16, :], total)
                tap = 9 * tx + 3 * ty + tz
                blocks[tap // 8] = jnp.where(group == tap % 8, fold(total, 16), blocks[tap // 8])
    for k in range(4):
        out_ref[64 + 16 * k : 80 + 16 * k, :] = blocks[k] * conv_scale


def params(mib):
    return pltpu.CompilerParams(vmem_limit_bytes=mib << 20)


def cost(flops, nbytes):
    return pl.CostEstimate(flops=flops, bytes_accessed=nbytes, transcendentals=0)


def shape(dims, dtype):
    return jax.ShapeDtypeStruct(dims, dtype)


def sum_everywhere(value, axes):
    for axis in axes:
        size = lax.axis_size(axis)
        step = 1
        while step < size:
            value = value + lax.ppermute(value, axis, [(i, i ^ step) for i in range(size)])
            step *= 2
    return value


def per_device(
    labels, wall_dist, material_table, dist_weight, conv_weight, down_weight, mix_weight, cotangent
):
    count_y = lax.axis_size("sy")
    count_z = lax.axis_size("sz")
    mine = 64 // count_z
    width = mix_weight.shape[1]
    features = pl.pallas_call(
        feature_kernel,
        out_shape=shape((32, 128, 80), BF16),
        in_specs=[VMEM] * 2,
        out_specs=VMEM,
        scratch_shapes=[pltpu.VMEM((16, 32, 64), jnp.int32), pltpu.VMEM((16, 32, 64), F32)],
        compiler_params=params(16),
        cost_estimate=cost(32 * 128 * 64 * 80 * 2, 2 << 20),
        name="features",
    )(jnp.transpose(labels, (0, 2, 1)), jnp.transpose(wall_dist, (0, 2, 1)))
    up_y = [(i, i + 1) for i in range(count_y - 1)]
    up_z = [(i, i + 1) for i in range(count_z - 1)]
    ylo = lax.ppermute(features[:, 63, :], "sy", up_y)
    yhi = lax.ppermute(features[:, 0, :], "sy", [(j, i) for i, j in up_y])

    def whole(z):
        row = lax.broadcasted_iota(jnp.int32, (128, 80), 0)
        face = jnp.where(row == 64, ylo[z][None], features[z])
        return jnp.where(row == 127, yhi[z][None], face)

    zlo = lax.ppermute(whole(31), "sz", up_z)
    zhi = lax.ppermute(whole(0), "sz", [(j, i) for i, j in up_z])

    flat_conv = jnp.transpose(conv_weight, (2, 0, 1)).reshape(16, 432)
    rows = jnp.concatenate([material_table, dist_weight[None], jnp.zeros((3, 16), BF16)], axis=0)
    band, dband, table = pl.pallas_call(
        weight_kernel,
        out_shape=(shape((9, 256, 256), BF16), shape((4, 512, 256), BF16), shape((80, 256), BF16)),
        in_specs=[VMEM] * 3,
        out_specs=(VMEM,) * 3,
        compiler_params=params(16),
        cost_estimate=cost(27 * 256 * 16 * 256 * 2, 3 << 20),
        name="weights",
    )(flat_conv, jnp.transpose(down_weight, (0, 2, 1)), rows)

    embedded, slope, hidden, coarse = pl.pallas_call(
        forward_kernel,
        out_shape=(
            shape((34, 128, 256), BF16),
            shape((4, 512, 256), F32),
            shape((4, 512, 256), BF16),
            shape((1024, 256), BF16),
        ),
        in_specs=[VMEM] * 8,
        out_specs=(VMEM,) * 4,
        scratch_shapes=[pltpu.VMEM((512, 512), F32), pltpu.VMEM((2, 1024, 128), F32)],
        compiler_params=params(32),
        cost_estimate=cost(3 << 30, 10 << 20),
        name="forward",
    )(features, zlo, zhi, ylo, yhi, table, band, dband)

    sent = lax.all_to_all(
        coarse.reshape(count_z, mine * 16, 256), "sz", split_axis=0, concat_axis=0, tiled=True
    )
    block = lambda *dims: pl.BlockSpec(dims, lambda c: (c,) + (0,) * (len(dims) - 1))
    mid, mix_partial, back = pl.pallas_call(
        lambda *refs: mix_kernel(1.0 / math.sqrt(8 * 32 * count_y), *refs),
        grid=(mine,),
        out_shape=(
            shape((mine, 256, width), BF16),
            shape((mine, width, width), F32),
            shape((count_z, mine * 16, 256), BF16),
        ),
        in_specs=[
            pl.BlockSpec((count_z, 16, 256), lambda c: (0, c, 0)),
            block(1, width, width),
            block(1, 256, width),
        ],
        out_specs=(
            block(1, 256, width),
            block(1, width, width),
            pl.BlockSpec((count_z, 16, 256), lambda c: (0, c, 0)),
        ),
        compiler_params=params(16),
        cost_estimate=cost(mine * 3 * 2 * 256 * width * width, 5 << 20),
        name="mix",
    )(sent, mix_weight, cotangent.reshape(mine, 256, width))
    coarse_grad = lax.all_to_all(back, "sz", split_axis=0, concat_axis=0, tiled=True)
    mix_grad = lax.psum_scatter(mix_partial, "sy", scatter_dimension=1, tiled=True)

    cells = 16 * 64 * count_y * 32 * count_z
    sums = pl.pallas_call(
        lambda *refs: backward_kernel(
            1.0 / math.sqrt(cells // 8), 1.0 / math.sqrt(cells), *refs
        ),
        out_shape=shape((128, 128), F32),
        in_specs=[VMEM] * 5,
        out_specs=VMEM,
        scratch_shapes=[
            pltpu.VMEM((512, 512), F32),
            pltpu.VMEM((2, 1024, 128), F32),
            pltpu.VMEM((4, 256, 512), BF16),
        ],
        compiler_params=params(32),
        cost_estimate=cost(4 << 30, 8 << 20),
        name="backward",
    )(coarse_grad.reshape(1024, 256), embedded.reshape(17, 2, 128, 256), slope, hidden, dband)
    sums = sum_everywhere(sums, ("sz", "sy"))
    down_grad = jnp.transpose(sums[:64].reshape(64, 4, 2, 16), (2, 1, 0, 3)).reshape(8, 64, 16)
    conv_grad = jnp.transpose(sums[64:].reshape(4, 16, 8, 16), (0, 2, 1, 3)).reshape(32, 16, 16)[:27]
    return (mid.reshape(cotangent.shape), mix_grad, down_grad, conv_grad)


def solution(mesh):
    in_specs = (
        P(None, "sy", "sz"),
        P(None, "sy", "sz"),
        P(),
        P(),
        P(),
        P(),
        P("sz", None, None),
        P("sz", None, "sy", None),
    )
    out_specs = (P("sz", None, "sy", None), P("sz", "sy", None), P(), P())
    return jax.shard_map(
        per_device, mesh=mesh, in_specs=in_specs, out_specs=out_specs, check_vma=False
    )
```

```python
import math

import jax
import jax.numpy as jnp
from jax import lax
from jax.experimental import pallas as pl
from jax.experimental.pallas import tpu as pltpu
from jax.sharding import PartitionSpec as P

F32 = jnp.float32
BF16 = jnp.bfloat16
VMEM = pl.BlockSpec(memory_space=pltpu.VMEM)
HBM = pl.BlockSpec(memory_space=pltpu.HBM)
RUNS = ((64, 0, 32), (0, 32, 96))


def dot(a, b, ca, cb):
    return lax.dot_general(a, b, (((ca,), (cb,)), ((), ())), preferred_element_type=F32)


def iota(shape, dim):
    return lax.broadcasted_iota(jnp.int32, shape, dim)


def fetch(sources, targets, sem):
    copies = [pltpu.make_async_copy(a, b, sem.at[k]) for k, (a, b) in enumerate(zip(sources, targets))]
    for copy in copies:
        copy.start()
    return copies


def feature_kernel(lab_hbm, wd_hbm, out_ref, first_ref, last_ref, lab_s, wd_b, wd_s, first_s, last_s, sem):
    copies = fetch((lab_hbm, wd_hbm), (lab_s, wd_b), sem)
    row = iota((128, 64), 0)
    run, r = row // 32, row % 32
    y = jnp.where(run == 0, 2 * r, jnp.where(run == 1, 2 * r + 1, jnp.where(run == 2, 2 * r - 1, 2 * r + 2)))
    pick = (y == iota((128, 64), 1)).astype(BF16)
    for copy in copies:
        copy.wait()
    wd_s[...] = wd_b[...].astype(F32)
    for z in range(out_ref.shape[0]):
        lab = lab_s[:, z, :]
        parts = [(lab == m).astype(F32).astype(BF16) for m in range(4)]
        parts.append(wd_s[:, z, :].astype(BF16))
        rows = dot(pick, jnp.concatenate(parts, axis=0), 1, 1)
        out_ref[z] = rows.astype(BF16)
        first_s[z : z + 1, :] = rows[0:1, :]
        last_s[z : z + 1, :] = rows[63:64, :]
    first_ref[...] = first_s[...].astype(BF16)
    last_ref[...] = last_s[...].astype(BF16)


def weight_kernel(
    conv_hbm, down_hbm, mat_hbm, dist_hbm, band_ref, dband_ref, table_ref,
    conv_ref, down_ref, mat_ref, dist_ref, sem,
):
    copies = fetch(
        (conv_hbm, down_hbm, mat_hbm, dist_hbm), (conv_ref, down_ref, mat_ref, dist_ref), sem
    )
    for copy in copies:
        copy.wait()
    spread = (iota((256, 16), 0) % 16 == iota((256, 16), 1)).astype(BF16)
    taps = conv_ref[...].reshape(256, 27)
    repeat = (iota((27, 432), 0) == iota((27, 432), 1) // 16).astype(BF16)
    own = iota((256, 432), 0) // 16 == iota((256, 432), 1) % 16
    apart = jnp.where(own, dot(taps, repeat, 1, 0), 0.0).astype(BF16)
    gather = (iota((256, 256), 0) % 16 == iota((256, 256), 1) % 16).astype(BF16)
    wide = dot(gather, apart, 1, 0).astype(BF16)
    offset = iota((256, 256), 0) // 16 - iota((256, 256), 1) // 16 + 1
    for t in range(9):
        total = jnp.zeros((256, 256), F32)
        for tx in range(3):
            at = (tx * 9 + t) * 16
            tile = dot(wide[:, at : at + 16], spread, 1, 1)
            total = jnp.where(offset == tx, tile, total)
        band_ref[t] = total.astype(BF16)
    lane_x = iota((64, 256), 1) // 16
    for bc in range(4):
        tiles = [dot(down_ref[4 * a + bc], spread, 0, 1) for a in range(2)]
        both = jnp.where(lane_x % 2 == 0, tiles[0], tiles[1])
        for x2 in range(8):
            dband_ref[bc, 64 * x2 : 64 * x2 + 64, :] = jnp.where(lane_x // 2 == x2, both, 0.0).astype(BF16)
    lane_e = iota((16, 256), 1) // 16
    row_e = iota((16, 256), 0)
    mat = dot(mat_ref[...], spread, 1, 1)
    dist = dot(dist_ref[...], spread, 1, 1)
    for m in range(5):
        line = jnp.broadcast_to(mat[m : m + 1, :] if m < 4 else dist, (16, 256))
        table_ref[16 * m : 16 * m + 16, :] = jnp.where(lane_e == row_e, line, 0.0).astype(BF16)


def activate(acc):
    sigma = jax.nn.sigmoid(acc)
    return (acc * sigma).astype(BF16), sigma * (1.0 + acc * (1.0 - sigma))


def inner_kernel(
    feat_ref, ylo_ref, yhi_ref, table_ref, band_ref, emb_ref, slope_ref, hidden_ref, edge_ref
):
    table = table_ref[...]
    row = iota((128, 80), 0)
    emb_ref[0] = jnp.zeros((128, 256), BF16)
    emb_ref[33] = jnp.zeros((128, 256), BF16)
    ylo = ylo_ref[...].astype(F32)
    yhi = yhi_ref[...].astype(F32)
    for z in range(32):
        f = feat_ref[z].astype(F32)
        f = jnp.where(row == 64, ylo[z : z + 1, :], f)
        f = jnp.where(row == 127, yhi[z : z + 1, :], f)
        emb_ref[z + 1] = dot(f.astype(BF16), table, 1, 0).astype(BF16)
    chunk = 8
    for b in range(2):
        for z0 in range(0, 32, chunk):
            acc = None
            for ty in range(3):
                for tz in range(3):
                    run = RUNS[b][ty]
                    rows = emb_ref[z0 + tz : z0 + tz + chunk, run : run + 32, :].reshape(32 * chunk, 256)
                    part = dot(rows, band_ref[3 * ty + tz], 1, 0)
                    acc = part if acc is None else acc + part
            hid, slope = activate(acc)
            if z0 == 0:
                edge_ref[0, 32 * b : 32 * b + 32, :] = acc[:32]
            if z0 == 32 - chunk:
                edge_ref[1, 32 * b : 32 * b + 32, :] = acc[32 * chunk - 32 :]
            for k in range(chunk):
                z2, c = (z0 + k) // 2, k % 2
                hidden_ref[2 * b + c, 32 * z2 : 32 * z2 + 32, :] = hid[32 * k : 32 * k + 32]
                slope_ref[2 * b + c, 32 * z2 : 32 * z2 + 32, :] = slope[32 * k : 32 * k + 32]


def outer_kernel(
    zlo_ref, zhi_ref, table_ref, band_ref, dband_ref, edge_ref, inner_ref,
    emb_ref, slope_ref, hidden_ref, coarse_ref, turn_a, turn_b,
):
    table = table_ref[...]
    hidden_ref[...] = inner_ref[...]
    for side, face in enumerate((zlo_ref, zhi_ref)):
        plane = dot(face[...], table, 1, 0).astype(BF16)
        emb_ref[side] = plane
        for b in range(2):
            acc = edge_ref[side, 32 * b : 32 * b + 32, :]
            for ty in range(3):
                run = RUNS[b][ty]
                acc = acc + dot(plane[run : run + 32], band_ref[3 * ty + 2 * side], 1, 0)
            hid, slope = activate(acc)
            hidden_ref[2 * b + side, 480 * side : 480 * side + 32, :] = hid
            slope_ref[side, 32 * b : 32 * b + 32, :] = slope
    for x2 in range(8):
        at = slice(64 * x2, 64 * x2 + 64)
        acc = None
        for bc in range(4):
            part = dot(dband_ref[bc, at, :], hidden_ref[bc], 1, 1)
            acc = part if acc is None else acc + part
        turn_a[at, :] = acc
    for z2 in range(16):
        for half in range(2):
            pieces = [
                turn_a[64 * x2 : 64 * x2 + 64, 32 * z2 : 32 * z2 + 32]
                for x2 in range(4 * half, 4 * half + 4)
            ]
            turn_b[half, pl.ds(z2, 64, stride=16), :] = jnp.concatenate(pieces, axis=1)
    for half in range(2):
        coarse_ref[:, 128 * half : 128 * half + 128] = turn_b[half].astype(BF16)


def mix_kernel(scale, coarse_ref, mix_ref, cot_ref, mid_ref, mixg_ref, grad_ref):
    width = mix_ref.shape[1]
    coarse = coarse_ref[...].reshape(width, 256)
    mix = mix_ref[0]
    flat = coarse.T
    pre = dot(flat, mix, 1, 1)
    sigma = jax.nn.sigmoid(pre)
    mid_ref[0] = (pre * sigma).astype(BF16)
    grad = (cot_ref[0].astype(F32) * (sigma * (1.0 + pre * (1.0 - sigma)))).astype(BF16)
    turned = grad.T
    mixg_ref[0] = dot(turned, flat, 1, 0) * scale
    out = dot(mix.T, turned, 1, 0)
    grad_ref[...] = out.astype(BF16).reshape(grad_ref.shape)


def fold(value, step):
    lanes = value.shape[-1]
    if lanes == 256:
        value = value[:, :128] + value[:, 128:]
    shift = 64
    while shift >= step:
        value = value + pltpu.roll(value, shift, 1)
        shift //= 2
    return value


def backward_kernel(
    down_scale, conv_scale, cgrad_ref, emb_ref, slope_hbm, hidden_hbm, dband_hbm, face_ref, edge_ref,
    out_ref, turn_a, turn_b, turned_pg, hidden_ref, dband_ref, slope_ref, sem,
):
    copies = fetch((hidden_hbm, dband_hbm, slope_hbm), (hidden_ref, dband_ref, slope_ref), sem)
    for half in range(2):
        turn_b[half] = cgrad_ref[:, 128 * half : 128 * half + 128].astype(F32)
    for half in range(2):
        for quad in range(4):
            pieces = [turn_b[half, pl.ds(4 * quad + k, 64, stride=16), :] for k in range(4)]
            for k in range(4):
                x2 = 4 * half + k
                turn_a[64 * x2 : 64 * x2 + 64, 128 * quad : 128 * quad + 128] = jnp.concatenate(
                    [p[:, 32 * k : 32 * k + 32] for p in pieces], axis=1
                )
    cg_t = turn_a[...].astype(BF16)
    cg = cg_t.T
    lane = iota((64, 256), 1)
    low = iota((64, 128), 1)
    down = jnp.zeros((64, 128), F32)
    copies[0].wait()
    for bc in range(4):
        total = jnp.zeros((64, 256), F32)
        for x2 in range(8):
            part = dot(cg_t[64 * x2 : 64 * x2 + 64, :], hidden_ref[bc], 1, 0)
            total = jnp.where(lane // 32 == x2, part, total)
        down = jnp.where(low // 32 == bc, fold(total, 32), down)
    out_ref[0:64, :] = down * down_scale
    copies[1].wait()
    copies[2].wait()
    for bc in range(4):
        hgrad = dot(cg, dband_ref[bc], 1, 0)
        edge = edge_ref[bc % 2, 32 * (bc // 2) : 32 * (bc // 2) + 32, :]
        if bc % 2 == 0:
            slope = jnp.concatenate([edge, slope_ref[bc, 32:, :]], axis=0)
        else:
            slope = jnp.concatenate([slope_ref[bc, :480, :], edge], axis=0)
        pgrad = (hgrad * slope).astype(BF16)
        turned_pg[bc] = pgrad.T
    lane_x = iota((16, 256), 1) // 16
    own = iota((8, 128), 1) // 16 == iota((8, 128), 0)
    for ty in range(3):
        for tz in range(3):
            acc = None
            for bc in range(4):
                b, c = bc // 2, bc % 2
                run = RUNS[b][ty]
                q, p = (c + tz) // 2, (c + tz) % 2
                rows = emb_ref[q : q + 16, p, run : run + 32, :].reshape(512, 256)
                if c + tz == 0:
                    rows = jnp.concatenate([face_ref[0, run : run + 32, :], rows[32:]], axis=0)
                if c + tz == 3:
                    rows = jnp.concatenate([rows[:480], face_ref[1, run : run + 32, :]], axis=0)
                part = dot(turned_pg[bc], rows, 1, 0)
                acc = part if acc is None else acc + part
            for tx in range(3):
                total = jnp.zeros((16, 256), F32)
                for x in range(16):
                    if 0 <= x + tx - 1 < 16:
                        total = jnp.where(lane_x == x + tx - 1, acc[16 * x : 16 * x + 16, :], total)
                tap = 9 * tx + 3 * ty + tz
                total = fold(total, 16) * conv_scale
                for half in range(2):
                    part = jnp.where(own, total[8 * half : 8 * half + 8], 0.0)
                    line = 64 + 32 * half + tap
                    out_ref[line : line + 1, :] = jnp.sum(part, axis=0, keepdims=True)
    for half in range(2):
        out_ref[91 + 32 * half : 96 + 32 * half, :] = jnp.zeros((5, 128), F32)


def finish_kernel(a_ref, b_ref, c_ref, d_ref, down_ref, conv_ref):
    total = (a_ref[...] + b_ref[...]) + (c_ref[...] + d_ref[...])
    down = total[:64].T
    for a in range(2):
        for bc in range(4):
            at = (2 * bc + a) * 16
            down_ref[4 * a + bc] = down[at : at + 16, :]
    for half in range(2):
        conv = total[64 + 32 * half : 96 + 32 * half].T
        conv_ref[128 * half : 128 * half + 128, :] = conv[:, :27]


def kept(*values):
    return [pltpu.with_memory_space_constraint(v, pltpu.HBM) for v in values]


def params(mib):
    return pltpu.CompilerParams(vmem_limit_bytes=mib << 20)


def cost(flops, nbytes):
    return pl.CostEstimate(flops=flops, bytes_accessed=nbytes, transcendentals=0)


def shape(dims, dtype):
    return jax.ShapeDtypeStruct(dims, dtype)


def sum_rounds(count_y, count_z):
    in_z = [1 << k for k in range(count_z.bit_length() - 1)]
    in_y = [count_z << k for k in range(count_y.bit_length() - 1)]
    order = in_z[:1] + in_z[1:2] + in_y[:1] + in_z[2:] + in_y[1:]
    rounds, order = ([order[:1]] if len(order) % 2 else []), order[len(order) % 2 :]
    return rounds + [order[k : k + 2] for k in range(0, len(order), 2)]


def exchanged(value, masks, count):
    masks = list(masks) + [masks[0] ^ masks[1]] if len(masks) == 2 else masks
    return [lax.ppermute(value, ("sy", "sz"), [(i, i ^ m) for i in range(count)]) for m in masks]


def per_device(
    labels, wall_dist, material_table, dist_weight, conv_weight, down_weight, mix_weight, cotangent
):
    count_y = lax.axis_size("sy")
    count_z = lax.axis_size("sz")
    mine = 64 // count_z
    width = mix_weight.shape[1]
    features, first, last = pl.pallas_call(
        feature_kernel,
        out_shape=(shape((32, 128, 80), BF16), shape((32, 80), BF16), shape((32, 80), BF16)),
        in_specs=[HBM] * 2,
        out_specs=(VMEM,) * 3,
        scratch_shapes=[
            pltpu.VMEM((16, 32, 64), jnp.int32),
            pltpu.VMEM((16, 32, 64), BF16),
            pltpu.VMEM((16, 32, 64), F32),
            pltpu.VMEM((32, 80), F32),
            pltpu.VMEM((32, 80), F32),
            pltpu.SemaphoreType.DMA((2,)),
        ],
        compiler_params=params(8),
        cost_estimate=cost(32 * 128 * 64 * 80 * 2, 2 << 20),
        name="features",
    )(*kept(jnp.transpose(labels, (0, 2, 1)), jnp.transpose(wall_dist, (0, 2, 1))))
    up_y = [(i, i + 1) for i in range(count_y - 1)]
    up_z = [(i, i + 1) for i in range(count_z - 1)]
    ylo = lax.ppermute(last, "sy", up_y)
    yhi = lax.ppermute(first, "sy", [(j, i) for i, j in up_y])
    band, dband, table = pl.pallas_call(
        weight_kernel,
        out_shape=(shape((9, 256, 256), BF16), shape((4, 512, 256), BF16), shape((80, 256), BF16)),
        in_specs=[HBM] * 4,
        out_specs=(VMEM,) * 3,
        scratch_shapes=[
            pltpu.VMEM((16, 16, 27), BF16),
            pltpu.VMEM((8, 16, 64), BF16),
            pltpu.VMEM((4, 16), BF16),
            pltpu.VMEM((1, 16), BF16),
            pltpu.SemaphoreType.DMA((4,)),
        ],
        compiler_params=params(8),
        cost_estimate=cost(27 * 256 * 16 * 256 * 2, 3 << 20),
        name="weights",
    )(
        *kept(
            jnp.transpose(conv_weight, (1, 2, 0)),
            jnp.transpose(down_weight, (0, 2, 1)),
            material_table,
            dist_weight[None],
        )
    )
    ylo, yhi, band, dband, table = lax.optimization_barrier((ylo, yhi, band, dband, table))

    def whole(z):
        row = lax.broadcasted_iota(jnp.int32, (128, 80), 0)
        face = jnp.where(row == 64, ylo[z][None], features[z])
        return jnp.where(row == 127, yhi[z][None], face)

    zlo = lax.ppermute(whole(31), "sz", up_z)
    zhi = lax.ppermute(whole(0), "sz", [(j, i) for i, j in up_z])
    embedded, slope, hidden, edge = pl.pallas_call(
        inner_kernel,
        out_shape=(
            shape((34, 128, 256), BF16),
            shape((4, 512, 256), F32),
            shape((4, 512, 256), BF16),
            shape((2, 64, 256), F32),
        ),
        in_specs=[VMEM] * 5,
        out_specs=(VMEM,) * 4,
        compiler_params=params(8),
        cost_estimate=cost(3 << 30, 10 << 20),
        name="inner",
    )(features, ylo, yhi, table, band)
    faces, edge_slope, hidden, coarse = pl.pallas_call(
        outer_kernel,
        out_shape=(
            shape((2, 128, 256), BF16),
            shape((2, 64, 256), F32),
            shape((4, 512, 256), BF16),
            shape((1024, 256), BF16),
        ),
        in_specs=[VMEM] * 7,
        out_specs=(VMEM,) * 4,
        scratch_shapes=[pltpu.VMEM((512, 512), F32), pltpu.VMEM((2, 1024, 128), F32)],
        compiler_params=params(8),
        cost_estimate=cost(1 << 30, 4 << 20),
        name="outer",
    )(zlo, zhi, table, band, dband, edge, hidden)

    sent = lax.all_to_all(
        coarse.reshape(count_z, mine * 16, 256), "sz", split_axis=0, concat_axis=0, tiled=True
    )
    block = lambda *dims: pl.BlockSpec(dims, lambda c: (c,) + (0,) * (len(dims) - 1))
    mid, mix_partial, back = pl.pallas_call(
        lambda *refs: mix_kernel(1.0 / math.sqrt(8 * 32 * count_y), *refs),
        grid=(mine,),
        out_shape=(
            shape((mine, 256, width), BF16),
            shape((mine, width, width), F32),
            shape((count_z, mine * 16, 256), BF16),
        ),
        in_specs=[
            pl.BlockSpec((count_z, 16, 256), lambda c: (0, c, 0)),
            block(1, width, width),
            block(1, 256, width),
        ],
        out_specs=(
            block(1, 256, width),
            block(1, width, width),
            pl.BlockSpec((count_z, 16, 256), lambda c: (0, c, 0)),
        ),
        compiler_params=params(12),
        cost_estimate=cost(mine * 3 * 2 * 256 * width * width, 5 << 20),
        name="mix",
    )(sent, mix_weight, cotangent.reshape(mine, 256, width))
    coarse_grad = lax.all_to_all(back, "sz", split_axis=0, concat_axis=0, tiled=True)
    mix_grad = lax.psum_scatter(mix_partial, "sy", scatter_dimension=1, tiled=True)

    cells = 16 * 64 * count_y * 32 * count_z
    sums = pl.pallas_call(
        lambda *refs: backward_kernel(
            1.0 / math.sqrt(cells // 8), 1.0 / math.sqrt(cells), *refs
        ),
        out_shape=shape((128, 128), F32),
        in_specs=[VMEM, VMEM, HBM, HBM, HBM, VMEM, VMEM],
        out_specs=VMEM,
        scratch_shapes=[
            pltpu.VMEM((512, 512), F32),
            pltpu.VMEM((2, 1024, 128), F32),
            pltpu.VMEM((4, 256, 512), BF16),
            pltpu.VMEM((4, 512, 256), BF16),
            pltpu.VMEM((4, 512, 256), BF16),
            pltpu.VMEM((4, 512, 256), F32),
            pltpu.SemaphoreType.DMA((3,)),
        ],
        compiler_params=params(16),
        cost_estimate=cost(4 << 30, 8 << 20),
        name="backward",
    )(coarse_grad.reshape(1024, 256), embedded.reshape(17, 2, 128, 256), *kept(slope, hidden, dband), faces, edge_slope)
    rounds = sum_rounds(count_y, count_z)
    for masks in rounds[:-1]:
        parts = [sums] + exchanged(sums, masks, count_y * count_z)
        sums = parts[0] + parts[1] if len(parts) == 2 else (parts[0] + parts[1]) + (parts[2] + parts[3])
    down_grad, conv_grad = pl.pallas_call(
        finish_kernel,
        out_shape=(shape((8, 16, 64), F32), shape((256, 27), F32)),
        in_specs=[VMEM] * 4,
        out_specs=(VMEM,) * 2,
        compiler_params=params(8),
        cost_estimate=cost(1 << 20, 1 << 18),
        name="finish",
    )(sums, *exchanged(sums, rounds[-1], count_y * count_z))
    down_grad = jnp.transpose(down_grad, (0, 2, 1))
    conv_grad = jnp.transpose(conv_grad.reshape(16, 16, 27), (2, 0, 1))
    return (mid.reshape(cotangent.shape), mix_grad, down_grad, conv_grad)


def solution(mesh):
    in_specs = (
        P(None, "sy", "sz"),
        P(None, "sy", "sz"),
        P(),
        P(),
        P(),
        P(),
        P("sz", None, None),
        P("sz", None, "sy", None),
    )
    out_specs = (P("sz", None, "sy", None), P("sz", "sy", None), P(), P())
    return jax.shard_map(
        per_device, mesh=mesh, in_specs=in_specs, out_specs=out_specs, check_vma=False
    )
```

```python
import math

import jax
import jax.numpy as jnp
from jax import lax
from jax.experimental import pallas as pl
from jax.experimental.pallas import tpu as pltpu
from jax.sharding import PartitionSpec as P

F32 = jnp.float32
BF16 = jnp.bfloat16
VMEM = pl.BlockSpec(memory_space=pltpu.VMEM)
HBM = pl.BlockSpec(memory_space=pltpu.HBM)
RUNS = ((64, 0, 32), (0, 32, 96))


def dot(a, b, ca, cb):
    return lax.dot_general(a, b, (((ca,), (cb,)), ((), ())), preferred_element_type=F32)


def iota(shape, dim):
    return lax.broadcasted_iota(jnp.int32, shape, dim)


def fetch(sources, targets, sem):
    copies = [pltpu.make_async_copy(a, b, sem.at[k]) for k, (a, b) in enumerate(zip(sources, targets))]
    for copy in copies:
        copy.start()
    return copies


def feature_kernel(lab_hbm, wd_hbm, out_ref, first_ref, last_ref, lab_s, wd_b, wd_s, first_s, last_s, sem):
    copies = fetch((lab_hbm, wd_hbm), (lab_s, wd_b), sem)
    row = iota((128, 64), 0)
    run, r = row // 32, row % 32
    y = jnp.where(run == 0, 2 * r, jnp.where(run == 1, 2 * r + 1, jnp.where(run == 2, 2 * r - 1, 2 * r + 2)))
    pick = (y == iota((128, 64), 1)).astype(BF16)
    for copy in copies:
        copy.wait()
    wd_s[...] = wd_b[...].astype(F32)
    for z in range(out_ref.shape[0]):
        lab = lab_s[:, z, :]
        parts = [(lab == m).astype(F32).astype(BF16) for m in range(4)]
        parts.append(wd_s[:, z, :].astype(BF16))
        rows = dot(pick, jnp.concatenate(parts, axis=0), 1, 1)
        out_ref[z] = rows.astype(BF16)
        first_s[z : z + 1, :] = rows[0:1, :]
        last_s[z : z + 1, :] = rows[63:64, :]
    first_ref[...] = first_s[...].astype(BF16)
    last_ref[...] = last_s[...].astype(BF16)


def weight_kernel(
    conv_hbm, down_hbm, mat_hbm, dist_hbm, band_ref, dband_ref, table_ref,
    conv_ref, down_ref, mat_ref, dist_ref, sem,
):
    copies = fetch(
        (conv_hbm, down_hbm, mat_hbm, dist_hbm), (conv_ref, down_ref, mat_ref, dist_ref), sem
    )
    for copy in copies:
        copy.wait()
    spread = (iota((256, 16), 0) % 16 == iota((256, 16), 1)).astype(BF16)
    taps = conv_ref[...].reshape(256, 27)
    repeat = (iota((27, 432), 0) == iota((27, 432), 1) // 16).astype(BF16)
    own = iota((256, 432), 0) // 16 == iota((256, 432), 1) % 16
    apart = jnp.where(own, dot(taps, repeat, 1, 0), 0.0).astype(BF16)
    gather = (iota((256, 256), 0) % 16 == iota((256, 256), 1) % 16).astype(BF16)
    wide = dot(gather, apart, 1, 0).astype(BF16)
    offset = iota((256, 256), 0) // 16 - iota((256, 256), 1) // 16 + 1
    for t in range(9):
        total = jnp.zeros((256, 256), F32)
        for tx in range(3):
            at = (tx * 9 + t) * 16
            tile = dot(wide[:, at : at + 16], spread, 1, 1)
            total = jnp.where(offset == tx, tile, total)
        band_ref[t] = total.astype(BF16)
    lane_x = iota((64, 256), 1) // 16
    for bc in range(4):
        tiles = [dot(down_ref[4 * a + bc], spread, 0, 1) for a in range(2)]
        both = jnp.where(lane_x % 2 == 0, tiles[0], tiles[1])
        for x2 in range(8):
            dband_ref[bc, 64 * x2 : 64 * x2 + 64, :] = jnp.where(lane_x // 2 == x2, both, 0.0).astype(BF16)
    lane_e = iota((16, 256), 1) // 16
    row_e = iota((16, 256), 0)
    mat = dot(mat_ref[...], spread, 1, 1)
    dist = dot(dist_ref[...], spread, 1, 1)
    for m in range(5):
        line = jnp.broadcast_to(mat[m : m + 1, :] if m < 4 else dist, (16, 256))
        table_ref[16 * m : 16 * m + 16, :] = jnp.where(lane_e == row_e, line, 0.0).astype(BF16)


def activate(acc):
    sigma = jax.nn.sigmoid(acc)
    return (acc * sigma).astype(BF16), sigma * (1.0 + acc * (1.0 - sigma))


def inner_kernel(
    feat_ref, ylo_ref, yhi_ref, table_ref, band_ref, emb_hbm, slope_hbm, hidden_ref, edge_ref,
    emb_ref, slope_ref, sem,
):
    table = table_ref[...]
    row = iota((128, 80), 0)
    emb_ref[0] = jnp.zeros((128, 256), BF16)
    emb_ref[33] = jnp.zeros((128, 256), BF16)
    ylo = ylo_ref[...].astype(F32)
    yhi = yhi_ref[...].astype(F32)
    for z in range(32):
        f = feat_ref[z].astype(F32)
        f = jnp.where(row == 64, ylo[z : z + 1, :], f)
        f = jnp.where(row == 127, yhi[z : z + 1, :], f)
        emb_ref[z + 1] = dot(f.astype(BF16), table, 1, 0).astype(BF16)
    copies = [pltpu.make_async_copy(emb_ref, emb_hbm, sem.at[0])]
    copies[0].start()
    chunk = 8
    for b in range(2):
        for z0 in range(0, 32, chunk):
            acc = None
            for ty in range(3):
                for tz in range(3):
                    run = RUNS[b][ty]
                    rows = emb_ref[z0 + tz : z0 + tz + chunk, run : run + 32, :].reshape(32 * chunk, 256)
                    part = dot(rows, band_ref[3 * ty + tz], 1, 0)
                    acc = part if acc is None else acc + part
            hid, slope = activate(acc)
            if z0 == 0:
                edge_ref[0, 32 * b : 32 * b + 32, :] = acc[:32]
            if z0 == 32 - chunk:
                edge_ref[1, 32 * b : 32 * b + 32, :] = acc[32 * chunk - 32 :]
            for k in range(chunk):
                z2, c = (z0 + k) // 2, k % 2
                hidden_ref[2 * b + c, 32 * z2 : 32 * z2 + 32, :] = hid[32 * k : 32 * k + 32]
                slope_ref[2 * b + c, 32 * z2 : 32 * z2 + 32, :] = slope[32 * k : 32 * k + 32]
            at = (pl.ds(2 * b, 2), pl.ds(16 * z0, 16 * chunk))
            copies.append(pltpu.make_async_copy(slope_ref.at[at], slope_hbm.at[at], sem.at[len(copies)]))
            copies[-1].start()
    for copy in copies:
        copy.wait()


def outer_kernel(
    zlo_ref, zhi_ref, table_ref, band_ref, dband_ref, edge_ref, inner_ref,
    emb_ref, slope_ref, hidden_hbm, coarse_ref, turn_a, turn_b, hidden_ref, sem,
):
    table = table_ref[...]
    hidden_ref[...] = inner_ref[...]
    for side, face in enumerate((zlo_ref, zhi_ref)):
        plane = dot(face[...], table, 1, 0).astype(BF16)
        emb_ref[side] = plane
        for b in range(2):
            acc = edge_ref[side, 32 * b : 32 * b + 32, :]
            for ty in range(3):
                run = RUNS[b][ty]
                acc = acc + dot(plane[run : run + 32], band_ref[3 * ty + 2 * side], 1, 0)
            hid, slope = activate(acc)
            hidden_ref[2 * b + side, 480 * side : 480 * side + 32, :] = hid
            slope_ref[side, 32 * b : 32 * b + 32, :] = slope
    copy = pltpu.make_async_copy(hidden_ref, hidden_hbm, sem)
    copy.start()
    for x2 in range(8):
        at = slice(64 * x2, 64 * x2 + 64)
        acc = None
        for bc in range(4):
            part = dot(dband_ref[bc, at, :], hidden_ref[bc], 1, 1)
            acc = part if acc is None else acc + part
        turn_a[at, :] = acc
    for z2 in range(16):
        for half in range(2):
            pieces = [
                turn_a[64 * x2 : 64 * x2 + 64, 32 * z2 : 32 * z2 + 32]
                for x2 in range(4 * half, 4 * half + 4)
            ]
            turn_b[half, pl.ds(z2, 64, stride=16), :] = jnp.concatenate(pieces, axis=1)
    for half in range(2):
        coarse_ref[:, 128 * half : 128 * half + 128] = turn_b[half].astype(BF16)
    copy.wait()


def mix_kernel(scale, me_ref, coarse_ref, mix_ref, cot_ref, mid_ref, grad_ref, *more_refs):
    *share_refs, total_ref = more_refs
    width = mix_ref.shape[1]
    coarse = coarse_ref[...].reshape(width, 256)
    mix = mix_ref[0]
    flat = coarse.T
    pre = dot(flat, mix, 1, 1)
    sigma = jax.nn.sigmoid(pre)
    mid_ref[0] = (pre * sigma).astype(BF16)
    grad = (cot_ref[0].astype(F32) * (sigma * (1.0 + pre * (1.0 - sigma)))).astype(BF16)
    turned = grad.T
    total_ref[...] = dot(turned, flat, 1, 0) * scale
    rows = width // (2 * len(share_refs))
    for place in range(2 * len(share_refs)):
        start = pl.multiple_of(jnp.bitwise_xor(me_ref[0], place) * rows, rows)
        at = place % 2 * rows
        share_refs[place // 2][0, at : at + rows, :] = total_ref[pl.ds(start, rows), :]
    out = dot(mix.T, turned, 1, 0)
    grad_ref[...] = out.astype(BF16).reshape(grad_ref.shape)


def fold(value, step):
    lanes = value.shape[-1]
    if lanes == 256:
        value = value[:, :128] + value[:, 128:]
    shift = 64
    while shift >= step:
        value = value + pltpu.roll(value, shift, 1)
        shift //= 2
    return value


def backward_kernel(
    down_scale, conv_scale, cgrad_ref, emb_hbm, slope_hbm, hidden_ref, dband_ref, face_ref, edge_ref,
    out_ref, turn_a, turn_b, turned_pg, emb_ref, slope_ref, sem,
):
    copies = fetch((slope_hbm, emb_hbm), (slope_ref, emb_ref), sem)
    for half in range(2):
        turn_b[half] = cgrad_ref[:, 128 * half : 128 * half + 128].astype(F32)
    for half in range(2):
        for quad in range(4):
            pieces = [turn_b[half, pl.ds(4 * quad + k, 64, stride=16), :] for k in range(4)]
            for k in range(4):
                x2 = 4 * half + k
                turn_a[64 * x2 : 64 * x2 + 64, 128 * quad : 128 * quad + 128] = jnp.concatenate(
                    [p[:, 32 * k : 32 * k + 32] for p in pieces], axis=1
                )
    cg_t = turn_a[...].astype(BF16)
    cg = cg_t.T
    lane = iota((64, 256), 1)
    low = iota((64, 128), 1)
    down = jnp.zeros((64, 128), F32)
    for bc in range(4):
        total = jnp.zeros((64, 256), F32)
        for x2 in range(8):
            part = dot(cg_t[64 * x2 : 64 * x2 + 64, :], hidden_ref[bc], 1, 0)
            total = jnp.where(lane // 32 == x2, part, total)
        down = jnp.where(low // 32 == bc, fold(total, 32), down)
    out_ref[0:64, :] = down * down_scale
    copies[0].wait()
    for bc in range(4):
        hgrad = dot(cg, dband_ref[bc], 1, 0)
        edge = edge_ref[bc % 2, 32 * (bc // 2) : 32 * (bc // 2) + 32, :]
        if bc % 2 == 0:
            slope = jnp.concatenate([edge, slope_ref[bc, 32:, :]], axis=0)
        else:
            slope = jnp.concatenate([slope_ref[bc, :480, :], edge], axis=0)
        pgrad = (hgrad * slope).astype(BF16)
        turned_pg[bc] = pgrad.T
    copies[1].wait()
    lane_x = iota((16, 256), 1) // 16
    own = iota((8, 128), 1) // 16 == iota((8, 128), 0)
    for ty in range(3):
        for tz in range(3):
            acc = None
            for bc in range(4):
                b, c = bc // 2, bc % 2
                run = RUNS[b][ty]
                q, p = (c + tz) // 2, (c + tz) % 2
                rows = emb_ref[q : q + 16, p, run : run + 32, :].reshape(512, 256)
                if c + tz == 0:
                    rows = jnp.concatenate([face_ref[0, run : run + 32, :], rows[32:]], axis=0)
                if c + tz == 3:
                    rows = jnp.concatenate([rows[:480], face_ref[1, run : run + 32, :]], axis=0)
                part = dot(turned_pg[bc], rows, 1, 0)
                acc = part if acc is None else acc + part
            for tx in range(3):
                total = jnp.zeros((16, 256), F32)
                for x in range(16):
                    if 0 <= x + tx - 1 < 16:
                        total = jnp.where(lane_x == x + tx - 1, acc[16 * x : 16 * x + 16, :], total)
                tap = 9 * tx + 3 * ty + tz
                total = fold(total, 16) * conv_scale
                for half in range(2):
                    part = jnp.where(own, total[8 * half : 8 * half + 8], 0.0)
                    line = 64 + 32 * half + tap
                    out_ref[line : line + 1, :] = jnp.sum(part, axis=0, keepdims=True)
    for half in range(2):
        out_ref[91 + 32 * half : 96 + 32 * half, :] = jnp.zeros((5, 128), F32)


def finish_kernel(a_ref, b_ref, c_ref, d_ref, down_ref, conv_ref):
    total = (a_ref[...] + b_ref[...]) + (c_ref[...] + d_ref[...])
    down = total[:64].T
    for a in range(2):
        for bc in range(4):
            at = (2 * bc + a) * 16
            down_ref[4 * a + bc] = down[at : at + 16, :]
    for half in range(2):
        conv = total[64 + 32 * half : 96 + 32 * half].T
        conv_ref[128 * half : 128 * half + 128, :] = conv[:, :27]


def kept(*values):
    return [pltpu.with_memory_space_constraint(v, pltpu.HBM) for v in values]


def params(mib):
    return pltpu.CompilerParams(vmem_limit_bytes=mib << 20)


def cost(flops, nbytes):
    return pl.CostEstimate(flops=flops, bytes_accessed=nbytes, transcendentals=0)


def shape(dims, dtype):
    return jax.ShapeDtypeStruct(dims, dtype)


def sum_rounds(count_y, count_z):
    in_z = [1 << k for k in range(count_z.bit_length() - 1)]
    in_y = [count_z << k for k in range(count_y.bit_length() - 1)]
    order = in_z[:1] + in_z[1:2] + in_y[:1] + in_z[2:] + in_y[1:]
    rounds, order = ([order[:1]] if len(order) % 2 else []), order[len(order) % 2 :]
    return rounds + [order[k : k + 2] for k in range(0, len(order), 2)]


def exchanged(value, masks, count):
    masks = list(masks) + [masks[0] ^ masks[1]] if len(masks) == 2 else masks
    return [lax.ppermute(value, ("sy", "sz"), [(i, i ^ m) for i in range(count)]) for m in masks]


def per_device(
    labels, wall_dist, material_table, dist_weight, conv_weight, down_weight, mix_weight, cotangent
):
    count_y = lax.axis_size("sy")
    count_z = lax.axis_size("sz")
    mine = 64 // count_z
    width = mix_weight.shape[1]
    features, first, last = pl.pallas_call(
        feature_kernel,
        out_shape=(shape((32, 128, 80), BF16), shape((32, 80), BF16), shape((32, 80), BF16)),
        in_specs=[HBM] * 2,
        out_specs=(VMEM,) * 3,
        scratch_shapes=[
            pltpu.VMEM((16, 32, 64), jnp.int32),
            pltpu.VMEM((16, 32, 64), BF16),
            pltpu.VMEM((16, 32, 64), F32),
            pltpu.VMEM((32, 80), F32),
            pltpu.VMEM((32, 80), F32),
            pltpu.SemaphoreType.DMA((2,)),
        ],
        compiler_params=params(8),
        cost_estimate=cost(32 * 128 * 64 * 80 * 2, 2 << 20),
        name="features",
    )(*kept(jnp.transpose(labels, (0, 2, 1)), jnp.transpose(wall_dist, (0, 2, 1))))
    up_y = [(i, i + 1) for i in range(count_y - 1)]
    up_z = [(i, i + 1) for i in range(count_z - 1)]
    ylo = lax.ppermute(last, "sy", up_y)
    yhi = lax.ppermute(first, "sy", [(j, i) for i, j in up_y])
    band, dband, table = pl.pallas_call(
        weight_kernel,
        out_shape=(shape((9, 256, 256), BF16), shape((4, 512, 256), BF16), shape((80, 256), BF16)),
        in_specs=[HBM] * 4,
        out_specs=(VMEM,) * 3,
        scratch_shapes=[
            pltpu.VMEM((16, 16, 27), BF16),
            pltpu.VMEM((8, 16, 64), BF16),
            pltpu.VMEM((4, 16), BF16),
            pltpu.VMEM((1, 16), BF16),
            pltpu.SemaphoreType.DMA((4,)),
        ],
        compiler_params=params(8),
        cost_estimate=cost(27 * 256 * 16 * 256 * 2, 3 << 20),
        name="weights",
    )(
        *kept(
            jnp.transpose(conv_weight, (1, 2, 0)),
            jnp.transpose(down_weight, (0, 2, 1)),
            material_table,
            dist_weight[None],
        )
    )
    ylo, yhi, band, dband, table = lax.optimization_barrier((ylo, yhi, band, dband, table))

    def whole(z):
        row = lax.broadcasted_iota(jnp.int32, (128, 80), 0)
        face = jnp.where(row == 64, ylo[z][None], features[z])
        return jnp.where(row == 127, yhi[z][None], face)

    zlo = lax.ppermute(whole(31), "sz", up_z)
    zhi = lax.ppermute(whole(0), "sz", [(j, i) for i, j in up_z])
    embedded, slope, hidden, edge = pl.pallas_call(
        inner_kernel,
        out_shape=(
            pltpu.HBM((34, 128, 256), BF16),
            pltpu.HBM((4, 512, 256), F32),
            shape((4, 512, 256), BF16),
            shape((2, 64, 256), F32),
        ),
        in_specs=[VMEM] * 5,
        out_specs=(HBM, HBM, VMEM, VMEM),
        scratch_shapes=[
            pltpu.VMEM((34, 128, 256), BF16),
            pltpu.VMEM((4, 512, 256), F32),
            pltpu.SemaphoreType.DMA((9,)),
        ],
        compiler_params=params(12),
        cost_estimate=cost(3 << 30, 10 << 20),
        name="inner",
    )(features, ylo, yhi, table, band)
    faces, edge_slope, hidden, coarse = pl.pallas_call(
        outer_kernel,
        out_shape=(
            shape((2, 128, 256), BF16),
            shape((2, 64, 256), F32),
            pltpu.HBM((4, 512, 256), BF16),
            shape((1024, 256), BF16),
        ),
        in_specs=[VMEM] * 7,
        out_specs=(VMEM, VMEM, HBM, VMEM),
        scratch_shapes=[
            pltpu.VMEM((512, 512), F32),
            pltpu.VMEM((2, 1024, 128), F32),
            pltpu.VMEM((4, 512, 256), BF16),
            pltpu.SemaphoreType.DMA,
        ],
        compiler_params=params(8),
        cost_estimate=cost(1 << 30, 4 << 20),
        name="outer",
    )(zlo, zhi, table, band, dband, edge, hidden)

    sent = lax.all_to_all(
        coarse.reshape(count_z, mine * 16, 256), "sz", split_axis=0, concat_axis=0, tiled=True
    )
    block = lambda *dims: pl.BlockSpec(dims, lambda c: (c,) + (0,) * (len(dims) - 1))
    shares = count_y // 2
    mid, back, *mix_parts = pl.pallas_call(
        lambda *refs: mix_kernel(1.0 / math.sqrt(8 * 32 * count_y), *refs),
        grid=(mine,),
        out_shape=[shape((mine, 256, width), BF16), shape((count_z, mine * 16, 256), BF16)]
        + [pltpu.HBM((mine, width // shares, width), F32)] * shares,
        in_specs=[
            pl.BlockSpec(memory_space=pltpu.SMEM),
            pl.BlockSpec((count_z, 16, 256), lambda c: (0, c, 0)),
            block(1, width, width),
            block(1, 256, width),
        ],
        out_specs=[block(1, 256, width), pl.BlockSpec((count_z, 16, 256), lambda c: (0, c, 0))]
        + [block(1, width // shares, width)] * shares,
        scratch_shapes=[pltpu.VMEM((width, width), F32)],
        compiler_params=params(12),
        cost_estimate=cost(mine * 3 * 2 * 256 * width * width, 5 << 20),
        name="mix",
    )(lax.axis_index("sy")[None], sent, mix_weight, cotangent.reshape(mine, 256, width))
    mix_sum = mix_parts[0]
    for k, part in enumerate(mix_parts[1:], 1):
        mix_sum = mix_sum + lax.ppermute(part, "sy", [(i, i ^ (2 * k)) for i in range(count_y)])
    coarse_grad = lax.all_to_all(back, "sz", split_axis=0, concat_axis=0, tiled=True)
    mix_sum, coarse_grad = lax.optimization_barrier((mix_sum, coarse_grad))
    mine_last, other = jnp.split(mix_sum, 2, axis=1)
    mix_grad = mine_last + lax.ppermute(other, "sy", [(i, i ^ 1) for i in range(count_y)])

    cells = 16 * 64 * count_y * 32 * count_z
    sums = pl.pallas_call(
        lambda *refs: backward_kernel(
            1.0 / math.sqrt(cells // 8), 1.0 / math.sqrt(cells), *refs
        ),
        out_shape=shape((128, 128), F32),
        in_specs=[VMEM, HBM, HBM, VMEM, VMEM, VMEM, VMEM],
        out_specs=VMEM,
        scratch_shapes=[
            pltpu.VMEM((512, 512), F32),
            pltpu.VMEM((2, 1024, 128), F32),
            pltpu.VMEM((4, 256, 512), BF16),
            pltpu.VMEM((17, 2, 128, 256), BF16),
            pltpu.VMEM((4, 512, 256), F32),
            pltpu.SemaphoreType.DMA((2,)),
        ],
        compiler_params=params(16),
        cost_estimate=cost(4 << 30, 8 << 20),
        name="backward",
    )(
        coarse_grad.reshape(1024, 256),
        *kept(embedded.reshape(17, 2, 128, 256), slope),
        hidden,
        dband,
        faces,
        edge_slope,
    )
    rounds = sum_rounds(count_y, count_z)
    for masks in rounds[:-1]:
        parts = [sums] + exchanged(sums, masks, count_y * count_z)
        sums = parts[0] + parts[1] if len(parts) == 2 else (parts[0] + parts[1]) + (parts[2] + parts[3])
    down_grad, conv_grad = pl.pallas_call(
        finish_kernel,
        out_shape=(shape((8, 16, 64), F32), shape((256, 27), F32)),
        in_specs=[VMEM] * 4,
        out_specs=(VMEM,) * 2,
        compiler_params=params(8),
        cost_estimate=cost(1 << 20, 1 << 18),
        name="finish",
    )(sums, *exchanged(sums, rounds[-1], count_y * count_z))
    down_grad = jnp.transpose(down_grad, (0, 2, 1))
    conv_grad = jnp.transpose(conv_grad.reshape(16, 16, 27), (2, 0, 1))
    return (mid.reshape(cotangent.shape), mix_grad, down_grad, conv_grad)


def solution(mesh):
    in_specs = (
        P(None, "sy", "sz"),
        P(None, "sy", "sz"),
        P(),
        P(),
        P(),
        P(),
        P("sz", None, None),
        P("sz", None, "sy", None),
    )
    out_specs = (P("sz", None, "sy", None), P("sz", "sy", None), P(), P())
    return jax.shard_map(
        per_device, mesh=mesh, in_specs=in_specs, out_specs=out_specs, check_vma=False
    )
```

```python
import math

import jax
import jax.numpy as jnp
from jax import lax
from jax.experimental import pallas as pl
from jax.experimental.pallas import tpu as pltpu
from jax.sharding import PartitionSpec as P

F32 = jnp.float32
BF16 = jnp.bfloat16
VMEM = pl.BlockSpec(memory_space=pltpu.VMEM)
HBM = pl.BlockSpec(memory_space=pltpu.HBM)
RUNS = ((64, 0, 32), (0, 32, 96))


def dot(a, b, ca, cb):
    return lax.dot_general(a, b, (((ca,), (cb,)), ((), ())), preferred_element_type=F32)


def iota(shape, dim):
    return lax.broadcasted_iota(jnp.int32, shape, dim)


def fetch(sources, targets, sem):
    copies = [pltpu.make_async_copy(a, b, sem.at[k]) for k, (a, b) in enumerate(zip(sources, targets))]
    for copy in copies:
        copy.start()
    return copies


def feature_kernel(lab_hbm, wd_hbm, out_ref, first_ref, last_ref, lab_s, wd_b, wd_s, first_s, last_s, sem):
    copies = fetch((lab_hbm, wd_hbm), (lab_s, wd_b), sem)
    row = iota((128, 64), 0)
    run, r = row // 32, row % 32
    y = jnp.where(run == 0, 2 * r, jnp.where(run == 1, 2 * r + 1, jnp.where(run == 2, 2 * r - 1, 2 * r + 2)))
    pick = (y == iota((128, 64), 1)).astype(BF16)
    for copy in copies:
        copy.wait()
    wd_s[...] = wd_b[...].astype(F32)
    for z in range(out_ref.shape[0]):
        lab = lab_s[:, z, :]
        parts = [(lab == m).astype(F32).astype(BF16) for m in range(4)]
        parts.append(wd_s[:, z, :].astype(BF16))
        rows = dot(pick, jnp.concatenate(parts, axis=0), 1, 1)
        out_ref[z] = rows.astype(BF16)
        first_s[z : z + 1, :] = rows[0:1, :]
        last_s[z : z + 1, :] = rows[63:64, :]
    first_ref[...] = first_s[...].astype(BF16)
    last_ref[...] = last_s[...].astype(BF16)


def weight_kernel(
    conv_hbm, down_hbm, mat_hbm, dist_hbm, band_ref, pair_ref, pair_t_ref, table_ref,
    conv_ref, down_ref, mat_ref, dist_ref, sem,
):
    copies = fetch(
        (conv_hbm, down_hbm, mat_hbm, dist_hbm), (conv_ref, down_ref, mat_ref, dist_ref), sem
    )
    for copy in copies:
        copy.wait()
    spread = (iota((256, 16), 0) % 16 == iota((256, 16), 1)).astype(BF16)
    taps = conv_ref[...].reshape(256, 27)
    repeat = (iota((27, 432), 0) == iota((27, 432), 1) // 16).astype(BF16)
    own = iota((256, 432), 0) % 16 == iota((256, 432), 1) % 16
    apart = jnp.where(own, dot(taps, repeat, 1, 0), 0.0).astype(BF16)
    gather = (iota((256, 256), 0) % 16 == iota((256, 256), 1) // 16).astype(BF16)
    wide = dot(gather, apart, 1, 0).astype(BF16)
    offset = iota((256, 256), 1) // 16 - iota((256, 256), 0) // 16 + 1
    for t in range(9):
        total = jnp.zeros((256, 256), F32)
        for tx in range(3):
            at = (tx * 9 + t) * 16
            tile = dot(wide[:, at : at + 16], spread, 1, 1)
            total = jnp.where(offset == tx, tile, total)
        band_ref[t] = total.astype(BF16)
    for bc in range(4):
        for x2 in range(2):
            for a in range(2):
                tap = down_ref[4 * a + bc]
                none = jnp.zeros_like(tap)
                at = 64 * bc + 32 * x2 + 16 * a
                pair_t_ref[at : at + 16, :] = jnp.concatenate([none, tap] if x2 else [tap, none], axis=1)
    pair_ref[...] = pair_t_ref[...].T
    lane_e = iota((16, 256), 1) // 16
    row_e = iota((16, 256), 0)
    mat = dot(mat_ref[...], spread, 1, 1)
    dist = dot(dist_ref[...], spread, 1, 1)
    for m in range(5):
        line = jnp.broadcast_to(mat[m : m + 1, :] if m < 4 else dist, (16, 256))
        table_ref[16 * m : 16 * m + 16, :] = jnp.where(lane_e == row_e, line, 0.0).astype(BF16)


def activate(acc):
    sigma = jax.nn.sigmoid(acc)
    return (acc * sigma).astype(BF16), sigma * (1.0 + acc * (1.0 - sigma))


def cells_of(emb_ref, b, c, ty, tz, half):
    run = RUNS[b][ty]
    q = (c + tz) // 2 + 8 * half
    return emb_ref[q : q + 8, (c + tz) % 2, run : run + 32, :].reshape(256, 256)


def inner_kernel(
    feat_ref, ylo_ref, yhi_ref, table_ref, band_ref, emb_hbm, slope_hbm, hidden_ref, edge_ref,
    emb_ref, slope_ref, sem,
):
    table = table_ref[...]
    row = iota((128, 80), 0)
    emb_ref[0, 0] = jnp.zeros((128, 256), BF16)
    emb_ref[16, 1] = jnp.zeros((128, 256), BF16)
    ylo = ylo_ref[...].astype(F32)
    yhi = yhi_ref[...].astype(F32)
    for z in range(32):
        f = feat_ref[z].astype(F32)
        f = jnp.where(row == 64, ylo[z : z + 1, :], f)
        f = jnp.where(row == 127, yhi[z : z + 1, :], f)
        emb_ref[(z + 1) // 2, (z + 1) % 2] = dot(f.astype(BF16), table, 1, 0).astype(BF16)
    copies = [pltpu.make_async_copy(emb_ref, emb_hbm, sem.at[0])]
    copies[0].start()
    for bc in range(4):
        b, c = bc // 2, bc % 2
        for half in range(2):
            acc = None
            for ty in range(3):
                for tz in range(3):
                    part = dot(band_ref[3 * ty + tz], cells_of(emb_ref, b, c, ty, tz, half), 1, 1)
                    acc = part if acc is None else acc + part
            if half == 0 and c == 0:
                edge_ref[0, b] = acc[:, :32]
            if half == 1 and c == 1:
                edge_ref[1, b] = acc[:, 224:]
            at = slice(256 * half, 256 * half + 256)
            hidden_ref[bc, :, at], slope_ref[bc, :, at] = activate(acc)
        copies.append(pltpu.make_async_copy(slope_ref.at[bc], slope_hbm.at[bc], sem.at[1 + bc]))
        copies[-1].start()
    for copy in copies:
        copy.wait()


def pair_rows(hidden_ref, pair):
    return jnp.concatenate([hidden_ref[bc, 64 * pair : 64 * pair + 64, :] for bc in range(4)], axis=0)


def outer_kernel(
    zlo_ref, zhi_ref, table_ref, band_ref, pair_ref, edge_ref, inner_ref,
    emb_ref, slope_ref, hidden_hbm, coarse_hbm, turn_a, turn_b, hidden_ref, coarse_ref, sem,
):
    table = table_ref[...]
    hidden_ref[...] = inner_ref[...]
    for side, face in enumerate((zlo_ref, zhi_ref)):
        plane = dot(face[...], table, 1, 0).astype(BF16)
        emb_ref[side] = plane
        for b in range(2):
            acc = edge_ref[side, b]
            for ty in range(3):
                run = RUNS[b][ty]
                acc = acc + dot(band_ref[3 * ty + 2 * side], plane[run : run + 32], 1, 1)
            at = slice(480 * side, 480 * side + 32)
            hidden_ref[2 * b + side, :, at], slope_ref[side, b] = activate(acc)
    copies = [pltpu.make_async_copy(hidden_ref, hidden_hbm, sem.at[0])]
    copies[0].start()
    for pair in range(4):
        turn_a[128 * pair : 128 * pair + 128, :] = dot(pair_ref[...], pair_rows(hidden_ref, pair), 1, 0)
    for half in range(2):
        for z2 in range(16):
            pieces = [
                turn_a[64 * x2 : 64 * x2 + 64, 32 * z2 : 32 * z2 + 32]
                for x2 in range(4 * half, 4 * half + 4)
            ]
            turn_b[half, pl.ds(z2, 64, stride=16), :] = jnp.concatenate(pieces, axis=1)
        at = (slice(None), pl.ds(128 * half, 128))
        coarse_ref[at] = turn_b[half].astype(BF16)
        copies.append(pltpu.make_async_copy(coarse_ref.at[at], coarse_hbm.at[at], sem.at[1 + half]))
        copies[-1].start()
    for copy in copies:
        copy.wait()


def mix_kernel(scale, me_ref, coarse_ref, mix_ref, cot_ref, mid_ref, grad_ref, *more_refs):
    *share_refs, total_ref = more_refs
    width = mix_ref.shape[1]
    coarse = coarse_ref[...].reshape(width, 256)
    mix = mix_ref[0]
    flat = coarse.T
    pre = dot(flat, mix, 1, 1)
    sigma = jax.nn.sigmoid(pre)
    mid_ref[0] = (pre * sigma).astype(BF16)
    grad = (cot_ref[0].astype(F32) * (sigma * (1.0 + pre * (1.0 - sigma)))).astype(BF16)
    turned = grad.T
    total_ref[...] = dot(turned, flat, 1, 0) * scale
    rows = width // (2 * len(share_refs))
    for place in range(2 * len(share_refs)):
        start = pl.multiple_of(jnp.bitwise_xor(me_ref[0], place) * rows, rows)
        at = place % 2 * rows
        share_refs[place // 2][0, at : at + rows, :] = total_ref[pl.ds(start, rows), :]
    out = dot(mix.T, turned, 1, 0)
    grad_ref[...] = out.astype(BF16).reshape(grad_ref.shape)


def fold(value, step):
    lanes = value.shape[-1]
    if lanes == 256:
        value = value[:, :128] + value[:, 128:]
    shift = 64
    while shift >= step:
        value = value + pltpu.roll(value, shift, 1)
        shift //= 2
    return value


def backward_kernel(
    down_scale, conv_scale, cgrad_ref, emb_hbm, slope_hbm, hidden_ref, pair_ref, pair_t_ref, face_ref, edge_ref,
    out_ref, turn_a, turn_b, turned_pg, emb_ref, slope_ref, sem,
):
    copies = fetch((slope_hbm, emb_hbm), (slope_ref, emb_ref), sem)
    for half in range(2):
        turn_b[half] = cgrad_ref[:, 128 * half : 128 * half + 128].astype(F32)
    for half in range(2):
        for quad in range(4):
            pieces = [turn_b[half, pl.ds(4 * quad + k, 64, stride=16), :] for k in range(4)]
            for k in range(4):
                x2 = 4 * half + k
                turn_a[64 * x2 : 64 * x2 + 64, 128 * quad : 128 * quad + 128] = jnp.concatenate(
                    [p[:, 32 * k : 32 * k + 32] for p in pieces], axis=1
                )
    cg_t = turn_a[...].astype(BF16)
    pairs = [cg_t[128 * pair : 128 * pair + 128, :] for pair in range(4)]
    down = None
    for pair in range(4):
        part = dot(pairs[pair], pair_rows(hidden_ref, pair), 1, 1)
        down = part if down is None else down + part
    down = jnp.where(iota((64, 256), 1) // 32 % 2 == 0, down[:64], down[64:]) * down_scale
    left = down[:, :128] + pltpu.roll(down[:, :128], 96, 1)
    right = down[:, 128:] + pltpu.roll(down[:, 128:], 32, 1)
    out_ref[0:64, :] = jnp.where(iota((64, 128), 1) // 32 % 2 == 0, left, right)
    copies[0].wait()
    for side in range(2):
        for b in range(2):
            slope_ref[2 * b + side, :, 480 * side : 480 * side + 32] = edge_ref[side, b]
    for pair in range(4):
        hgrad = dot(pair_t_ref[...], pairs[pair], 1, 0)
        at = slice(64 * pair, 64 * pair + 64)
        for bc in range(4):
            grad = hgrad[64 * bc : 64 * bc + 64] * slope_ref[bc, at, :]
            turned_pg[bc, at, :] = grad.astype(BF16)
    copies[1].wait()
    emb_ref[0, 0] = face_ref[0]
    emb_ref[16, 1] = face_ref[1]
    lane_x = iota((16, 256), 1) // 16
    own = iota((8, 128), 1) // 16 == iota((8, 128), 0)
    for ty in range(3):
        for tz in range(3):
            acc = None
            for bc in range(4):
                b, c = bc // 2, bc % 2
                for half in range(2):
                    rows = cells_of(emb_ref, b, c, ty, tz, half)
                    part = dot(turned_pg[bc, :, 256 * half : 256 * half + 256], rows, 1, 0)
                    acc = part if acc is None else acc + part
            for tx in range(3):
                total = jnp.zeros((16, 256), F32)
                for x in range(16):
                    if 0 <= x + tx - 1 < 16:
                        total = jnp.where(lane_x == x + tx - 1, acc[16 * x : 16 * x + 16, :], total)
                tap = 9 * tx + 3 * ty + tz
                total = fold(total, 16) * conv_scale
                for half in range(2):
                    part = jnp.where(own, total[8 * half : 8 * half + 8], 0.0)
                    line = 64 + 32 * half + tap
                    out_ref[line : line + 1, :] = jnp.sum(part, axis=0, keepdims=True)
    for half in range(2):
        out_ref[91 + 32 * half : 96 + 32 * half, :] = jnp.zeros((5, 128), F32)


def finish_kernel(a_ref, b_ref, c_ref, d_ref, down_ref, conv_ref):
    total = (a_ref[...] + b_ref[...]) + (c_ref[...] + d_ref[...])
    down = total[:64].T
    for a in range(2):
        for bc in range(4):
            at = (2 * (2 * (bc % 2) + bc // 2) + a) * 16
            down_ref[4 * a + bc] = down[at : at + 16, :]
    for half in range(2):
        conv = total[64 + 32 * half : 96 + 32 * half].T
        conv_ref[128 * half : 128 * half + 128, :] = conv[:, :27]


def kept(*values):
    return [pltpu.with_memory_space_constraint(v, pltpu.HBM) for v in values]


def params(mib):
    return pltpu.CompilerParams(vmem_limit_bytes=mib << 20)


def cost(flops, nbytes):
    return pl.CostEstimate(flops=flops, bytes_accessed=nbytes, transcendentals=0)


def shape(dims, dtype):
    return jax.ShapeDtypeStruct(dims, dtype)


def sum_rounds(count_y, count_z):
    in_z = [1 << k for k in range(count_z.bit_length() - 1)]
    in_y = [count_z << k for k in range(count_y.bit_length() - 1)]
    order = in_z[:1] + in_z[1:2] + in_y[:1] + in_z[2:] + in_y[1:]
    rounds, order = ([order[:1]] if len(order) % 2 else []), order[len(order) % 2 :]
    return rounds + [order[k : k + 2] for k in range(0, len(order), 2)]


def exchanged(value, masks, count):
    masks = list(masks) + [masks[0] ^ masks[1]] if len(masks) == 2 else masks
    return [lax.ppermute(value, ("sy", "sz"), [(i, i ^ m) for i in range(count)]) for m in masks]


def per_device(
    labels, wall_dist, material_table, dist_weight, conv_weight, down_weight, mix_weight, cotangent
):
    count_y = lax.axis_size("sy")
    count_z = lax.axis_size("sz")
    mine = 64 // count_z
    width = mix_weight.shape[1]
    features, first, last = pl.pallas_call(
        feature_kernel,
        out_shape=(shape((32, 128, 80), BF16), shape((32, 80), BF16), shape((32, 80), BF16)),
        in_specs=[HBM] * 2,
        out_specs=(VMEM,) * 3,
        scratch_shapes=[
            pltpu.VMEM((16, 32, 64), jnp.int32),
            pltpu.VMEM((16, 32, 64), BF16),
            pltpu.VMEM((16, 32, 64), F32),
            pltpu.VMEM((32, 80), F32),
            pltpu.VMEM((32, 80), F32),
            pltpu.SemaphoreType.DMA((2,)),
        ],
        compiler_params=params(8),
        cost_estimate=cost(32 * 128 * 64 * 80 * 2, 2 << 20),
        name="features",
    )(*kept(jnp.transpose(labels, (0, 2, 1)), jnp.transpose(wall_dist, (0, 2, 1))))
    up_y = [(i, i + 1) for i in range(count_y - 1)]
    up_z = [(i, i + 1) for i in range(count_z - 1)]
    ylo = lax.ppermute(last, "sy", up_y)
    yhi = lax.ppermute(first, "sy", [(j, i) for i, j in up_y])
    band, pair, pair_t, table = pl.pallas_call(
        weight_kernel,
        out_shape=(
            shape((9, 256, 256), BF16),
            shape((128, 256), BF16),
            shape((256, 128), BF16),
            shape((80, 256), BF16),
        ),
        in_specs=[HBM] * 4,
        out_specs=(VMEM,) * 4,
        scratch_shapes=[
            pltpu.VMEM((16, 16, 27), BF16),
            pltpu.VMEM((8, 16, 64), BF16),
            pltpu.VMEM((4, 16), BF16),
            pltpu.VMEM((1, 16), BF16),
            pltpu.SemaphoreType.DMA((4,)),
        ],
        compiler_params=params(8),
        cost_estimate=cost(27 * 256 * 16 * 256 * 2, 3 << 20),
        name="weights",
    )(
        *kept(
            jnp.transpose(conv_weight, (1, 2, 0)),
            jnp.transpose(down_weight, (0, 2, 1)),
            material_table,
            dist_weight[None],
        )
    )
    ylo, yhi, band, pair, pair_t, table = lax.optimization_barrier(
        (ylo, yhi, band, pair, pair_t, table)
    )

    def whole(z):
        row = lax.broadcasted_iota(jnp.int32, (128, 80), 0)
        face = jnp.where(row == 64, ylo[z][None], features[z])
        return jnp.where(row == 127, yhi[z][None], face)

    zlo = lax.ppermute(whole(31), "sz", up_z)
    zhi = lax.ppermute(whole(0), "sz", [(j, i) for i, j in up_z])
    embedded, slope, hidden, edge = pl.pallas_call(
        inner_kernel,
        out_shape=(
            pltpu.HBM((17, 2, 128, 256), BF16),
            pltpu.HBM((4, 256, 512), F32),
            shape((4, 256, 512), BF16),
            shape((2, 2, 256, 32), F32),
        ),
        in_specs=[VMEM] * 5,
        out_specs=(HBM, HBM, VMEM, VMEM),
        scratch_shapes=[
            pltpu.VMEM((17, 2, 128, 256), BF16),
            pltpu.VMEM((4, 256, 512), F32),
            pltpu.SemaphoreType.DMA((5,)),
        ],
        compiler_params=params(12),
        cost_estimate=cost(3 << 30, 10 << 20),
        name="inner",
    )(features, ylo, yhi, table, band)
    faces, edge_slope, hidden, coarse = pl.pallas_call(
        outer_kernel,
        out_shape=(
            shape((2, 128, 256), BF16),
            shape((2, 2, 256, 32), F32),
            pltpu.HBM((4, 256, 512), BF16),
            pltpu.HBM((1024, 256), BF16),
        ),
        in_specs=[VMEM] * 7,
        out_specs=(VMEM, VMEM, HBM, HBM),
        scratch_shapes=[
            pltpu.VMEM((512, 512), F32),
            pltpu.VMEM((2, 1024, 128), F32),
            pltpu.VMEM((4, 256, 512), BF16),
            pltpu.VMEM((1024, 256), BF16),
            pltpu.SemaphoreType.DMA((3,)),
        ],
        compiler_params=params(8),
        cost_estimate=cost(1 << 30, 4 << 20),
        name="outer",
    )(zlo, zhi, table, band, pair, edge, hidden)

    sent = lax.all_to_all(
        coarse.reshape(count_z, mine * 16, 256), "sz", split_axis=0, concat_axis=0, tiled=True
    )
    block = lambda *dims: pl.BlockSpec(dims, lambda c: (c,) + (0,) * (len(dims) - 1))
    shares = count_y // 2
    mid, back, *mix_parts = pl.pallas_call(
        lambda *refs: mix_kernel(1.0 / math.sqrt(8 * 32 * count_y), *refs),
        grid=(mine,),
        out_shape=[shape((mine, 256, width), BF16), shape((count_z, mine * 16, 256), BF16)]
        + [pltpu.HBM((mine, width // shares, width), F32)] * shares,
        in_specs=[
            pl.BlockSpec(memory_space=pltpu.SMEM),
            pl.BlockSpec((count_z, 16, 256), lambda c: (0, c, 0)),
            block(1, width, width),
            block(1, 256, width),
        ],
        out_specs=[block(1, 256, width), pl.BlockSpec((count_z, 16, 256), lambda c: (0, c, 0))]
        + [block(1, width // shares, width)] * shares,
        scratch_shapes=[pltpu.VMEM((width, width), F32)],
        compiler_params=params(12),
        cost_estimate=cost(mine * 3 * 2 * 256 * width * width, 5 << 20),
        name="mix",
    )(lax.axis_index("sy")[None], sent, mix_weight, cotangent.reshape(mine, 256, width))
    mix_sum = mix_parts[0]
    for k, part in enumerate(mix_parts[1:], 1):
        mix_sum = mix_sum + lax.ppermute(part, "sy", [(i, i ^ (2 * k)) for i in range(count_y)])
    coarse_grad = lax.all_to_all(back, "sz", split_axis=0, concat_axis=0, tiled=True)
    mix_sum, coarse_grad = lax.optimization_barrier((mix_sum, coarse_grad))
    mine_last, other = jnp.split(mix_sum, 2, axis=1)
    mix_grad = mine_last + lax.ppermute(other, "sy", [(i, i ^ 1) for i in range(count_y)])

    cells = 16 * 64 * count_y * 32 * count_z
    sums = pl.pallas_call(
        lambda *refs: backward_kernel(
            1.0 / math.sqrt(cells // 8), 1.0 / math.sqrt(cells), *refs
        ),
        out_shape=shape((128, 128), F32),
        in_specs=[VMEM, HBM, HBM] + [VMEM] * 5,
        out_specs=VMEM,
        scratch_shapes=[
            pltpu.VMEM((512, 512), F32),
            pltpu.VMEM((2, 1024, 128), F32),
            pltpu.VMEM((4, 256, 512), BF16),
            pltpu.VMEM((17, 2, 128, 256), BF16),
            pltpu.VMEM((4, 256, 512), F32),
            pltpu.SemaphoreType.DMA((2,)),
        ],
        compiler_params=params(16),
        cost_estimate=cost(4 << 30, 8 << 20),
        name="backward",
    )(
        coarse_grad.reshape(1024, 256),
        *kept(embedded, slope),
        hidden,
        pair,
        pair_t,
        faces,
        edge_slope,
    )
    rounds = sum_rounds(count_y, count_z)
    for masks in rounds[:-1]:
        parts = [sums] + exchanged(sums, masks, count_y * count_z)
        sums = parts[0] + parts[1] if len(parts) == 2 else (parts[0] + parts[1]) + (parts[2] + parts[3])
    down_grad, conv_grad = pl.pallas_call(
        finish_kernel,
        out_shape=(shape((8, 16, 64), F32), shape((256, 27), F32)),
        in_specs=[VMEM] * 4,
        out_specs=(VMEM,) * 2,
        compiler_params=params(8),
        cost_estimate=cost(1 << 20, 1 << 18),
        name="finish",
    )(sums, *exchanged(sums, rounds[-1], count_y * count_z))
    down_grad = jnp.transpose(down_grad, (0, 2, 1))
    conv_grad = jnp.transpose(conv_grad.reshape(16, 16, 27), (2, 0, 1))
    return (mid.reshape(cotangent.shape), mix_grad, down_grad, conv_grad)


def solution(mesh):
    in_specs = (
        P(None, "sy", "sz"),
        P(None, "sy", "sz"),
        P(),
        P(),
        P(),
        P(),
        P("sz", None, None),
        P("sz", None, "sy", None),
    )
    out_specs = (P("sz", None, "sy", None), P("sz", "sy", None), P(), P())
    return jax.shard_map(
        per_device, mesh=mesh, in_specs=in_specs, out_specs=out_specs, check_vma=False
    )
```

```python
import math

import jax
import jax.numpy as jnp
from jax import lax
from jax.experimental import pallas as pl
from jax.experimental.pallas import tpu as pltpu
from jax.sharding import PartitionSpec as P

F32 = jnp.float32
BF16 = jnp.bfloat16
VMEM = pl.BlockSpec(memory_space=pltpu.VMEM)
HBM = pl.BlockSpec(memory_space=pltpu.HBM)
RUNS = ((64, 0, 32), (0, 32, 96))


def dot(a, b, ca, cb):
    return lax.dot_general(a, b, (((ca,), (cb,)), ((), ())), preferred_element_type=F32)


def iota(shape, dim):
    return lax.broadcasted_iota(jnp.int32, shape, dim)


def fetch(sources, targets, sem):
    copies = [pltpu.make_async_copy(a, b, sem.at[k]) for k, (a, b) in enumerate(zip(sources, targets))]
    for copy in copies:
        copy.start()
    return copies


def feature_kernel(lab_hbm, wd_hbm, out_ref, first_ref, last_ref, lab_s, wd_b, wd_s, first_s, last_s, sem):
    copies = fetch((lab_hbm, wd_hbm), (lab_s, wd_b), sem)
    row = iota((128, 64), 0)
    run, r = row // 32, row % 32
    y = jnp.where(run == 0, 2 * r, jnp.where(run == 1, 2 * r + 1, jnp.where(run == 2, 2 * r - 1, 2 * r + 2)))
    pick = (y == iota((128, 64), 1)).astype(BF16)
    for copy in copies:
        copy.wait()
    wd_s[...] = wd_b[...].astype(F32)
    for z in range(out_ref.shape[0]):
        lab = lab_s[:, z, :]
        parts = [(lab == m).astype(F32).astype(BF16) for m in range(4)]
        parts.append(wd_s[:, z, :].astype(BF16))
        rows = dot(pick, jnp.concatenate(parts, axis=0), 1, 1)
        out_ref[z] = rows.astype(BF16)
        first_s[z : z + 1, :] = rows[0:1, :]
        last_s[z : z + 1, :] = rows[63:64, :]
    first_ref[...] = first_s[...].astype(BF16)
    last_ref[...] = last_s[...].astype(BF16)


def weight_kernel(
    conv_hbm, down_hbm, mat_hbm, dist_hbm, band_ref, pair_ref, pair_t_ref, table_ref,
    conv_ref, down_ref, mat_ref, dist_ref, sem,
):
    copies = fetch(
        (conv_hbm, down_hbm, mat_hbm, dist_hbm), (conv_ref, down_ref, mat_ref, dist_ref), sem
    )
    for copy in copies:
        copy.wait()
    spread = (iota((256, 16), 0) % 16 == iota((256, 16), 1)).astype(BF16)
    taps = conv_ref[...].reshape(256, 27)
    repeat = (iota((27, 432), 0) == iota((27, 432), 1) // 16).astype(BF16)
    own = iota((256, 432), 0) % 16 == iota((256, 432), 1) % 16
    apart = jnp.where(own, dot(taps, repeat, 1, 0), 0.0).astype(BF16)
    gather = (iota((256, 256), 0) % 16 == iota((256, 256), 1) // 16).astype(BF16)
    wide = dot(gather, apart, 1, 0).astype(BF16)
    offset = iota((256, 256), 1) // 16 - iota((256, 256), 0) // 16 + 1
    for t in range(9):
        total = jnp.zeros((256, 256), F32)
        for tx in range(3):
            at = (tx * 9 + t) * 16
            tile = dot(wide[:, at : at + 16], spread, 1, 1)
            total = jnp.where(offset == tx, tile, total)
        band_ref[t] = total.astype(BF16)
    for bc in range(4):
        for x2 in range(2):
            for a in range(2):
                tap = down_ref[4 * a + bc]
                none = jnp.zeros_like(tap)
                at = 64 * bc + 32 * x2 + 16 * a
                pair_t_ref[at : at + 16, :] = jnp.concatenate([none, tap] if x2 else [tap, none], axis=1)
    pair_ref[...] = pair_t_ref[...].T
    lane_e = iota((16, 256), 1) // 16
    row_e = iota((16, 256), 0)
    mat = dot(mat_ref[...], spread, 1, 1)
    dist = dot(dist_ref[...], spread, 1, 1)
    for m in range(5):
        line = jnp.broadcast_to(mat[m : m + 1, :] if m < 4 else dist, (16, 256))
        table_ref[16 * m : 16 * m + 16, :] = jnp.where(lane_e == row_e, line, 0.0).astype(BF16)


def activate(acc):
    sigma = jax.nn.sigmoid(acc)
    return (acc * sigma).astype(BF16), sigma * (1.0 + acc * (1.0 - sigma))


def cells_of(emb_ref, b, c, ty, tz, half):
    run = RUNS[b][ty]
    q = (c + tz) // 2 + 8 * half
    return emb_ref[q : q + 8, (c + tz) % 2, run : run + 32, :].reshape(256, 256)


def inner_kernel(
    feat_ref, ylo_ref, yhi_ref, table_ref, band_ref, emb_ref, slope_ref, hidden_ref, edge_ref,
):
    table = table_ref[...]
    row = iota((128, 80), 0)
    emb_ref[0, 0] = jnp.zeros((128, 256), BF16)
    emb_ref[16, 1] = jnp.zeros((128, 256), BF16)
    ylo = ylo_ref[...].astype(F32)
    yhi = yhi_ref[...].astype(F32)
    for z in range(32):
        f = feat_ref[z].astype(F32)
        f = jnp.where(row == 64, ylo[z : z + 1, :], f)
        f = jnp.where(row == 127, yhi[z : z + 1, :], f)
        emb_ref[(z + 1) // 2, (z + 1) % 2] = dot(f.astype(BF16), table, 1, 0).astype(BF16)
    for bc in range(4):
        b, c = bc // 2, bc % 2
        for half in range(2):
            acc = None
            for ty in range(3):
                for tz in range(3):
                    part = dot(band_ref[3 * ty + tz], cells_of(emb_ref, b, c, ty, tz, half), 1, 1)
                    acc = part if acc is None else acc + part
            if half == 0 and c == 0:
                edge_ref[0, b] = acc[:, :32]
            if half == 1 and c == 1:
                edge_ref[1, b] = acc[:, 224:]
            at = slice(256 * half, 256 * half + 256)
            hidden_ref[bc, :, at], slope_ref[bc, :, at] = activate(acc)


def pair_rows(hidden_ref, pair):
    return jnp.concatenate([hidden_ref[bc, 64 * pair : 64 * pair + 64, :] for bc in range(4)], axis=0)


def outer_kernel(
    zlo_ref, zhi_ref, table_ref, band_ref, pair_ref, edge_ref, inner_ref,
    emb_ref, slope_ref, hidden_hbm, coarse_hbm, turn_a, turn_b, hidden_ref, coarse_ref, sem,
):
    table = table_ref[...]
    hidden_ref[...] = inner_ref[...]
    for side, face in enumerate((zlo_ref, zhi_ref)):
        plane = dot(face[...], table, 1, 0).astype(BF16)
        emb_ref[side] = plane
        for b in range(2):
            acc = edge_ref[side, b]
            for ty in range(3):
                run = RUNS[b][ty]
                acc = acc + dot(band_ref[3 * ty + 2 * side], plane[run : run + 32], 1, 1)
            at = slice(480 * side, 480 * side + 32)
            hidden_ref[2 * b + side, :, at], slope_ref[:, 64 * side + 32 * b : 64 * side + 32 * b + 32] = activate(acc)
    copies = [pltpu.make_async_copy(hidden_ref, hidden_hbm, sem.at[0])]
    copies[0].start()
    for pair in range(4):
        turn_a[128 * pair : 128 * pair + 128, :] = dot(pair_ref[...], pair_rows(hidden_ref, pair), 1, 0)
    for half in range(2):
        for z2 in range(16):
            pieces = [
                turn_a[64 * x2 : 64 * x2 + 64, 32 * z2 : 32 * z2 + 32]
                for x2 in range(4 * half, 4 * half + 4)
            ]
            turn_b[half, pl.ds(z2, 64, stride=16), :] = jnp.concatenate(pieces, axis=1)
        at = (slice(None), pl.ds(128 * half, 128))
        coarse_ref[at] = turn_b[half].astype(BF16)
        copies.append(pltpu.make_async_copy(coarse_ref.at[at], coarse_hbm.at[at], sem.at[1 + half]))
        copies[-1].start()
    for copy in copies:
        copy.wait()


def mixed(coarse_ref, mix_ref, cot_ref):
    width = mix_ref.shape[1]
    flat = coarse_ref[...].reshape(width, 256).T
    pre = dot(flat, mix_ref[0], 1, 1)
    sigma = jax.nn.sigmoid(pre)
    grad = cot_ref[0].astype(F32) * (sigma * (1.0 + pre * (1.0 - sigma)))
    return flat, pre * sigma, grad.astype(BF16).T


def mix_kernel(coarse_ref, mix_ref, cot_ref, grad_ref):
    _, _, turned = mixed(coarse_ref, mix_ref, cot_ref)
    grad_ref[...] = dot(mix_ref[0].T, turned, 1, 0).astype(BF16).reshape(grad_ref.shape)


def mix_grad_kernel(scale, me_ref, coarse_ref, mix_ref, cot_ref, mid_ref, *more_refs):
    *share_refs, total_ref = more_refs
    flat, mid, turned = mixed(coarse_ref, mix_ref, cot_ref)
    mid_ref[0] = mid.astype(BF16)
    total_ref[...] = dot(turned, flat, 1, 0) * scale
    rows = total_ref.shape[0] // (2 * len(share_refs))
    for place in range(2 * len(share_refs)):
        start = pl.multiple_of(jnp.bitwise_xor(me_ref[0], place) * rows, rows)
        at = place % 2 * rows
        share_refs[place // 2][0, at : at + rows, :] = total_ref[pl.ds(start, rows), :]


def fold(value, step):
    lanes = value.shape[-1]
    if lanes == 256:
        value = value[:, :128] + value[:, 128:]
    shift = 64
    while shift >= step:
        value = value + pltpu.roll(value, shift, 1)
        shift //= 2
    return value


def backward_kernel(
    down_scale, conv_scale, cgrad_ref, emb_hbm, slope_hbm, hidden_ref, pair_ref, pair_t_ref, face_ref, edge_ref,
    out_ref, turn_a, turn_b, turned_pg, emb_in, slope_in, sem,
):
    copies = [
        pltpu.make_async_copy(slope_hbm, slope_in, sem.at[0]),
        pltpu.make_async_copy(emb_hbm, emb_in, sem.at[1]),
    ]
    copies[0].start()
    for half in range(2):
        turn_b[half] = cgrad_ref[:, 128 * half : 128 * half + 128].astype(F32)
    for half in range(2):
        for quad in range(4):
            pieces = [turn_b[half, pl.ds(4 * quad + k, 64, stride=16), :] for k in range(4)]
            for k in range(4):
                x2 = 4 * half + k
                turn_a[64 * x2 : 64 * x2 + 64, 128 * quad : 128 * quad + 128] = jnp.concatenate(
                    [p[:, 32 * k : 32 * k + 32] for p in pieces], axis=1
                )
    copies[1].start()
    cg_t = turn_a[...].astype(BF16)
    pairs = [cg_t[128 * pair : 128 * pair + 128, :] for pair in range(4)]
    down = None
    for pair in range(4):
        part = dot(pairs[pair], pair_rows(hidden_ref, pair), 1, 1)
        down = part if down is None else down + part
    down = jnp.where(iota((64, 256), 1) // 32 % 2 == 0, down[:64], down[64:]) * down_scale
    left = down[:, :128] + pltpu.roll(down[:, :128], 96, 1)
    right = down[:, 128:] + pltpu.roll(down[:, 128:], 32, 1)
    out_ref[0:64, :] = jnp.where(iota((64, 128), 1) // 32 % 2 == 0, left, right)
    copies[0].wait()
    for pair in range(4):
        hgrad = dot(pair_t_ref[...], pairs[pair], 1, 0)
        at = slice(64 * pair, 64 * pair + 64)
        for bc in range(4):
            rows = hgrad[64 * bc : 64 * bc + 64]
            turned_pg[bc, at, :] = (rows * slope_in[bc, at, :]).astype(BF16)
            edge = slice(480 * (bc % 2), 480 * (bc % 2) + 32)
            low = 64 * (bc % 2) + 32 * (bc // 2)
            turned_pg[bc, at, edge] = (rows[:, edge] * edge_ref[at, low : low + 32]).astype(BF16)
    copies[1].wait()
    lane_x = iota((16, 256), 1) // 16
    own = iota((8, 128), 1) // 16 == iota((8, 128), 0)
    for ty in range(3):
        for tz in range(3):
            acc = None
            for bc in range(4):
                b, c = bc // 2, bc % 2
                for half in range(2):
                    rows = cells_of(emb_in, b, c, ty, tz, half)
                    run = RUNS[b][ty]
                    if c + tz == 0 and half == 0:
                        rows = jnp.concatenate([face_ref[0, run : run + 32, :], rows[32:]], axis=0)
                    if c + tz == 3 and half == 1:
                        rows = jnp.concatenate([rows[:224], face_ref[1, run : run + 32, :]], axis=0)
                    part = dot(turned_pg[bc, :, 256 * half : 256 * half + 256], rows, 1, 0)
                    acc = part if acc is None else acc + part
            for tx in range(3):
                total = jnp.zeros((16, 256), F32)
                for x in range(16):
                    if 0 <= x + tx - 1 < 16:
                        total = jnp.where(lane_x == x + tx - 1, acc[16 * x : 16 * x + 16, :], total)
                tap = 9 * tx + 3 * ty + tz
                total = fold(total, 16) * conv_scale
                for half in range(2):
                    part = jnp.where(own, total[8 * half : 8 * half + 8], 0.0)
                    line = 64 + 32 * half + tap
                    out_ref[line : line + 1, :] = jnp.sum(part, axis=0, keepdims=True)
    for half in range(2):
        out_ref[91 + 32 * half : 96 + 32 * half, :] = jnp.zeros((5, 128), F32)


def finish_kernel(a_ref, b_ref, c_ref, d_ref, down_ref, conv_ref):
    total = (a_ref[...] + b_ref[...]) + (c_ref[...] + d_ref[...])
    down = total[:64].T
    for a in range(2):
        for bc in range(4):
            at = (2 * (2 * (bc % 2) + bc // 2) + a) * 16
            down_ref[4 * a + bc] = down[at : at + 16, :]
    for half in range(2):
        conv = total[64 + 32 * half : 96 + 32 * half].T
        conv_ref[128 * half : 128 * half + 128, :] = conv[:, :27]


def kept(*values):
    return [pltpu.with_memory_space_constraint(v, pltpu.HBM) for v in values]


def params(mib):
    return pltpu.CompilerParams(vmem_limit_bytes=mib << 20)


def cost(flops, nbytes):
    return pl.CostEstimate(flops=flops, bytes_accessed=nbytes, transcendentals=0)


def shape(dims, dtype):
    return jax.ShapeDtypeStruct(dims, dtype)


def sum_rounds(count_y, count_z):
    in_z = [1 << k for k in range(count_z.bit_length() - 1)]
    in_y = [count_z << k for k in range(count_y.bit_length() - 1)]
    order = in_z[:1] + in_z[1:2] + in_y[:1] + in_z[2:] + in_y[1:]
    rounds, order = ([order[:1]] if len(order) % 2 else []), order[len(order) % 2 :]
    return rounds + [order[k : k + 2] for k in range(0, len(order), 2)]


def exchanged(value, masks, count):
    masks = list(masks) + [masks[0] ^ masks[1]] if len(masks) == 2 else masks
    return [lax.ppermute(value, ("sy", "sz"), [(i, i ^ m) for i in range(count)]) for m in masks]


def per_device(
    labels, wall_dist, material_table, dist_weight, conv_weight, down_weight, mix_weight, cotangent
):
    count_y = lax.axis_size("sy")
    count_z = lax.axis_size("sz")
    mine = 64 // count_z
    width = mix_weight.shape[1]
    features, first, last = pl.pallas_call(
        feature_kernel,
        out_shape=(shape((32, 128, 80), BF16), shape((32, 80), BF16), shape((32, 80), BF16)),
        in_specs=[HBM] * 2,
        out_specs=(VMEM,) * 3,
        scratch_shapes=[
            pltpu.VMEM((16, 32, 64), jnp.int32),
            pltpu.VMEM((16, 32, 64), BF16),
            pltpu.VMEM((16, 32, 64), F32),
            pltpu.VMEM((32, 80), F32),
            pltpu.VMEM((32, 80), F32),
            pltpu.SemaphoreType.DMA((2,)),
        ],
        compiler_params=params(8),
        cost_estimate=cost(32 * 128 * 64 * 80 * 2, 2 << 20),
        name="features",
    )(*kept(jnp.transpose(labels, (0, 2, 1)), jnp.transpose(wall_dist, (0, 2, 1))))
    up_y = [(i, i + 1) for i in range(count_y - 1)]
    up_z = [(i, i + 1) for i in range(count_z - 1)]
    ylo = lax.ppermute(last, "sy", up_y)
    yhi = lax.ppermute(first, "sy", [(j, i) for i, j in up_y])
    band, pair, pair_t, table = pl.pallas_call(
        weight_kernel,
        out_shape=(
            shape((9, 256, 256), BF16),
            shape((128, 256), BF16),
            shape((256, 128), BF16),
            shape((80, 256), BF16),
        ),
        in_specs=[HBM] * 4,
        out_specs=(VMEM,) * 4,
        scratch_shapes=[
            pltpu.VMEM((16, 16, 27), BF16),
            pltpu.VMEM((8, 16, 64), BF16),
            pltpu.VMEM((4, 16), BF16),
            pltpu.VMEM((1, 16), BF16),
            pltpu.SemaphoreType.DMA((4,)),
        ],
        compiler_params=params(8),
        cost_estimate=cost(27 * 256 * 16 * 256 * 2, 3 << 20),
        name="weights",
    )(
        *kept(
            jnp.transpose(conv_weight, (1, 2, 0)),
            jnp.transpose(down_weight, (0, 2, 1)),
            material_table,
            dist_weight[None],
        )
    )
    ylo, yhi, band, pair, pair_t, table = lax.optimization_barrier(
        (ylo, yhi, band, pair, pair_t, table)
    )

    def whole(z):
        row = lax.broadcasted_iota(jnp.int32, (128, 80), 0)
        face = jnp.where(row == 64, ylo[z][None], features[z])
        return jnp.where(row == 127, yhi[z][None], face)

    zlo = lax.ppermute(whole(31), "sz", up_z)
    zhi = lax.ppermute(whole(0), "sz", [(j, i) for i, j in up_z])
    embedded, slope, hidden, edge = pl.pallas_call(
        inner_kernel,
        out_shape=(
            shape((17, 2, 128, 256), BF16),
            shape((4, 256, 512), F32),
            shape((4, 256, 512), BF16),
            shape((2, 2, 256, 32), F32),
        ),
        in_specs=[VMEM] * 5,
        out_specs=(VMEM,) * 4,
        compiler_params=params(12),
        cost_estimate=cost(3 << 30, 10 << 20),
        name="inner",
    )(features, ylo, yhi, table, band)
    faces, edge_slope, hidden, coarse = pl.pallas_call(
        outer_kernel,
        out_shape=(
            shape((2, 128, 256), BF16),
            shape((256, 128), F32),
            pltpu.HBM((4, 256, 512), BF16),
            pltpu.HBM((1024, 256), BF16),
        ),
        in_specs=[VMEM] * 7,
        out_specs=(VMEM, VMEM, HBM, HBM),
        scratch_shapes=[
            pltpu.VMEM((512, 512), F32),
            pltpu.VMEM((2, 1024, 128), F32),
            pltpu.VMEM((4, 256, 512), BF16),
            pltpu.VMEM((1024, 256), BF16),
            pltpu.SemaphoreType.DMA((3,)),
        ],
        compiler_params=params(8),
        cost_estimate=cost(1 << 30, 4 << 20),
        name="outer",
    )(zlo, zhi, table, band, pair, edge, hidden)

    sent = lax.all_to_all(
        coarse.reshape(count_z, mine * 16, 256), "sz", split_axis=0, concat_axis=0, tiled=True
    )
    block = lambda *dims: pl.BlockSpec(dims, lambda c: (c,) + (0,) * (len(dims) - 1))
    shares = count_y // 2
    mix_specs = [
        pl.BlockSpec((count_z, 16, 256), lambda c: (0, c, 0)),
        block(1, width, width),
        block(1, 256, width),
    ]
    cotangent_rows = cotangent.reshape(mine, 256, width)
    back = pl.pallas_call(
        mix_kernel,
        grid=(mine,),
        out_shape=shape((count_z, mine * 16, 256), BF16),
        in_specs=mix_specs,
        out_specs=pl.BlockSpec((count_z, 16, 256), lambda c: (0, c, 0)),
        compiler_params=params(8),
        cost_estimate=cost(mine * 2 * 2 * 256 * width * width, 2 << 20),
        name="mix",
    )(sent, mix_weight, cotangent_rows)
    coarse_grad = lax.all_to_all(back, "sz", split_axis=0, concat_axis=0, tiled=True)
    sent, back = lax.optimization_barrier((sent, back))
    mid, *mix_parts = pl.pallas_call(
        lambda *refs: mix_grad_kernel(1.0 / math.sqrt(8 * 32 * count_y), *refs),
        grid=(mine,),
        out_shape=[shape((mine, 256, width), BF16)]
        + [pltpu.HBM((mine, width // shares, width), F32)] * shares,
        in_specs=[pl.BlockSpec(memory_space=pltpu.SMEM)] + mix_specs,
        out_specs=[block(1, 256, width)] + [block(1, width // shares, width)] * shares,
        scratch_shapes=[pltpu.VMEM((width, width), F32)],
        compiler_params=params(8),
        cost_estimate=cost(mine * 2 * 2 * 256 * width * width, 3 << 20),
        name="mix_grad",
    )(lax.axis_index("sy")[None], sent, mix_weight, cotangent_rows)
    *mix_parts, coarse_grad = lax.optimization_barrier((*mix_parts, coarse_grad))
    mix_sum = mix_parts[0]
    for k, part in enumerate(mix_parts[1:], 1):
        mix_sum = mix_sum + lax.ppermute(part, "sy", [(i, i ^ (2 * k)) for i in range(count_y)])
    mine_last, other = jnp.split(mix_sum, 2, axis=1)
    mix_grad = mine_last + lax.ppermute(other, "sy", [(i, i ^ 1) for i in range(count_y)])

    cells = 16 * 64 * count_y * 32 * count_z
    sums = pl.pallas_call(
        lambda *refs: backward_kernel(
            1.0 / math.sqrt(cells // 8), 1.0 / math.sqrt(cells), *refs
        ),
        out_shape=shape((128, 128), F32),
        in_specs=[VMEM, HBM, HBM] + [VMEM] * 5,
        out_specs=VMEM,
        scratch_shapes=[
            pltpu.VMEM((512, 512), F32),
            pltpu.VMEM((2, 1024, 128), F32),
            pltpu.VMEM((4, 256, 512), BF16),
            pltpu.VMEM((17, 2, 128, 256), BF16),
            pltpu.VMEM((4, 256, 512), F32),
            pltpu.SemaphoreType.DMA((2,)),
        ],
        compiler_params=params(12),
        cost_estimate=cost(4 << 30, 8 << 20),
        name="backward",
    )(
        coarse_grad.reshape(1024, 256),
        *kept(embedded, slope),
        hidden,
        pair,
        pair_t,
        faces,
        edge_slope,
    )
    rounds = sum_rounds(count_y, count_z)
    for masks in rounds[:-1]:
        parts = [sums] + exchanged(sums, masks, count_y * count_z)
        sums = parts[0] + parts[1] if len(parts) == 2 else (parts[0] + parts[1]) + (parts[2] + parts[3])
    down_grad, conv_grad = pl.pallas_call(
        finish_kernel,
        out_shape=(shape((8, 16, 64), F32), shape((256, 27), F32)),
        in_specs=[VMEM] * 4,
        out_specs=(VMEM,) * 2,
        compiler_params=params(8),
        cost_estimate=cost(1 << 20, 1 << 18),
        name="finish",
    )(sums, *exchanged(sums, rounds[-1], count_y * count_z))
    down_grad = jnp.transpose(down_grad, (0, 2, 1))
    conv_grad = jnp.transpose(conv_grad.reshape(16, 16, 27), (2, 0, 1))
    return (mid.reshape(cotangent.shape), mix_grad, down_grad, conv_grad)


def solution(mesh):
    in_specs = (
        P(None, "sy", "sz"),
        P(None, "sy", "sz"),
        P(),
        P(),
        P(),
        P(),
        P("sz", None, None),
        P("sz", None, "sy", None),
    )
    out_specs = (P("sz", None, "sy", None), P("sz", "sy", None), P(), P())
    return jax.shard_map(
        per_device, mesh=mesh, in_specs=in_specs, out_specs=out_specs, check_vma=False
    )
```

```python
import math

import jax
import jax.numpy as jnp
from jax import lax
from jax.experimental import pallas as pl
from jax.experimental.pallas import tpu as pltpu
from jax.sharding import PartitionSpec as P

F32 = jnp.float32
BF16 = jnp.bfloat16
VMEM = pl.BlockSpec(memory_space=pltpu.VMEM)
HBM = pl.BlockSpec(memory_space=pltpu.HBM)
RUNS = ((64, 0, 32), (0, 32, 96))


def dot(a, b, ca, cb):
    return lax.dot_general(a, b, (((ca,), (cb,)), ((), ())), preferred_element_type=F32)


def iota(shape, dim):
    return lax.broadcasted_iota(jnp.int32, shape, dim)


def fetch(sources, targets, sem):
    copies = [pltpu.make_async_copy(a, b, sem.at[k]) for k, (a, b) in enumerate(zip(sources, targets))]
    for copy in copies:
        copy.start()
    return copies


def feature_kernel(lab_hbm, wd_hbm, out_ref, first_ref, last_ref, lab_s, wd_b, wd_s, first_s, last_s, sem):
    copies = fetch((lab_hbm, wd_hbm), (lab_s, wd_b), sem)
    row = iota((128, 64), 0)
    run, r = row // 32, row % 32
    y = jnp.where(run == 0, 2 * r, jnp.where(run == 1, 2 * r + 1, jnp.where(run == 2, 2 * r - 1, 2 * r + 2)))
    pick = (y == iota((128, 64), 1)).astype(BF16)
    for copy in copies:
        copy.wait()
    wd_s[...] = wd_b[...].astype(F32)
    for z in range(out_ref.shape[0]):
        lab = lab_s[:, z, :]
        parts = [(lab == m).astype(F32).astype(BF16) for m in range(4)]
        parts.append(wd_s[:, z, :].astype(BF16))
        rows = dot(pick, jnp.concatenate(parts, axis=0), 1, 1)
        out_ref[z] = rows.astype(BF16)
        first_s[z : z + 1, :] = rows[0:1, :]
        last_s[z : z + 1, :] = rows[63:64, :]
    first_ref[...] = first_s[...].astype(BF16)
    last_ref[...] = last_s[...].astype(BF16)


def weight_kernel(
    conv_hbm, down_hbm, mat_hbm, dist_hbm, band_ref, pair_ref, pair_t_ref, table_ref,
    conv_ref, down_ref, mat_ref, dist_ref, sem,
):
    copies = fetch(
        (conv_hbm, down_hbm, mat_hbm, dist_hbm), (conv_ref, down_ref, mat_ref, dist_ref), sem
    )
    for copy in copies:
        copy.wait()
    spread = (iota((256, 16), 0) % 16 == iota((256, 16), 1)).astype(BF16)
    taps = conv_ref[...].reshape(256, 27)
    repeat = (iota((27, 432), 0) == iota((27, 432), 1) // 16).astype(BF16)
    own = iota((256, 432), 0) % 16 == iota((256, 432), 1) % 16
    apart = jnp.where(own, dot(taps, repeat, 1, 0), 0.0).astype(BF16)
    gather = (iota((256, 256), 0) % 16 == iota((256, 256), 1) // 16).astype(BF16)
    wide = dot(gather, apart, 1, 0).astype(BF16)
    offset = iota((256, 256), 1) // 16 - iota((256, 256), 0) // 16 + 1
    for t in range(9):
        total = jnp.zeros((256, 256), F32)
        for tx in range(3):
            at = (tx * 9 + t) * 16
            tile = dot(wide[:, at : at + 16], spread, 1, 1)
            total = jnp.where(offset == tx, tile, total)
        band_ref[t] = total.astype(BF16)
    for bc in range(4):
        for x2 in range(2):
            for a in range(2):
                tap = down_ref[4 * a + bc]
                none = jnp.zeros_like(tap)
                at = 64 * bc + 32 * x2 + 16 * a
                pair_t_ref[at : at + 16, :] = jnp.concatenate([none, tap] if x2 else [tap, none], axis=1)
    pair_ref[...] = pair_t_ref[...].T
    lane_e = iota((16, 256), 1) // 16
    row_e = iota((16, 256), 0)
    mat = dot(mat_ref[...], spread, 1, 1)
    dist = dot(dist_ref[...], spread, 1, 1)
    for m in range(5):
        line = jnp.broadcast_to(mat[m : m + 1, :] if m < 4 else dist, (16, 256))
        table_ref[16 * m : 16 * m + 16, :] = jnp.where(lane_e == row_e, line, 0.0).astype(BF16)


def activate(acc):
    sigma = jax.nn.sigmoid(acc)
    return (acc * sigma).astype(BF16), sigma * (1.0 + acc * (1.0 - sigma))


def cells_of(emb_ref, b, c, ty, tz, half):
    run = RUNS[b][ty]
    q = (c + tz) // 2 + 8 * half
    return emb_ref[q : q + 8, (c + tz) % 2, run : run + 32, :].reshape(256, 256)


def inner_kernel(
    feat_ref, ylo_ref, yhi_ref, table_ref, band_ref, emb_ref, slope_ref, hidden_ref, edge_ref,
):
    table = table_ref[...]
    row = iota((128, 80), 0)
    emb_ref[0, 0] = jnp.zeros((128, 256), BF16)
    emb_ref[16, 1] = jnp.zeros((128, 256), BF16)
    ylo = ylo_ref[...].astype(F32)
    yhi = yhi_ref[...].astype(F32)
    for z in range(32):
        f = feat_ref[z].astype(F32)
        f = jnp.where(row == 64, ylo[z : z + 1, :], f)
        f = jnp.where(row == 127, yhi[z : z + 1, :], f)
        emb_ref[(z + 1) // 2, (z + 1) % 2] = dot(f.astype(BF16), table, 1, 0).astype(BF16)
    for bc in range(4):
        b, c = bc // 2, bc % 2
        for half in range(2):
            acc = None
            for ty in range(3):
                for tz in range(3):
                    part = dot(band_ref[3 * ty + tz], cells_of(emb_ref, b, c, ty, tz, half), 1, 1)
                    acc = part if acc is None else acc + part
            if half == 0 and c == 0:
                edge_ref[0, b] = acc[:, :32]
            if half == 1 and c == 1:
                edge_ref[1, b] = acc[:, 224:]
            at = slice(256 * half, 256 * half + 256)
            hidden_ref[bc, :, at], slope_ref[bc, :, at] = activate(acc)


def pair_rows(hidden_ref, pair):
    return jnp.concatenate([hidden_ref[bc, 64 * pair : 64 * pair + 64, :] for bc in range(4)], axis=0)


def outer_kernel(
    zlo_ref, zhi_ref, table_ref, band_ref, pair_ref, edge_ref, inner_ref,
    emb_ref, slope_ref, hidden_hbm, coarse_hbm, turn_a, turn_b, hidden_ref, coarse_ref, sem,
):
    table = table_ref[...]
    hidden_ref[...] = inner_ref[...]
    for side, face in enumerate((zlo_ref, zhi_ref)):
        plane = dot(face[...], table, 1, 0).astype(BF16)
        emb_ref[side] = plane
        for b in range(2):
            acc = edge_ref[side, b]
            for ty in range(3):
                run = RUNS[b][ty]
                acc = acc + dot(band_ref[3 * ty + 2 * side], plane[run : run + 32], 1, 1)
            at = slice(480 * side, 480 * side + 32)
            hidden_ref[2 * b + side, :, at], slope_ref[:, 64 * side + 32 * b : 64 * side + 32 * b + 32] = activate(acc)
    copies = [pltpu.make_async_copy(hidden_ref, hidden_hbm, sem.at[0])]
    copies[0].start()
    for pair in range(4):
        turn_a[128 * pair : 128 * pair + 128, :] = dot(pair_ref[...], pair_rows(hidden_ref, pair), 1, 0)
    for half in range(2):
        for z2 in range(16):
            pieces = [
                turn_a[64 * x2 : 64 * x2 + 64, 32 * z2 : 32 * z2 + 32]
                for x2 in range(4 * half, 4 * half + 4)
            ]
            turn_b[half, pl.ds(z2, 64, stride=16), :] = jnp.concatenate(pieces, axis=1)
        at = (slice(None), pl.ds(128 * half, 128))
        coarse_ref[at] = turn_b[half].astype(BF16)
        copies.append(pltpu.make_async_copy(coarse_ref.at[at], coarse_hbm.at[at], sem.at[1 + half]))
        copies[-1].start()
    for copy in copies:
        copy.wait()


def mixed(coarse_ref, mix_ref, cot_ref):
    width = mix_ref.shape[1]
    flat = coarse_ref[...].reshape(width, 256).T
    pre = dot(flat, mix_ref[0], 1, 1)
    sigma = jax.nn.sigmoid(pre)
    grad = cot_ref[0].astype(F32) * (sigma * (1.0 + pre * (1.0 - sigma)))
    return flat, pre * sigma, grad.astype(BF16).T


def mix_kernel(coarse_ref, mix_ref, cot_ref, grad_ref):
    _, _, turned = mixed(coarse_ref, mix_ref, cot_ref)
    grad_ref[...] = dot(mix_ref[0].T, turned, 1, 0).astype(BF16).reshape(grad_ref.shape)


def mix_grad_kernel(scale, me_ref, coarse_ref, mix_ref, cot_ref, mid_ref, *more_refs):
    *share_refs, total_ref = more_refs
    flat, mid, turned = mixed(coarse_ref, mix_ref, cot_ref)
    mid_ref[0] = mid.astype(BF16)
    total_ref[...] = dot(turned, flat, 1, 0) * scale
    rows = total_ref.shape[0] // (2 * len(share_refs))
    for place in range(2 * len(share_refs)):
        start = pl.multiple_of(jnp.bitwise_xor(me_ref[0], place) * rows, rows)
        at = place % 2 * rows
        share_refs[place // 2][0, at : at + rows, :] = total_ref[pl.ds(start, rows), :]


def fold(value, step):
    lanes = value.shape[-1]
    if lanes == 256:
        value = value[:, :128] + value[:, 128:]
    shift = 64
    while shift >= step:
        value = value + pltpu.roll(value, shift, 1)
        shift //= 2
    return value


def backward_kernel(
    down_scale, conv_scale, cgrad_ref, emb_hbm, slope_hbm, hidden_ref, pair_ref, pair_t_ref, face_ref, edge_ref,
    out_ref, turn_a, turn_b, turned_pg, emb_in, slope_in, sem,
):
    copies = [
        pltpu.make_async_copy(slope_hbm, slope_in, sem.at[0]),
        pltpu.make_async_copy(emb_hbm, emb_in, sem.at[1]),
    ]
    copies[0].start()
    for half in range(2):
        turn_b[half] = cgrad_ref[:, 128 * half : 128 * half + 128].astype(F32)
    for half in range(2):
        for quad in range(4):
            pieces = [turn_b[half, pl.ds(4 * quad + k, 64, stride=16), :] for k in range(4)]
            for k in range(4):
                x2 = 4 * half + k
                turn_a[64 * x2 : 64 * x2 + 64, 128 * quad : 128 * quad + 128] = jnp.concatenate(
                    [p[:, 32 * k : 32 * k + 32] for p in pieces], axis=1
                )
    copies[1].start()
    cg_t = turn_a[...].astype(BF16)
    pairs = [cg_t[128 * pair : 128 * pair + 128, :] for pair in range(4)]
    down = None
    for pair in range(4):
        part = dot(pairs[pair], pair_rows(hidden_ref, pair), 1, 1)
        down = part if down is None else down + part
    down = jnp.where(iota((64, 256), 1) // 32 % 2 == 0, down[:64], down[64:]) * down_scale
    left = down[:, :128] + pltpu.roll(down[:, :128], 96, 1)
    right = down[:, 128:] + pltpu.roll(down[:, 128:], 32, 1)
    out_ref[0:64, :] = jnp.where(iota((64, 128), 1) // 32 % 2 == 0, left, right)
    copies[0].wait()
    for pair in range(4):
        hgrad = dot(pair_t_ref[...], pairs[pair], 1, 0)
        at = slice(64 * pair, 64 * pair + 64)
        for bc in range(4):
            rows = hgrad[64 * bc : 64 * bc + 64]
            turned_pg[bc, at, :] = (rows * slope_in[bc, at, :]).astype(BF16)
            edge = slice(480 * (bc % 2), 480 * (bc % 2) + 32)
            low = 64 * (bc % 2) + 32 * (bc // 2)
            turned_pg[bc, at, edge] = (rows[:, edge] * edge_ref[at, low : low + 32]).astype(BF16)
    copies[1].wait()
    lane_x = iota((16, 256), 1) // 16
    own = iota((8, 128), 1) // 16 == iota((8, 128), 0)
    for ty in range(3):
        for tz in range(3):
            acc = None
            for bc in range(4):
                b, c = bc // 2, bc % 2
                for half in range(2):
                    rows = cells_of(emb_in, b, c, ty, tz, half)
                    run = RUNS[b][ty]
                    if c + tz == 0 and half == 0:
                        rows = jnp.concatenate([face_ref[0, run : run + 32, :], rows[32:]], axis=0)
                    if c + tz == 3 and half == 1:
                        rows = jnp.concatenate([rows[:224], face_ref[1, run : run + 32, :]], axis=0)
                    part = dot(turned_pg[bc, :, 256 * half : 256 * half + 256], rows, 1, 0)
                    acc = part if acc is None else acc + part
            for tx in range(3):
                total = jnp.zeros((16, 256), F32)
                for x in range(16):
                    if 0 <= x + tx - 1 < 16:
                        total = jnp.where(lane_x == x + tx - 1, acc[16 * x : 16 * x + 16, :], total)
                tap = 9 * tx + 3 * ty + tz
                total = fold(total, 16) * conv_scale
                for half in range(2):
                    part = jnp.where(own, total[8 * half : 8 * half + 8], 0.0)
                    line = 64 + 32 * half + tap
                    out_ref[line : line + 1, :] = jnp.sum(part, axis=0, keepdims=True)
    for half in range(2):
        out_ref[91 + 32 * half : 96 + 32 * half, :] = jnp.zeros((5, 128), F32)


def finish_kernel(a_ref, b_ref, c_ref, d_ref, down_ref, conv_ref):
    total = (a_ref[...] + b_ref[...]) + (c_ref[...] + d_ref[...])
    down = total[:64].T
    for a in range(2):
        for bc in range(4):
            at = (2 * (2 * (bc % 2) + bc // 2) + a) * 16
            down_ref[4 * a + bc] = down[at : at + 16, :]
    for half in range(2):
        conv = total[64 + 32 * half : 96 + 32 * half].T
        conv_ref[128 * half : 128 * half + 128, :] = conv[:, :27]


def kept(*values):
    return [pltpu.with_memory_space_constraint(v, pltpu.HBM) for v in values]


def params(mib):
    return pltpu.CompilerParams(vmem_limit_bytes=mib << 20)


def cost(flops, nbytes):
    return pl.CostEstimate(flops=flops, bytes_accessed=nbytes, transcendentals=0)


def shape(dims, dtype):
    return jax.ShapeDtypeStruct(dims, dtype)


def sum_rounds(count_y, count_z):
    in_z = [1 << k for k in range(count_z.bit_length() - 1)]
    in_y = [count_z << k for k in range(count_y.bit_length() - 1)]
    order = in_z[:1] + in_z[1:2] + in_y[:1] + in_z[2:] + in_y[1:]
    rounds, order = ([order[:1]] if len(order) % 2 else []), order[len(order) % 2 :]
    return rounds + [order[k : k + 2] for k in range(0, len(order), 2)]


def exchanged(value, masks, count):
    masks = list(masks) + [masks[0] ^ masks[1]] if len(masks) == 2 else masks
    return [lax.ppermute(value, ("sy", "sz"), [(i, i ^ m) for i in range(count)]) for m in masks]


def per_device(
    labels, wall_dist, material_table, dist_weight, conv_weight, down_weight, mix_weight, cotangent
):
    count_y = lax.axis_size("sy")
    count_z = lax.axis_size("sz")
    mine = 64 // count_z
    width = mix_weight.shape[1]
    features, first, last = pl.pallas_call(
        feature_kernel,
        out_shape=(shape((32, 128, 80), BF16), shape((32, 80), BF16), shape((32, 80), BF16)),
        in_specs=[HBM] * 2,
        out_specs=(VMEM,) * 3,
        scratch_shapes=[
            pltpu.VMEM((16, 32, 64), jnp.int32),
            pltpu.VMEM((16, 32, 64), BF16),
            pltpu.VMEM((16, 32, 64), F32),
            pltpu.VMEM((32, 80), F32),
            pltpu.VMEM((32, 80), F32),
            pltpu.SemaphoreType.DMA((2,)),
        ],
        compiler_params=params(8),
        cost_estimate=cost(32 * 128 * 64 * 80 * 2, 2 << 20),
        name="features",
    )(*kept(jnp.transpose(labels, (0, 2, 1)), jnp.transpose(wall_dist, (0, 2, 1))))
    up_y = [(i, i + 1) for i in range(count_y - 1)]
    up_z = [(i, i + 1) for i in range(count_z - 1)]
    ylo = lax.ppermute(last, "sy", up_y)
    yhi = lax.ppermute(first, "sy", [(j, i) for i, j in up_y])
    band, pair, pair_t, table = pl.pallas_call(
        weight_kernel,
        out_shape=(
            shape((9, 256, 256), BF16),
            shape((128, 256), BF16),
            shape((256, 128), BF16),
            shape((80, 256), BF16),
        ),
        in_specs=[HBM] * 4,
        out_specs=(VMEM,) * 4,
        scratch_shapes=[
            pltpu.VMEM((16, 16, 27), BF16),
            pltpu.VMEM((8, 16, 64), BF16),
            pltpu.VMEM((4, 16), BF16),
            pltpu.VMEM((1, 16), BF16),
            pltpu.SemaphoreType.DMA((4,)),
        ],
        compiler_params=params(8),
        cost_estimate=cost(27 * 256 * 16 * 256 * 2, 3 << 20),
        name="weights",
    )(
        *kept(
            jnp.transpose(conv_weight, (1, 2, 0)),
            jnp.transpose(down_weight, (0, 2, 1)),
            material_table,
            dist_weight[None],
        )
    )
    ylo, yhi, band, pair, pair_t, table = lax.optimization_barrier(
        (ylo, yhi, band, pair, pair_t, table)
    )

    def whole(z):
        row = lax.broadcasted_iota(jnp.int32, (128, 80), 0)
        face = jnp.where(row == 64, ylo[z][None], features[z])
        return jnp.where(row == 127, yhi[z][None], face)

    zlo = lax.ppermute(whole(31), "sz", up_z)
    zhi = lax.ppermute(whole(0), "sz", [(j, i) for i, j in up_z])
    embedded, slope, hidden, edge = pl.pallas_call(
        inner_kernel,
        out_shape=(
            shape((17, 2, 128, 256), BF16),
            shape((4, 256, 512), F32),
            shape((4, 256, 512), BF16),
            shape((2, 2, 256, 32), F32),
        ),
        in_specs=[VMEM] * 5,
        out_specs=(VMEM,) * 4,
        compiler_params=params(12),
        cost_estimate=cost(3 << 30, 10 << 20),
        name="inner",
    )(features, ylo, yhi, table, band)
    faces, edge_slope, hidden, coarse = pl.pallas_call(
        outer_kernel,
        out_shape=(
            shape((2, 128, 256), BF16),
            shape((256, 128), F32),
            pltpu.HBM((4, 256, 512), BF16),
            pltpu.HBM((1024, 256), BF16),
        ),
        in_specs=[VMEM] * 7,
        out_specs=(VMEM, VMEM, HBM, HBM),
        scratch_shapes=[
            pltpu.VMEM((512, 512), F32),
            pltpu.VMEM((2, 1024, 128), F32),
            pltpu.VMEM((4, 256, 512), BF16),
            pltpu.VMEM((1024, 256), BF16),
            pltpu.SemaphoreType.DMA((3,)),
        ],
        compiler_params=params(8),
        cost_estimate=cost(1 << 30, 4 << 20),
        name="outer",
    )(zlo, zhi, table, band, pair, edge, hidden)

    sent = lax.all_to_all(
        coarse.reshape(count_z, mine * 16, 256), "sz", split_axis=0, concat_axis=0, tiled=True
    )
    block = lambda *dims: pl.BlockSpec(dims, lambda c: (c,) + (0,) * (len(dims) - 1))
    shares = count_y // 2
    mix_specs = [
        pl.BlockSpec((count_z, 16, 256), lambda c: (0, c, 0)),
        block(1, width, width),
        block(1, 256, width),
    ]
    cotangent_rows = cotangent.reshape(mine, 256, width)
    back = pl.pallas_call(
        mix_kernel,
        grid=(mine,),
        out_shape=shape((count_z, mine * 16, 256), BF16),
        in_specs=mix_specs,
        out_specs=pl.BlockSpec((count_z, 16, 256), lambda c: (0, c, 0)),
        compiler_params=params(8),
        cost_estimate=cost(mine * 2 * 2 * 256 * width * width, 2 << 20),
        name="mix",
    )(sent, mix_weight, cotangent_rows)
    coarse_grad = lax.all_to_all(back, "sz", split_axis=0, concat_axis=0, tiled=True)
    sent, back = lax.optimization_barrier((sent, back))
    mid, *mix_parts = pl.pallas_call(
        lambda *refs: mix_grad_kernel(1.0 / math.sqrt(8 * 32 * count_y), *refs),
        grid=(mine,),
        out_shape=[shape((mine, 256, width), BF16)]
        + [pltpu.HBM((mine, width // shares, width), F32)] * shares,
        in_specs=[pl.BlockSpec(memory_space=pltpu.SMEM)] + mix_specs,
        out_specs=[block(1, 256, width)] + [block(1, width // shares, width)] * shares,
        scratch_shapes=[pltpu.VMEM((width, width), F32)],
        compiler_params=params(8),
        cost_estimate=cost(mine * 2 * 2 * 256 * width * width, 3 << 20),
        name="mix_grad",
    )(lax.axis_index("sy")[None], sent, mix_weight, cotangent_rows)
    mix_sum = mix_parts[0]
    moved = []
    for k, part in enumerate(mix_parts[1:], 1):
        moved.append(lax.ppermute(part, "sy", [(i, i ^ (2 * k)) for i in range(count_y)]))
    cells = 16 * 64 * count_y * 32 * count_z
    sums = pl.pallas_call(
        lambda *refs: backward_kernel(
            1.0 / math.sqrt(cells // 8), 1.0 / math.sqrt(cells), *refs
        ),
        out_shape=shape((128, 128), F32),
        in_specs=[VMEM, HBM, HBM] + [VMEM] * 5,
        out_specs=VMEM,
        scratch_shapes=[
            pltpu.VMEM((512, 512), F32),
            pltpu.VMEM((2, 1024, 128), F32),
            pltpu.VMEM((4, 256, 512), BF16),
            pltpu.VMEM((17, 2, 128, 256), BF16),
            pltpu.VMEM((4, 256, 512), F32),
            pltpu.SemaphoreType.DMA((2,)),
        ],
        compiler_params=params(12),
        cost_estimate=cost(4 << 30, 8 << 20),
        name="backward",
    )(
        coarse_grad.reshape(1024, 256),
        *kept(embedded, slope),
        hidden,
        pair,
        pair_t,
        faces,
        edge_slope,
    )
    *moved, sums = lax.optimization_barrier((*moved, sums))
    for part in moved:
        mix_sum = mix_sum + part
    mine_last, other = jnp.split(mix_sum, 2, axis=1)
    mix_grad = mine_last + lax.ppermute(other, "sy", [(i, i ^ 1) for i in range(count_y)])

    rounds = sum_rounds(count_y, count_z)
    for masks in rounds[:-1]:
        parts = [sums] + exchanged(sums, masks, count_y * count_z)
        sums = parts[0] + parts[1] if len(parts) == 2 else (parts[0] + parts[1]) + (parts[2] + parts[3])
    down_grad, conv_grad = pl.pallas_call(
        finish_kernel,
        out_shape=(shape((8, 16, 64), F32), shape((256, 27), F32)),
        in_specs=[VMEM] * 4,
        out_specs=(VMEM,) * 2,
        compiler_params=params(8),
        cost_estimate=cost(1 << 20, 1 << 18),
        name="finish",
    )(sums, *exchanged(sums, rounds[-1], count_y * count_z))
    down_grad = jnp.transpose(down_grad, (0, 2, 1))
    conv_grad = jnp.transpose(conv_grad.reshape(16, 16, 27), (2, 0, 1))
    return (mid.reshape(cotangent.shape), mix_grad, down_grad, conv_grad)


def solution(mesh):
    in_specs = (
        P(None, "sy", "sz"),
        P(None, "sy", "sz"),
        P(),
        P(),
        P(),
        P(),
        P("sz", None, None),
        P("sz", None, "sy", None),
    )
    out_specs = (P("sz", None, "sy", None), P("sz", "sy", None), P(), P())
    return jax.shard_map(
        per_device, mesh=mesh, in_specs=in_specs, out_specs=out_specs, check_vma=False
    )
```

```python
import math

import jax
import jax.numpy as jnp
from jax import lax
from jax.experimental import pallas as pl
from jax.experimental.pallas import tpu as pltpu
from jax.sharding import PartitionSpec as P

F32 = jnp.float32
BF16 = jnp.bfloat16
VMEM = pl.BlockSpec(memory_space=pltpu.VMEM)
HBM = pl.BlockSpec(memory_space=pltpu.HBM)
RUNS = ((64, 0, 32), (0, 32, 96))


def dot(a, b, ca, cb):
    return lax.dot_general(a, b, (((ca,), (cb,)), ((), ())), preferred_element_type=F32)


def iota(shape, dim):
    return lax.broadcasted_iota(jnp.int32, shape, dim)


def fetch(sources, targets, sem):
    copies = [pltpu.make_async_copy(a, b, sem.at[k]) for k, (a, b) in enumerate(zip(sources, targets))]
    for copy in copies:
        copy.start()
    return copies


def feature_kernel(lab_hbm, wd_hbm, out_ref, first_ref, last_ref, lab_s, wd_b, wd_s, first_s, last_s, sem):
    copies = fetch((lab_hbm, wd_hbm), (lab_s, wd_b), sem)
    row = iota((128, 64), 0)
    run, r = row // 32, row % 32
    y = jnp.where(run == 0, 2 * r, jnp.where(run == 1, 2 * r + 1, jnp.where(run == 2, 2 * r - 1, 2 * r + 2)))
    pick = (y == iota((128, 64), 1)).astype(BF16)
    for copy in copies:
        copy.wait()
    wd_s[...] = wd_b[...].astype(F32)
    for z in range(out_ref.shape[0]):
        lab = lab_s[:, z, :]
        parts = [(lab == m).astype(F32).astype(BF16) for m in range(4)]
        parts.append(wd_s[:, z, :].astype(BF16))
        rows = dot(pick, jnp.concatenate(parts, axis=0), 1, 1)
        out_ref[z] = rows.astype(BF16)
        first_s[z : z + 1, :] = rows[0:1, :]
        last_s[z : z + 1, :] = rows[63:64, :]
    first_ref[...] = first_s[...].astype(BF16)
    last_ref[...] = last_s[...].astype(BF16)


def weight_kernel(
    conv_hbm, down_hbm, mat_hbm, dist_hbm, band_ref, pair_ref, pair_t_ref, table_ref,
    conv_ref, down_ref, mat_ref, dist_ref, sem,
):
    copies = fetch(
        (conv_hbm, down_hbm, mat_hbm, dist_hbm), (conv_ref, down_ref, mat_ref, dist_ref), sem
    )
    for copy in copies:
        copy.wait()
    spread = (iota((256, 16), 0) % 16 == iota((256, 16), 1)).astype(BF16)
    taps = conv_ref[...].reshape(256, 27)
    repeat = (iota((27, 432), 0) == iota((27, 432), 1) // 16).astype(BF16)
    own = iota((256, 432), 0) % 16 == iota((256, 432), 1) % 16
    apart = jnp.where(own, dot(taps, repeat, 1, 0), 0.0).astype(BF16)
    gather = (iota((256, 256), 0) % 16 == iota((256, 256), 1) // 16).astype(BF16)
    wide = dot(gather, apart, 1, 0).astype(BF16)
    offset = iota((256, 256), 1) // 16 - iota((256, 256), 0) // 16 + 1
    for t in range(9):
        total = jnp.zeros((256, 256), F32)
        for tx in range(3):
            at = (tx * 9 + t) * 16
            tile = dot(wide[:, at : at + 16], spread, 1, 1)
            total = jnp.where(offset == tx, tile, total)
        band_ref[t] = total.astype(BF16)
    for bc in range(4):
        for x2 in range(2):
            for a in range(2):
                tap = down_ref[4 * a + bc]
                none = jnp.zeros_like(tap)
                at = 64 * bc + 32 * x2 + 16 * a
                pair_t_ref[at : at + 16, :] = jnp.concatenate([none, tap] if x2 else [tap, none], axis=1)
    pair_ref[...] = pair_t_ref[...].T
    lane_e = iota((16, 256), 1) // 16
    row_e = iota((16, 256), 0)
    mat = dot(mat_ref[...], spread, 1, 1)
    dist = dot(dist_ref[...], spread, 1, 1)
    for m in range(5):
        line = jnp.broadcast_to(mat[m : m + 1, :] if m < 4 else dist, (16, 256))
        table_ref[16 * m : 16 * m + 16, :] = jnp.where(lane_e == row_e, line, 0.0).astype(BF16)


def activate(acc):
    sigma = jax.nn.sigmoid(acc)
    return (acc * sigma).astype(BF16), sigma * (1.0 + acc * (1.0 - sigma))


def cells_of(emb_ref, b, c, ty, tz, half):
    run = RUNS[b][ty]
    q = (c + tz) // 2 + 8 * half
    return emb_ref[q : q + 8, (c + tz) % 2, run : run + 32, :].reshape(256, 256)


def inner_kernel(
    feat_ref, ylo_ref, yhi_ref, table_ref, band_ref, emb_ref, slope_hbm, hidden_ref, edge_ref,
    slope_ref, sem,
):
    table = table_ref[...]
    row = iota((128, 80), 0)
    emb_ref[0, 0] = jnp.zeros((128, 256), BF16)
    emb_ref[16, 1] = jnp.zeros((128, 256), BF16)
    ylo = ylo_ref[...].astype(F32)
    yhi = yhi_ref[...].astype(F32)
    for z in range(32):
        f = feat_ref[z].astype(F32)
        f = jnp.where(row == 64, ylo[z : z + 1, :], f)
        f = jnp.where(row == 127, yhi[z : z + 1, :], f)
        emb_ref[(z + 1) // 2, (z + 1) % 2] = dot(f.astype(BF16), table, 1, 0).astype(BF16)
    copies = []
    for bc in range(4):
        b, c = bc // 2, bc % 2
        for half in range(2):
            acc = None
            for ty in range(3):
                for tz in range(3):
                    part = dot(band_ref[3 * ty + tz], cells_of(emb_ref, b, c, ty, tz, half), 1, 1)
                    acc = part if acc is None else acc + part
            if half == 0 and c == 0:
                edge_ref[0, b] = acc[:, :32]
            if half == 1 and c == 1:
                edge_ref[1, b] = acc[:, 224:]
            at = slice(256 * half, 256 * half + 256)
            hidden_ref[bc, :, at], slope_ref[bc, :, at] = activate(acc)
            part = (bc, slice(None), pl.ds(256 * half, 256))
            copies.append(pltpu.make_async_copy(slope_ref.at[part], slope_hbm.at[part], sem.at[len(copies)]))
            copies[-1].start()
    for copy in copies:
        copy.wait()


def pair_rows(hidden_ref, pair):
    return jnp.concatenate([hidden_ref[bc, 64 * pair : 64 * pair + 64, :] for bc in range(4)], axis=0)


def outer_kernel(
    zlo_ref, zhi_ref, table_ref, band_ref, pair_ref, edge_ref, inner_ref,
    emb_ref, slope_ref, hidden_hbm, coarse_hbm, turn_a, turn_b, hidden_ref, coarse_ref, sem,
):
    table = table_ref[...]
    hidden_ref[...] = inner_ref[...]
    for side, face in enumerate((zlo_ref, zhi_ref)):
        plane = dot(face[...], table, 1, 0).astype(BF16)
        emb_ref[side] = plane
        for b in range(2):
            acc = edge_ref[side, b]
            for ty in range(3):
                run = RUNS[b][ty]
                acc = acc + dot(band_ref[3 * ty + 2 * side], plane[run : run + 32], 1, 1)
            at = slice(480 * side, 480 * side + 32)
            hidden_ref[2 * b + side, :, at], slope_ref[:, 64 * side + 32 * b : 64 * side + 32 * b + 32] = activate(acc)
    copies = [pltpu.make_async_copy(hidden_ref, hidden_hbm, sem.at[0])]
    copies[0].start()
    for pair in range(4):
        turn_a[128 * pair : 128 * pair + 128, :] = dot(pair_ref[...], pair_rows(hidden_ref, pair), 1, 0)
    for half in range(2):
        for z2 in range(16):
            pieces = [
                turn_a[64 * x2 : 64 * x2 + 64, 32 * z2 : 32 * z2 + 32]
                for x2 in range(4 * half, 4 * half + 4)
            ]
            turn_b[half, pl.ds(z2, 64, stride=16), :] = jnp.concatenate(pieces, axis=1)
        at = (slice(None), pl.ds(128 * half, 128))
        coarse_ref[at] = turn_b[half].astype(BF16)
        copies.append(pltpu.make_async_copy(coarse_ref.at[at], coarse_hbm.at[at], sem.at[1 + half]))
        copies[-1].start()
    for copy in copies:
        copy.wait()


def turn_kernel(mix_ref, cot_ref, mix_t_ref, cot_t_ref):
    mix_t_ref[0] = mix_ref[0].T
    cot_t_ref[0] = cot_ref[0].T


def mixed(coarse_ref, mix_ref, cot_t_ref):
    coarse = coarse_ref[...].reshape(mix_ref.shape[1], 256)
    pre = dot(mix_ref[0], coarse, 1, 0)
    sigma = jax.nn.sigmoid(pre)
    grad = cot_t_ref[0].astype(F32) * (sigma * (1.0 + pre * (1.0 - sigma)))
    return coarse, pre * sigma, grad.astype(BF16)


def mix_kernel(coarse_ref, mix_ref, cot_t_ref, mix_t_ref, grad_ref):
    _, _, grad = mixed(coarse_ref, mix_ref, cot_t_ref)
    grad_ref[...] = dot(mix_t_ref[0], grad, 1, 0).astype(BF16).reshape(grad_ref.shape)


def mix_grad_kernel(scale, me_ref, coarse_ref, mix_ref, cot_t_ref, mid_ref, *more_refs):
    *share_refs, total_ref = more_refs
    coarse, mid, grad = mixed(coarse_ref, mix_ref, cot_t_ref)
    mid_ref[0] = mid.astype(BF16).T
    total_ref[...] = dot(grad, coarse, 1, 1) * scale
    rows = total_ref.shape[0] // (2 * len(share_refs))
    for place in range(2 * len(share_refs)):
        start = pl.multiple_of(jnp.bitwise_xor(me_ref[0], place) * rows, rows)
        at = place % 2 * rows
        share_ref = share_refs[place // 2]
        share_ref[0, at : at + rows, :] = total_ref[pl.ds(start, rows), :].astype(share_ref.dtype)


def fold(value, step):
    lanes = value.shape[-1]
    if lanes == 256:
        value = value[:, :128] + value[:, 128:]
    shift = 64
    while shift >= step:
        value = value + pltpu.roll(value, shift, 1)
        shift //= 2
    return value


def backward_kernel(
    down_scale, conv_scale, cgrad_ref, emb_hbm, slope_hbm, hidden_hbm, pair_ref, pair_t_ref, face_ref, edge_ref,
    out_ref, turn_a, turn_b, turned_pg, emb_in, slope_in, hidden_ref, sem,
):
    copies = [
        pltpu.make_async_copy(slope_hbm, slope_in, sem.at[0]),
        pltpu.make_async_copy(emb_hbm, emb_in, sem.at[1]),
        pltpu.make_async_copy(hidden_hbm, hidden_ref, sem.at[2]),
    ]
    copies[2].start()
    copies[0].start()
    for half in range(2):
        turn_b[half] = cgrad_ref[:, 128 * half : 128 * half + 128].astype(F32)
    for half in range(2):
        for quad in range(4):
            pieces = [turn_b[half, pl.ds(4 * quad + k, 64, stride=16), :] for k in range(4)]
            for k in range(4):
                x2 = 4 * half + k
                turn_a[64 * x2 : 64 * x2 + 64, 128 * quad : 128 * quad + 128] = jnp.concatenate(
                    [p[:, 32 * k : 32 * k + 32] for p in pieces], axis=1
                )
    copies[1].start()
    cg_t = turn_a[...].astype(BF16)
    pairs = [cg_t[128 * pair : 128 * pair + 128, :] for pair in range(4)]
    copies[2].wait()
    down = None
    for pair in range(4):
        part = dot(pairs[pair], pair_rows(hidden_ref, pair), 1, 1)
        down = part if down is None else down + part
    down = jnp.where(iota((64, 256), 1) // 32 % 2 == 0, down[:64], down[64:]) * down_scale
    left = down[:, :128] + pltpu.roll(down[:, :128], 96, 1)
    right = down[:, 128:] + pltpu.roll(down[:, 128:], 32, 1)
    out_ref[0:64, :] = jnp.where(iota((64, 128), 1) // 32 % 2 == 0, left, right)
    copies[0].wait()
    for pair in range(4):
        hgrad = dot(pair_t_ref[...], pairs[pair], 1, 0)
        at = slice(64 * pair, 64 * pair + 64)
        for bc in range(4):
            rows = hgrad[64 * bc : 64 * bc + 64]
            turned_pg[bc, at, :] = (rows * slope_in[bc, at, :]).astype(BF16)
            edge = slice(480 * (bc % 2), 480 * (bc % 2) + 32)
            low = 64 * (bc % 2) + 32 * (bc // 2)
            turned_pg[bc, at, edge] = (rows[:, edge] * edge_ref[at, low : low + 32]).astype(BF16)
    copies[1].wait()
    lane_x = iota((16, 256), 1) // 16
    own = iota((8, 128), 1) // 16 == iota((8, 128), 0)
    for ty in range(3):
        for tz in range(3):
            acc = None
            for bc in range(4):
                b, c = bc // 2, bc % 2
                for half in range(2):
                    rows = cells_of(emb_in, b, c, ty, tz, half)
                    run = RUNS[b][ty]
                    if c + tz == 0 and half == 0:
                        rows = jnp.concatenate([face_ref[0, run : run + 32, :], rows[32:]], axis=0)
                    if c + tz == 3 and half == 1:
                        rows = jnp.concatenate([rows[:224], face_ref[1, run : run + 32, :]], axis=0)
                    part = dot(turned_pg[bc, :, 256 * half : 256 * half + 256], rows, 1, 0)
                    acc = part if acc is None else acc + part
            for tx in range(3):
                total = jnp.zeros((16, 256), F32)
                for x in range(16):
                    if 0 <= x + tx - 1 < 16:
                        total = jnp.where(lane_x == x + tx - 1, acc[16 * x : 16 * x + 16, :], total)
                tap = 9 * tx + 3 * ty + tz
                total = fold(total, 16) * conv_scale
                for half in range(2):
                    part = jnp.where(own, total[8 * half : 8 * half + 8], 0.0)
                    line = 64 + 32 * half + tap
                    out_ref[line : line + 1, :] = jnp.sum(part, axis=0, keepdims=True)
    for half in range(2):
        out_ref[91 + 32 * half : 96 + 32 * half, :] = jnp.zeros((5, 128), F32)


def finish_kernel(a_ref, b_ref, c_ref, d_ref, down_ref, conv_ref):
    total = (a_ref[...] + b_ref[...]) + (c_ref[...] + d_ref[...])
    down = total[:64].T
    for a in range(2):
        for bc in range(4):
            at = (2 * (2 * (bc % 2) + bc // 2) + a) * 16
            down_ref[4 * a + bc] = down[at : at + 16, :]
    for half in range(2):
        conv = total[64 + 32 * half : 96 + 32 * half].T
        conv_ref[128 * half : 128 * half + 128, :] = conv[:, :27]


def kept(*values):
    return [pltpu.with_memory_space_constraint(v, pltpu.HBM) for v in values]


def params(mib):
    return pltpu.CompilerParams(vmem_limit_bytes=mib << 20)


def cost(flops, nbytes):
    return pl.CostEstimate(flops=flops, bytes_accessed=nbytes, transcendentals=0)


def shape(dims, dtype):
    return jax.ShapeDtypeStruct(dims, dtype)


def sum_rounds(count_y, count_z):
    in_z = [1 << k for k in range(count_z.bit_length() - 1)]
    in_y = [count_z << k for k in range(count_y.bit_length() - 1)]
    order = in_z[:1] + in_z[1:2] + in_y[:1] + in_z[2:] + in_y[1:]
    rounds, order = ([order[:1]] if len(order) % 2 else []), order[len(order) % 2 :]
    return rounds + [order[k : k + 2] for k in range(0, len(order), 2)]


def exchanged(value, masks, count):
    masks = list(masks) + [masks[0] ^ masks[1]] if len(masks) == 2 else masks
    return [lax.ppermute(value, ("sy", "sz"), [(i, i ^ m) for i in range(count)]) for m in masks]


def per_device(
    labels, wall_dist, material_table, dist_weight, conv_weight, down_weight, mix_weight, cotangent
):
    count_y = lax.axis_size("sy")
    count_z = lax.axis_size("sz")
    mine = 64 // count_z
    width = mix_weight.shape[1]
    features, first, last = pl.pallas_call(
        feature_kernel,
        out_shape=(shape((32, 128, 80), BF16), shape((32, 80), BF16), shape((32, 80), BF16)),
        in_specs=[HBM] * 2,
        out_specs=(VMEM,) * 3,
        scratch_shapes=[
            pltpu.VMEM((16, 32, 64), jnp.int32),
            pltpu.VMEM((16, 32, 64), BF16),
            pltpu.VMEM((16, 32, 64), F32),
            pltpu.VMEM((32, 80), F32),
            pltpu.VMEM((32, 80), F32),
            pltpu.SemaphoreType.DMA((2,)),
        ],
        compiler_params=params(8),
        cost_estimate=cost(32 * 128 * 64 * 80 * 2, 2 << 20),
        name="features",
    )(*kept(jnp.transpose(labels, (0, 2, 1)), jnp.transpose(wall_dist, (0, 2, 1))))
    up_y = [(i, i + 1) for i in range(count_y - 1)]
    up_z = [(i, i + 1) for i in range(count_z - 1)]
    ylo = lax.ppermute(last, "sy", up_y)
    yhi = lax.ppermute(first, "sy", [(j, i) for i, j in up_y])
    band, pair, pair_t, table = pl.pallas_call(
        weight_kernel,
        out_shape=(
            shape((9, 256, 256), BF16),
            shape((128, 256), BF16),
            shape((256, 128), BF16),
            shape((80, 256), BF16),
        ),
        in_specs=[HBM] * 4,
        out_specs=(VMEM,) * 4,
        scratch_shapes=[
            pltpu.VMEM((16, 16, 27), BF16),
            pltpu.VMEM((8, 16, 64), BF16),
            pltpu.VMEM((4, 16), BF16),
            pltpu.VMEM((1, 16), BF16),
            pltpu.SemaphoreType.DMA((4,)),
        ],
        compiler_params=params(8),
        cost_estimate=cost(27 * 256 * 16 * 256 * 2, 3 << 20),
        name="weights",
    )(
        *kept(
            jnp.transpose(conv_weight, (1, 2, 0)),
            jnp.transpose(down_weight, (0, 2, 1)),
            material_table,
            dist_weight[None],
        )
    )
    ylo, yhi, band, pair, pair_t, table = lax.optimization_barrier(
        (ylo, yhi, band, pair, pair_t, table)
    )

    def whole(z):
        row = lax.broadcasted_iota(jnp.int32, (128, 80), 0)
        face = jnp.where(row == 64, ylo[z][None], features[z])
        return jnp.where(row == 127, yhi[z][None], face)

    zlo = lax.ppermute(whole(31), "sz", up_z)
    zhi = lax.ppermute(whole(0), "sz", [(j, i) for i, j in up_z])
    embedded, slope, hidden, edge = pl.pallas_call(
        inner_kernel,
        out_shape=(
            shape((17, 2, 128, 256), BF16),
            pltpu.HBM((4, 256, 512), F32),
            shape((4, 256, 512), BF16),
            shape((2, 2, 256, 32), F32),
        ),
        in_specs=[VMEM] * 5,
        out_specs=(VMEM, HBM, VMEM, VMEM),
        scratch_shapes=[pltpu.VMEM((4, 256, 512), F32), pltpu.SemaphoreType.DMA((8,))],
        compiler_params=params(12),
        cost_estimate=cost(3 << 30, 10 << 20),
        name="inner",
    )(features, ylo, yhi, table, band)
    faces, edge_slope, hidden, coarse = pl.pallas_call(
        outer_kernel,
        out_shape=(
            shape((2, 128, 256), BF16),
            shape((256, 128), F32),
            pltpu.HBM((4, 256, 512), BF16),
            pltpu.HBM((1024, 256), BF16),
        ),
        in_specs=[VMEM] * 7,
        out_specs=(VMEM, VMEM, HBM, HBM),
        scratch_shapes=[
            pltpu.VMEM((512, 512), F32),
            pltpu.VMEM((2, 1024, 128), F32),
            pltpu.VMEM((4, 256, 512), BF16),
            pltpu.VMEM((1024, 256), BF16),
            pltpu.SemaphoreType.DMA((3,)),
        ],
        compiler_params=params(8),
        cost_estimate=cost(1 << 30, 4 << 20),
        name="outer",
    )(zlo, zhi, table, band, pair, edge, hidden)

    mix_weight, cotangent_rows, coarse = lax.optimization_barrier(
        (mix_weight, cotangent.reshape(mine, 256, width), coarse)
    )
    sent = lax.all_to_all(
        coarse.reshape(count_z, mine * 16, 256), "sz", split_axis=0, concat_axis=0, tiled=True
    )
    block = lambda *dims: pl.BlockSpec(dims, lambda c: (c,) + (0,) * (len(dims) - 1))
    shares = count_y // 2
    mix_specs = [
        pl.BlockSpec((count_z, 16, 256), lambda c: (0, c, 0)),
        block(1, width, width),
        block(1, width, 256),
    ]
    mix_t, cotangent_t = pl.pallas_call(
        turn_kernel,
        grid=(mine,),
        out_shape=(shape((mine, width, width), BF16), shape((mine, width, 256), BF16)),
        in_specs=[block(1, width, width), block(1, 256, width)],
        out_specs=(block(1, width, width), block(1, width, 256)),
        compiler_params=params(4),
        cost_estimate=cost(1 << 20, 2 << 20),
        name="turn",
    )(mix_weight, cotangent_rows)
    back = pl.pallas_call(
        mix_kernel,
        grid=(mine,),
        out_shape=shape((count_z, mine * 16, 256), BF16),
        in_specs=mix_specs + [block(1, width, width)],
        out_specs=pl.BlockSpec((count_z, 16, 256), lambda c: (0, c, 0)),
        compiler_params=params(8),
        cost_estimate=cost(mine * 2 * 2 * 256 * width * width, 2 << 20),
        name="mix",
    )(sent, mix_weight, cotangent_t, mix_t)
    coarse_grad = lax.all_to_all(back, "sz", split_axis=0, concat_axis=0, tiled=True)
    sent, back = lax.optimization_barrier((sent, back))
    mid, *mix_parts = pl.pallas_call(
        lambda *refs: mix_grad_kernel(1.0 / math.sqrt(8 * 32 * count_y), *refs),
        grid=(mine,),
        out_shape=[shape((mine, 256, width), BF16)]
        + [
            pltpu.HBM((mine, width // shares, width), BF16 if k else F32) for k in range(shares)
        ],
        in_specs=[pl.BlockSpec(memory_space=pltpu.SMEM)] + mix_specs,
        out_specs=[block(1, 256, width)] + [block(1, width // shares, width)] * shares,
        scratch_shapes=[pltpu.VMEM((width, width), F32)],
        compiler_params=params(8),
        cost_estimate=cost(mine * 2 * 2 * 256 * width * width, 3 << 20),
        name="mix_grad",
    )(lax.axis_index("sy")[None], sent, mix_weight, cotangent_t)
    mix_sum = mix_parts[0]
    moved = []
    for k, part in enumerate(mix_parts[1:], 1):
        moved.append(lax.ppermute(part, "sy", [(i, i ^ (2 * k)) for i in range(count_y)]))
    cells = 16 * 64 * count_y * 32 * count_z
    sums = pl.pallas_call(
        lambda *refs: backward_kernel(
            1.0 / math.sqrt(cells // 8), 1.0 / math.sqrt(cells), *refs
        ),
        out_shape=shape((128, 128), F32),
        in_specs=[VMEM, HBM, HBM, HBM] + [VMEM] * 4,
        out_specs=VMEM,
        scratch_shapes=[
            pltpu.VMEM((512, 512), F32),
            pltpu.VMEM((2, 1024, 128), F32),
            pltpu.VMEM((4, 256, 512), BF16),
            pltpu.VMEM((17, 2, 128, 256), BF16),
            pltpu.VMEM((4, 256, 512), F32),
            pltpu.VMEM((4, 256, 512), BF16),
            pltpu.SemaphoreType.DMA((3,)),
        ],
        compiler_params=params(12),
        cost_estimate=cost(4 << 30, 8 << 20),
        name="backward",
    )(
        coarse_grad.reshape(1024, 256),
        *kept(embedded, slope, hidden),
        pair,
        pair_t,
        faces,
        edge_slope,
    )
    *moved, sums = lax.optimization_barrier((*moved, sums))
    for part in moved:
        mix_sum = mix_sum + part.astype(F32)
    mine_last, other = jnp.split(mix_sum, 2, axis=1)
    other = lax.ppermute(other.astype(BF16), "sy", [(i, i ^ 1) for i in range(count_y)])
    mix_grad = mine_last + other.astype(F32)

    rounds = sum_rounds(count_y, count_z)
    for masks in rounds[:-1]:
        parts = [sums] + exchanged(sums, masks, count_y * count_z)
        sums = parts[0] + parts[1] if len(parts) == 2 else (parts[0] + parts[1]) + (parts[2] + parts[3])
    down_grad, conv_grad = pl.pallas_call(
        finish_kernel,
        out_shape=(shape((8, 16, 64), F32), shape((256, 27), F32)),
        in_specs=[VMEM] * 4,
        out_specs=(VMEM,) * 2,
        compiler_params=params(8),
        cost_estimate=cost(1 << 20, 1 << 18),
        name="finish",
    )(sums, *exchanged(sums, rounds[-1], count_y * count_z))
    down_grad = jnp.transpose(down_grad, (0, 2, 1))
    conv_grad = jnp.transpose(conv_grad.reshape(16, 16, 27), (2, 0, 1))
    return (mid.reshape(cotangent.shape), mix_grad, down_grad, conv_grad)


def solution(mesh):
    in_specs = (
        P(None, "sy", "sz"),
        P(None, "sy", "sz"),
        P(),
        P(),
        P(),
        P(),
        P("sz", None, None),
        P("sz", None, "sy", None),
    )
    out_specs = (P("sz", None, "sy", None), P("sz", "sy", None), P(), P())
    return jax.shard_map(
        per_device, mesh=mesh, in_specs=in_specs, out_specs=out_specs, check_vma=False
    )
```

```python
import math

import jax
import jax.numpy as jnp
from jax import lax
from jax.experimental import pallas as pl
from jax.experimental.pallas import tpu as pltpu
from jax.sharding import PartitionSpec as P

F32 = jnp.float32
BF16 = jnp.bfloat16
VMEM = pl.BlockSpec(memory_space=pltpu.VMEM)
HBM = pl.BlockSpec(memory_space=pltpu.HBM)
RUNS = ((64, 0, 32), (0, 32, 96))


def dot(a, b, ca, cb):
    return lax.dot_general(a, b, (((ca,), (cb,)), ((), ())), preferred_element_type=F32)


def iota(shape, dim):
    return lax.broadcasted_iota(jnp.int32, shape, dim)


def fetch(sources, targets, sem):
    copies = [pltpu.make_async_copy(a, b, sem.at[k]) for k, (a, b) in enumerate(zip(sources, targets))]
    for copy in copies:
        copy.start()
    return copies


def feature_kernel(lab_hbm, wd_hbm, out_ref, first_ref, last_ref, lab_s, wd_b, wd_s, first_s, last_s, sem):
    copies = fetch((lab_hbm, wd_hbm), (lab_s, wd_b), sem)
    row = iota((128, 64), 0)
    run, r = row // 32, row % 32
    y = jnp.where(run == 0, 2 * r, jnp.where(run == 1, 2 * r + 1, jnp.where(run == 2, 2 * r - 1, 2 * r + 2)))
    pick = (y == iota((128, 64), 1)).astype(BF16)
    for copy in copies:
        copy.wait()
    wd_s[...] = wd_b[...].astype(F32)
    for z in range(out_ref.shape[0]):
        lab = lab_s[pl.ds(z, 16, stride=32), :]
        parts = [(lab == m).astype(F32).astype(BF16) for m in range(4)]
        parts.append(wd_s[pl.ds(z, 16, stride=32), :].astype(BF16))
        rows = dot(pick, jnp.concatenate(parts, axis=0), 1, 1)
        out_ref[z] = rows.astype(BF16)
        first_s[z : z + 1, :] = rows[0:1, :]
        last_s[z : z + 1, :] = rows[63:64, :]
    first_ref[...] = first_s[...].astype(BF16)
    last_ref[...] = last_s[...].astype(BF16)


def weight_kernel(
    conv_hbm, down_hbm, mat_hbm, dist_hbm, band_ref, pair_ref, pair_t_ref, table_ref,
    conv_ref, down_ref, mat_ref, dist_ref, sem,
):
    copies = fetch(
        (conv_hbm, down_hbm, mat_hbm, dist_hbm), (conv_ref, down_ref, mat_ref, dist_ref), sem
    )
    for copy in copies:
        copy.wait()
    spread = (iota((256, 16), 0) % 16 == iota((256, 16), 1)).astype(BF16)
    taps = conv_ref[...].reshape(256, 27)
    repeat = (iota((27, 432), 0) == iota((27, 432), 1) // 16).astype(BF16)
    own = iota((256, 432), 0) % 16 == iota((256, 432), 1) % 16
    apart = jnp.where(own, dot(taps, repeat, 1, 0), 0.0).astype(BF16)
    gather = (iota((256, 256), 0) % 16 == iota((256, 256), 1) // 16).astype(BF16)
    wide = dot(gather, apart, 1, 0).astype(BF16)
    offset = iota((256, 256), 1) // 16 - iota((256, 256), 0) // 16 + 1
    for t in range(9):
        total = jnp.zeros((256, 256), F32)
        for tx in range(3):
            at = (tx * 9 + t) * 16
            tile = dot(wide[:, at : at + 16], spread, 1, 1)
            total = jnp.where(offset == tx, tile, total)
        band_ref[t] = total.astype(BF16)
    for bc in range(4):
        for x2 in range(2):
            for a in range(2):
                tap = down_ref[4 * a + bc]
                none = jnp.zeros_like(tap)
                at = 64 * bc + 32 * x2 + 16 * a
                pair_t_ref[at : at + 16, :] = jnp.concatenate([none, tap] if x2 else [tap, none], axis=1)
    pair_ref[...] = pair_t_ref[...].T
    lane_e = iota((16, 256), 1) // 16
    row_e = iota((16, 256), 0)
    mat = dot(mat_ref[...], spread, 1, 1)
    dist = dot(dist_ref[...], spread, 1, 1)
    for m in range(5):
        line = jnp.broadcast_to(mat[m : m + 1, :] if m < 4 else dist, (16, 256))
        table_ref[16 * m : 16 * m + 16, :] = jnp.where(lane_e == row_e, line, 0.0).astype(BF16)


def activate(acc):
    sigma = jax.nn.sigmoid(acc)
    return (acc * sigma).astype(BF16), sigma * (1.0 + acc * (1.0 - sigma))


def cells_of(emb_ref, b, c, ty, tz, half):
    run = RUNS[b][ty]
    q = (c + tz) // 2 + 8 * half
    return emb_ref[q : q + 8, (c + tz) % 2, run : run + 32, :].reshape(256, 256)


def inner_kernel(
    feat_ref, ylo_ref, yhi_ref, table_ref, band_ref, emb_ref, slope_hbm, hidden_ref, edge_ref,
    slope_ref, sem,
):
    table = table_ref[...]
    row = iota((128, 80), 0)
    emb_ref[0, 0] = jnp.zeros((128, 256), BF16)
    emb_ref[16, 1] = jnp.zeros((128, 256), BF16)
    ylo = ylo_ref[...].astype(F32)
    yhi = yhi_ref[...].astype(F32)
    for z in range(32):
        f = feat_ref[z].astype(F32)
        f = jnp.where(row == 64, ylo[z : z + 1, :], f)
        f = jnp.where(row == 127, yhi[z : z + 1, :], f)
        emb_ref[(z + 1) // 2, (z + 1) % 2] = dot(f.astype(BF16), table, 1, 0).astype(BF16)
    copies = []
    for bc in range(4):
        b, c = bc // 2, bc % 2
        for half in range(2):
            acc = None
            for ty in range(3):
                for tz in range(3):
                    part = dot(band_ref[3 * ty + tz], cells_of(emb_ref, b, c, ty, tz, half), 1, 1)
                    acc = part if acc is None else acc + part
            if half == 0 and c == 0:
                edge_ref[0, b] = acc[:, :32]
            if half == 1 and c == 1:
                edge_ref[1, b] = acc[:, 224:]
            at = slice(256 * half, 256 * half + 256)
            hidden_ref[bc, :, at], slope_ref[bc, :, at] = activate(acc)
            part = (bc, slice(None), pl.ds(256 * half, 256))
            copies.append(pltpu.make_async_copy(slope_ref.at[part], slope_hbm.at[part], sem.at[len(copies)]))
            copies[-1].start()
    for copy in copies:
        copy.wait()


def pair_rows(hidden_ref, pair):
    return jnp.concatenate([hidden_ref[bc, 64 * pair : 64 * pair + 64, :] for bc in range(4)], axis=0)


def outer_kernel(
    zlo_ref, zhi_ref, table_ref, band_ref, pair_ref, edge_ref, inner_ref,
    emb_ref, slope_ref, hidden_hbm, coarse_hbm, turn_a, turn_b, hidden_ref, coarse_ref, sem,
):
    table = table_ref[...]
    hidden_ref[...] = inner_ref[...]
    for side, face in enumerate((zlo_ref, zhi_ref)):
        plane = dot(face[...], table, 1, 0).astype(BF16)
        emb_ref[side] = plane
        for b in range(2):
            acc = edge_ref[side, b]
            for ty in range(3):
                run = RUNS[b][ty]
                acc = acc + dot(band_ref[3 * ty + 2 * side], plane[run : run + 32], 1, 1)
            at = slice(480 * side, 480 * side + 32)
            hidden_ref[2 * b + side, :, at], slope_ref[:, 64 * side + 32 * b : 64 * side + 32 * b + 32] = activate(acc)
    copies = [pltpu.make_async_copy(hidden_ref, hidden_hbm, sem.at[0])]
    copies[0].start()
    for pair in range(4):
        turn_a[128 * pair : 128 * pair + 128, :] = dot(pair_ref[...], pair_rows(hidden_ref, pair), 1, 0)
    for half in range(2):
        for z2 in range(16):
            pieces = [
                turn_a[64 * x2 : 64 * x2 + 64, 32 * z2 : 32 * z2 + 32]
                for x2 in range(4 * half, 4 * half + 4)
            ]
            turn_b[half, pl.ds(z2, 64, stride=16), :] = jnp.concatenate(pieces, axis=1)
        at = (slice(None), pl.ds(128 * half, 128))
        coarse_ref[at] = turn_b[half].astype(BF16)
        copies.append(pltpu.make_async_copy(coarse_ref.at[at], coarse_hbm.at[at], sem.at[1 + half]))
        copies[-1].start()
    for copy in copies:
        copy.wait()


def turn_kernel(mix_ref, cot_ref, mix_t_ref, cot_t_ref):
    mix_t_ref[0] = mix_ref[0].T
    cot_t_ref[0] = cot_ref[0].T


def mixed(coarse, mix, cot_t):
    pre = dot(mix, coarse, 1, 0)
    sigma = jax.nn.sigmoid(pre)
    grad = cot_t.astype(F32) * (sigma * (1.0 + pre * (1.0 - sigma)))
    return pre * sigma, grad.astype(BF16)


def mix_kernel(coarse_ref, mix_ref, cot_t_ref, mix_t_ref, grad_hbm, grad_ref, sem):
    copies = []
    for c in range(mix_ref.shape[0]):
        at = (slice(None), pl.ds(16 * c, 16), slice(None))
        _, grad = mixed(coarse_ref[at].reshape(-1, 256), mix_ref[c], cot_t_ref[c])
        part = dot(mix_t_ref[c], grad, 1, 0).astype(BF16)
        grad_ref[at] = part.reshape(-1, 16, 256)
        copies.append(pltpu.make_async_copy(grad_ref.at[at], grad_hbm.at[at], sem.at[c]))
        copies[-1].start()
    for copy in copies:
        copy.wait()


def mix_grad_kernel(scale, me_ref, coarse_ref, mix_ref, cot_t_ref, mid_ref, *more_refs):
    *share_refs, total_ref = more_refs
    coarse = coarse_ref[...].reshape(-1, 256)
    mid, grad = mixed(coarse, mix_ref[0], cot_t_ref[0])
    mid_ref[0] = mid.astype(BF16).T
    total_ref[...] = dot(grad, coarse, 1, 1) * scale
    rows = total_ref.shape[0] // (2 * len(share_refs))
    for place in range(2 * len(share_refs)):
        start = pl.multiple_of(jnp.bitwise_xor(me_ref[0], place) * rows, rows)
        at = place % 2 * rows
        share_ref = share_refs[place // 2]
        share_ref[0, at : at + rows, :] = total_ref[pl.ds(start, rows), :].astype(share_ref.dtype)


def fold(value, step):
    lanes = value.shape[-1]
    if lanes == 256:
        value = value[:, :128] + value[:, 128:]
    shift = 64
    while shift >= step:
        value = value + pltpu.roll(value, shift, 1)
        shift //= 2
    return value


def backward_kernel(
    down_scale, conv_scale, cgrad_ref, emb_hbm, slope_hbm, hidden_hbm, pair_ref, pair_t_ref, face_ref, edge_ref,
    out_ref, turn_a, turn_b, turned_pg, emb_in, slope_in, hidden_ref, sem,
):
    copies = [
        pltpu.make_async_copy(slope_hbm, slope_in, sem.at[0]),
        pltpu.make_async_copy(emb_hbm, emb_in, sem.at[1]),
        pltpu.make_async_copy(hidden_hbm, hidden_ref, sem.at[2]),
    ]
    copies[2].start()
    copies[0].start()
    for half in range(2):
        turn_b[half] = cgrad_ref[:, 128 * half : 128 * half + 128].astype(F32)
    for half in range(2):
        for quad in range(4):
            pieces = [turn_b[half, pl.ds(4 * quad + k, 64, stride=16), :] for k in range(4)]
            for k in range(4):
                x2 = 4 * half + k
                turn_a[64 * x2 : 64 * x2 + 64, 128 * quad : 128 * quad + 128] = jnp.concatenate(
                    [p[:, 32 * k : 32 * k + 32] for p in pieces], axis=1
                )
    copies[1].start()
    cg_t = turn_a[...].astype(BF16)
    pairs = [cg_t[128 * pair : 128 * pair + 128, :] for pair in range(4)]
    copies[2].wait()
    down = None
    for pair in range(4):
        part = dot(pairs[pair], pair_rows(hidden_ref, pair), 1, 1)
        down = part if down is None else down + part
    down = jnp.where(iota((64, 256), 1) // 32 % 2 == 0, down[:64], down[64:]) * down_scale
    left = down[:, :128] + pltpu.roll(down[:, :128], 96, 1)
    right = down[:, 128:] + pltpu.roll(down[:, 128:], 32, 1)
    out_ref[0:64, :] = jnp.where(iota((64, 128), 1) // 32 % 2 == 0, left, right)
    copies[0].wait()
    for pair in range(4):
        hgrad = dot(pair_t_ref[...], pairs[pair], 1, 0)
        at = slice(64 * pair, 64 * pair + 64)
        for bc in range(4):
            rows = hgrad[64 * bc : 64 * bc + 64]
            turned_pg[bc, at, :] = (rows * slope_in[bc, at, :]).astype(BF16)
            edge = slice(480 * (bc % 2), 480 * (bc % 2) + 32)
            low = 64 * (bc % 2) + 32 * (bc // 2)
            turned_pg[bc, at, edge] = (rows[:, edge] * edge_ref[at, low : low + 32]).astype(BF16)
    copies[1].wait()
    lane_x = iota((16, 128), 1) // 16
    own = iota((8, 128), 1) // 16 == iota((8, 128), 0)
    for ty in range(3):
        for tz in range(3):
            acc = None
            for bc in range(4):
                b, c = bc // 2, bc % 2
                for half in range(2):
                    rows = cells_of(emb_in, b, c, ty, tz, half)
                    run = RUNS[b][ty]
                    if c + tz == 0 and half == 0:
                        rows = jnp.concatenate([face_ref[0, run : run + 32, :], rows[32:]], axis=0)
                    if c + tz == 3 and half == 1:
                        rows = jnp.concatenate([rows[:224], face_ref[1, run : run + 32, :]], axis=0)
                    part = dot(turned_pg[bc, :, 256 * half : 256 * half + 256], rows, 1, 0)
                    acc = part if acc is None else acc + part
            for tx in range(3):
                total = None
                for side in range(2):
                    half = jnp.zeros((16, 128), F32)
                    for x in range(16):
                        lane = x + tx - 1 - 8 * side
                        if 0 <= lane < 8:
                            part = acc[16 * x : 16 * x + 16, 128 * side : 128 * side + 128]
                            half = jnp.where(lane_x == lane, part, half)
                    total = half if total is None else total + half
                tap = 9 * tx + 3 * ty + tz
                total = fold(total, 16) * conv_scale
                for half in range(2):
                    part = jnp.where(own, total[8 * half : 8 * half + 8], 0.0)
                    line = 64 + 32 * half + tap
                    out_ref[line : line + 1, :] = jnp.sum(part, axis=0, keepdims=True)
    for half in range(2):
        out_ref[91 + 32 * half : 96 + 32 * half, :] = jnp.zeros((5, 128), F32)


def finish_kernel(a_ref, b_ref, c_ref, d_ref, down_ref, conv_ref):
    total = (a_ref[...] + b_ref[...]) + (c_ref[...] + d_ref[...])
    down = total[:64].T
    for a in range(2):
        for bc in range(4):
            at = (2 * (2 * (bc % 2) + bc // 2) + a) * 16
            down_ref[4 * a + bc] = down[at : at + 16, :]
    for half in range(2):
        conv = total[64 + 32 * half : 96 + 32 * half].T
        conv_ref[128 * half : 128 * half + 128, :] = conv[:, :27]


def kept(*values):
    return [pltpu.with_memory_space_constraint(v, pltpu.HBM) for v in values]


def params(mib):
    return pltpu.CompilerParams(vmem_limit_bytes=mib << 20)


def cost(flops, nbytes):
    return pl.CostEstimate(flops=flops, bytes_accessed=nbytes, transcendentals=0)


def shape(dims, dtype):
    return jax.ShapeDtypeStruct(dims, dtype)


def sum_rounds(count_y, count_z):
    in_z = [1 << k for k in range(count_z.bit_length() - 1)]
    in_y = [count_z << k for k in range(count_y.bit_length() - 1)]
    order = in_z[:1] + in_z[1:2] + in_y[:1] + in_z[2:] + in_y[1:]
    rounds, order = ([order[:1]] if len(order) % 2 else []), order[len(order) % 2 :]
    return rounds + [order[k : k + 2] for k in range(0, len(order), 2)]


def exchanged(value, masks, count):
    masks = list(masks) + [masks[0] ^ masks[1]] if len(masks) == 2 else masks
    return [lax.ppermute(value, ("sy", "sz"), [(i, i ^ m) for i in range(count)]) for m in masks]


def per_device(
    labels, wall_dist, material_table, dist_weight, conv_weight, down_weight, mix_weight, cotangent
):
    count_y = lax.axis_size("sy")
    count_z = lax.axis_size("sz")
    mine = 64 // count_z
    width = mix_weight.shape[1]
    features, first, last = pl.pallas_call(
        feature_kernel,
        out_shape=(shape((32, 128, 80), BF16), shape((32, 80), BF16), shape((32, 80), BF16)),
        in_specs=[HBM] * 2,
        out_specs=(VMEM,) * 3,
        scratch_shapes=[
            pltpu.VMEM((512, 64), jnp.int32),
            pltpu.VMEM((512, 64), BF16),
            pltpu.VMEM((512, 64), F32),
            pltpu.VMEM((32, 80), F32),
            pltpu.VMEM((32, 80), F32),
            pltpu.SemaphoreType.DMA((2,)),
        ],
        compiler_params=params(8),
        cost_estimate=cost(32 * 128 * 64 * 80 * 2, 2 << 20),
        name="features",
    )(
        *kept(
            jnp.transpose(labels, (0, 2, 1)).reshape(512, 64),
            jnp.transpose(wall_dist, (0, 2, 1)).reshape(512, 64),
        )
    )
    up_y = [(i, i + 1) for i in range(count_y - 1)]
    up_z = [(i, i + 1) for i in range(count_z - 1)]
    ylo = lax.ppermute(last, "sy", up_y)
    yhi = lax.ppermute(first, "sy", [(j, i) for i, j in up_y])
    band, pair, pair_t, table = pl.pallas_call(
        weight_kernel,
        out_shape=(
            shape((9, 256, 256), BF16),
            shape((128, 256), BF16),
            shape((256, 128), BF16),
            shape((80, 256), BF16),
        ),
        in_specs=[HBM] * 4,
        out_specs=(VMEM,) * 4,
        scratch_shapes=[
            pltpu.VMEM((16, 16, 27), BF16),
            pltpu.VMEM((8, 16, 64), BF16),
            pltpu.VMEM((4, 16), BF16),
            pltpu.VMEM((1, 16), BF16),
            pltpu.SemaphoreType.DMA((4,)),
        ],
        compiler_params=params(8),
        cost_estimate=cost(27 * 256 * 16 * 256 * 2, 3 << 20),
        name="weights",
    )(
        *kept(
            jnp.transpose(conv_weight, (1, 2, 0)),
            jnp.transpose(down_weight, (0, 2, 1)),
            material_table,
            dist_weight[None],
        )
    )
    ylo, yhi, band, pair, pair_t, table = lax.optimization_barrier(
        (ylo, yhi, band, pair, pair_t, table)
    )

    def whole(z):
        row = lax.broadcasted_iota(jnp.int32, (128, 80), 0)
        face = jnp.where(row == 64, ylo[z][None], features[z])
        return jnp.where(row == 127, yhi[z][None], face)

    zlo = lax.ppermute(whole(31), "sz", up_z)
    zhi = lax.ppermute(whole(0), "sz", [(j, i) for i, j in up_z])
    embedded, slope, hidden, edge = pl.pallas_call(
        inner_kernel,
        out_shape=(
            shape((17, 2, 128, 256), BF16),
            pltpu.HBM((4, 256, 512), F32),
            shape((4, 256, 512), BF16),
            shape((2, 2, 256, 32), F32),
        ),
        in_specs=[VMEM] * 5,
        out_specs=(VMEM, HBM, VMEM, VMEM),
        scratch_shapes=[pltpu.VMEM((4, 256, 512), F32), pltpu.SemaphoreType.DMA((8,))],
        compiler_params=params(12),
        cost_estimate=cost(3 << 30, 10 << 20),
        name="inner",
    )(features, ylo, yhi, table, band)
    faces, edge_slope, hidden, coarse = pl.pallas_call(
        outer_kernel,
        out_shape=(
            shape((2, 128, 256), BF16),
            shape((256, 128), F32),
            pltpu.HBM((4, 256, 512), BF16),
            pltpu.HBM((1024, 256), BF16),
        ),
        in_specs=[VMEM] * 7,
        out_specs=(VMEM, VMEM, HBM, HBM),
        scratch_shapes=[
            pltpu.VMEM((512, 512), F32),
            pltpu.VMEM((2, 1024, 128), F32),
            pltpu.VMEM((4, 256, 512), BF16),
            pltpu.VMEM((1024, 256), BF16),
            pltpu.SemaphoreType.DMA((3,)),
        ],
        compiler_params=params(8),
        cost_estimate=cost(1 << 30, 4 << 20),
        name="outer",
    )(zlo, zhi, table, band, pair, edge, hidden)

    mix_weight, cotangent_rows, coarse = lax.optimization_barrier(
        (mix_weight, cotangent.reshape(mine, 256, width), coarse)
    )
    sent = lax.all_to_all(
        coarse.reshape(count_z, mine * 16, 256), "sz", split_axis=0, concat_axis=0, tiled=True
    )
    block = lambda *dims: pl.BlockSpec(dims, lambda c: (c,) + (0,) * (len(dims) - 1))
    shares = count_y // 2
    mix_specs = [
        pl.BlockSpec((count_z, 16, 256), lambda c: (0, c, 0)),
        block(1, width, width),
        block(1, width, 256),
    ]
    mix_t, cotangent_t = pl.pallas_call(
        turn_kernel,
        grid=(mine,),
        out_shape=(shape((mine, width, width), BF16), shape((mine, width, 256), BF16)),
        in_specs=[block(1, width, width), block(1, 256, width)],
        out_specs=(block(1, width, width), block(1, width, 256)),
        compiler_params=params(4),
        cost_estimate=cost(1 << 20, 2 << 20),
        name="turn",
    )(mix_weight, cotangent_rows)
    back = pl.pallas_call(
        mix_kernel,
        out_shape=pltpu.HBM((count_z, mine * 16, 256), BF16),
        in_specs=[VMEM] * 4,
        out_specs=HBM,
        scratch_shapes=[
            pltpu.VMEM((count_z, mine * 16, 256), BF16),
            pltpu.SemaphoreType.DMA((mine,)),
        ],
        compiler_params=params(8),
        cost_estimate=cost(mine * 2 * 2 * 256 * width * width, 2 << 20),
        name="mix",
    )(sent, mix_weight, cotangent_t, mix_t)
    coarse_grad = lax.all_to_all(back, "sz", split_axis=0, concat_axis=0, tiled=True)
    sent, back = lax.optimization_barrier((sent, back))
    mid, *mix_parts = pl.pallas_call(
        lambda *refs: mix_grad_kernel(1.0 / math.sqrt(8 * 32 * count_y), *refs),
        grid=(mine,),
        out_shape=[shape((mine, 256, width), BF16)]
        + [
            pltpu.HBM((mine, width // shares, width), BF16 if k else F32) for k in range(shares)
        ],
        in_specs=[pl.BlockSpec(memory_space=pltpu.SMEM)] + mix_specs,
        out_specs=[block(1, 256, width)] + [block(1, width // shares, width)] * shares,
        scratch_shapes=[pltpu.VMEM((width, width), F32)],
        compiler_params=params(8),
        cost_estimate=cost(mine * 2 * 2 * 256 * width * width, 3 << 20),
        name="mix_grad",
    )(lax.axis_index("sy")[None], sent, mix_weight, cotangent_t)
    mix_sum = mix_parts[0]
    moved = []
    for k, part in enumerate(mix_parts[1:], 1):
        moved.append(lax.ppermute(part, "sy", [(i, i ^ (2 * k)) for i in range(count_y)]))
    cells = 16 * 64 * count_y * 32 * count_z
    sums = pl.pallas_call(
        lambda *refs: backward_kernel(
            1.0 / math.sqrt(cells // 8), 1.0 / math.sqrt(cells), *refs
        ),
        out_shape=shape((128, 128), F32),
        in_specs=[VMEM, HBM, HBM, HBM] + [VMEM] * 4,
        out_specs=VMEM,
        scratch_shapes=[
            pltpu.VMEM((512, 512), F32),
            pltpu.VMEM((2, 1024, 128), F32),
            pltpu.VMEM((4, 256, 512), BF16),
            pltpu.VMEM((17, 2, 128, 256), BF16),
            pltpu.VMEM((4, 256, 512), F32),
            pltpu.VMEM((4, 256, 512), BF16),
            pltpu.SemaphoreType.DMA((3,)),
        ],
        compiler_params=params(12),
        cost_estimate=cost(4 << 30, 8 << 20),
        name="backward",
    )(
        coarse_grad.reshape(1024, 256),
        *kept(embedded, slope, hidden),
        pair,
        pair_t,
        faces,
        edge_slope,
    )
    *moved, sums = lax.optimization_barrier((*moved, sums))
    for part in moved:
        mix_sum = mix_sum + part.astype(F32)
    mine_last, other = jnp.split(mix_sum, 2, axis=1)
    other = lax.ppermute(other.astype(BF16), "sy", [(i, i ^ 1) for i in range(count_y)])
    mix_grad = mine_last + other.astype(F32)

    rounds = sum_rounds(count_y, count_z)
    for masks in rounds[:-1]:
        parts = [sums] + exchanged(sums, masks, count_y * count_z)
        sums = parts[0] + parts[1] if len(parts) == 2 else (parts[0] + parts[1]) + (parts[2] + parts[3])
    down_grad, conv_grad = pl.pallas_call(
        finish_kernel,
        out_shape=(shape((8, 16, 64), F32), shape((256, 27), F32)),
        in_specs=[VMEM] * 4,
        out_specs=(VMEM,) * 2,
        compiler_params=params(8),
        cost_estimate=cost(1 << 20, 1 << 18),
        name="finish",
    )(sums, *exchanged(sums, rounds[-1], count_y * count_z))
    down_grad = jnp.transpose(down_grad, (0, 2, 1))
    conv_grad = jnp.transpose(conv_grad.reshape(16, 16, 27), (2, 0, 1))
    return (mid.reshape(cotangent.shape), mix_grad, down_grad, conv_grad)


def solution(mesh):
    in_specs = (
        P(None, "sy", "sz"),
        P(None, "sy", "sz"),
        P(),
        P(),
        P(),
        P(),
        P("sz", None, None),
        P("sz", None, "sy", None),
    )
    out_specs = (P("sz", None, "sy", None), P("sz", "sy", None), P(), P())
    return jax.shard_map(
        per_device, mesh=mesh, in_specs=in_specs, out_specs=out_specs, check_vma=False
    )
```

```python
import math

import jax
import jax.numpy as jnp
from jax import lax
from jax.experimental import pallas as pl
from jax.experimental.pallas import tpu as pltpu
from jax.sharding import PartitionSpec as P

F32 = jnp.float32
BF16 = jnp.bfloat16
VMEM = pl.BlockSpec(memory_space=pltpu.VMEM)
HBM = pl.BlockSpec(memory_space=pltpu.HBM)
RUNS = ((64, 0, 32), (0, 32, 96))


def dot(a, b, ca, cb):
    return lax.dot_general(a, b, (((ca,), (cb,)), ((), ())), preferred_element_type=F32)


def iota(shape, dim):
    return lax.broadcasted_iota(jnp.int32, shape, dim)


def fetch(sources, targets, sem):
    copies = [pltpu.make_async_copy(a, b, sem.at[k]) for k, (a, b) in enumerate(zip(sources, targets))]
    for copy in copies:
        copy.start()
    return copies


def feature_kernel(
    lab_hbm, wd_hbm, conv_hbm, down_hbm, mat_hbm, dist_hbm,
    out_ref, first_ref, last_ref, conv_ref, down_ref, mat_ref, dist_ref,
    lab_s, wd_b, wd_s, first_s, last_s, sem,
):
    copies = fetch(
        (lab_hbm, wd_hbm, conv_hbm, down_hbm, mat_hbm, dist_hbm),
        (lab_s, wd_b, conv_ref, down_ref, mat_ref, dist_ref),
        sem,
    )
    row = iota((128, 64), 0)
    run, r = row // 32, row % 32
    y = jnp.where(run == 0, 2 * r, jnp.where(run == 1, 2 * r + 1, jnp.where(run == 2, 2 * r - 1, 2 * r + 2)))
    pick = (y == iota((128, 64), 1)).astype(BF16)
    copies[0].wait()
    copies[1].wait()
    wd_s[...] = wd_b[...].astype(F32)
    for z in range(out_ref.shape[0]):
        lab = lab_s[pl.ds(z, 16, stride=32), :]
        parts = [(lab == m).astype(F32).astype(BF16) for m in range(4)]
        parts.append(wd_s[pl.ds(z, 16, stride=32), :].astype(BF16))
        rows = dot(pick, jnp.concatenate(parts, axis=0), 1, 1)
        out_ref[z] = rows.astype(BF16)
        first_s[z : z + 1, :] = rows[0:1, :]
        last_s[z : z + 1, :] = rows[63:64, :]
    first_ref[...] = first_s[...].astype(BF16)
    last_ref[...] = last_s[...].astype(BF16)
    for copy in copies[2:]:
        copy.wait()


def weight_kernel(
    conv_ref, down_ref, mat_ref, dist_ref, band_ref, pair_ref, pair_t_ref, table_ref
):
    spread = (iota((256, 16), 0) % 16 == iota((256, 16), 1)).astype(BF16)
    taps = conv_ref[...].reshape(256, 27)
    repeat = (iota((27, 432), 0) == iota((27, 432), 1) // 16).astype(BF16)
    own = iota((256, 432), 0) % 16 == iota((256, 432), 1) % 16
    apart = jnp.where(own, dot(taps, repeat, 1, 0), 0.0).astype(BF16)
    gather = (iota((256, 256), 0) % 16 == iota((256, 256), 1) // 16).astype(BF16)
    wide = dot(gather, apart, 1, 0).astype(BF16)
    offset = iota((256, 256), 1) // 16 - iota((256, 256), 0) // 16 + 1
    for t in range(9):
        total = jnp.zeros((256, 256), F32)
        for tx in range(3):
            at = (tx * 9 + t) * 16
            tile = dot(wide[:, at : at + 16], spread, 1, 1)
            total = jnp.where(offset == tx, tile, total)
        band_ref[t] = total.astype(BF16)
    for bc in range(4):
        for x2 in range(2):
            for a in range(2):
                tap = down_ref[4 * a + bc]
                none = jnp.zeros_like(tap)
                at = 64 * bc + 32 * x2 + 16 * a
                pair_t_ref[at : at + 16, :] = jnp.concatenate([none, tap] if x2 else [tap, none], axis=1)
    pair_ref[...] = pair_t_ref[...].T
    lane_e = iota((16, 256), 1) // 16
    row_e = iota((16, 256), 0)
    mat = dot(mat_ref[...], spread, 1, 1)
    dist = dot(dist_ref[...], spread, 1, 1)
    for m in range(5):
        line = jnp.broadcast_to(mat[m : m + 1, :] if m < 4 else dist, (16, 256))
        table_ref[16 * m : 16 * m + 16, :] = jnp.where(lane_e == row_e, line, 0.0).astype(BF16)


def activate(acc):
    sigma = jax.nn.sigmoid(acc)
    return (acc * sigma).astype(BF16), sigma * (1.0 + acc * (1.0 - sigma))


def cells_of(emb_ref, b, c, ty, tz, half):
    run = RUNS[b][ty]
    q = (c + tz) // 2 + 8 * half
    return emb_ref[q : q + 8, (c + tz) % 2, run : run + 32, :].reshape(256, 256)


def inner_kernel(
    feat_ref, ylo_ref, yhi_ref, table_ref, band_ref, emb_ref, slope_hbm, hidden_ref, edge_ref,
    slope_ref, sem,
):
    table = table_ref[...]
    row = iota((128, 80), 0)
    emb_ref[0, 0] = jnp.zeros((128, 256), BF16)
    emb_ref[16, 1] = jnp.zeros((128, 256), BF16)
    ylo = ylo_ref[...].astype(F32)
    yhi = yhi_ref[...].astype(F32)
    for z in range(32):
        f = feat_ref[z].astype(F32)
        f = jnp.where(row == 64, ylo[z : z + 1, :], f)
        f = jnp.where(row == 127, yhi[z : z + 1, :], f)
        emb_ref[(z + 1) // 2, (z + 1) % 2] = dot(f.astype(BF16), table, 1, 0).astype(BF16)
    copies = []
    for bc in range(4):
        b, c = bc // 2, bc % 2
        for half in range(2):
            acc = None
            for ty in range(3):
                for tz in range(3):
                    part = dot(band_ref[3 * ty + tz], cells_of(emb_ref, b, c, ty, tz, half), 1, 1)
                    acc = part if acc is None else acc + part
            if half == 0 and c == 0:
                edge_ref[0, b] = acc[:, :32]
            if half == 1 and c == 1:
                edge_ref[1, b] = acc[:, 224:]
            at = slice(256 * half, 256 * half + 256)
            hidden_ref[bc, :, at], slope_ref[bc, :, at] = activate(acc)
            part = (bc, slice(None), pl.ds(256 * half, 256))
            copies.append(pltpu.make_async_copy(slope_ref.at[part], slope_hbm.at[part], sem.at[len(copies)]))
            copies[-1].start()
    for copy in copies:
        copy.wait()


def pair_rows(hidden_ref, pair):
    return jnp.concatenate([hidden_ref[bc, 64 * pair : 64 * pair + 64, :] for bc in range(4)], axis=0)


def outer_kernel(
    zlo_ref, zhi_ref, table_ref, band_ref, pair_ref, edge_ref, inner_ref,
    emb_ref, slope_ref, hidden_hbm, coarse_hbm, turn_a, turn_b, hidden_ref, coarse_ref, sem,
):
    table = table_ref[...]
    hidden_ref[...] = inner_ref[...]
    for side, face in enumerate((zlo_ref, zhi_ref)):
        f = face[...].astype(F32)
        runs = [f[:64], f[64:65], f[32:63], f[1:32], f[65:66]]
        plane = dot(jnp.concatenate(runs, axis=0).astype(BF16), table, 1, 0).astype(BF16)
        emb_ref[side] = plane
        for b in range(2):
            acc = edge_ref[side, b]
            for ty in range(3):
                run = RUNS[b][ty]
                acc = acc + dot(band_ref[3 * ty + 2 * side], plane[run : run + 32], 1, 1)
            at = slice(480 * side, 480 * side + 32)
            hidden_ref[2 * b + side, :, at], slope_ref[:, 64 * side + 32 * b : 64 * side + 32 * b + 32] = activate(acc)
    copies = [pltpu.make_async_copy(hidden_ref, hidden_hbm, sem.at[0])]
    copies[0].start()
    for pair in range(4):
        turn_a[128 * pair : 128 * pair + 128, :] = dot(pair_ref[...], pair_rows(hidden_ref, pair), 1, 0)
    for half in range(2):
        for z2 in range(16):
            pieces = [
                turn_a[64 * x2 : 64 * x2 + 64, 32 * z2 : 32 * z2 + 32]
                for x2 in range(4 * half, 4 * half + 4)
            ]
            turn_b[half, pl.ds(z2, 64, stride=16), :] = jnp.concatenate(pieces, axis=1)
        at = (slice(None), pl.ds(128 * half, 128))
        coarse_ref[at] = turn_b[half].astype(BF16)
        copies.append(pltpu.make_async_copy(coarse_ref.at[at], coarse_hbm.at[at], sem.at[1 + half]))
        copies[-1].start()
    for copy in copies:
        copy.wait()


def turn_kernel(mix_ref, cot_ref, mix_t_ref, cot_t_ref):
    mix_t_ref[0] = mix_ref[0].T
    cot_t_ref[0] = cot_ref[0].T


def mixed(coarse, mix, cot_t):
    pre = dot(mix, coarse, 1, 0)
    sigma = jax.nn.sigmoid(pre)
    grad = cot_t.astype(F32) * (sigma * (1.0 + pre * (1.0 - sigma)))
    return pre * sigma, grad.astype(BF16)


def mix_kernel(coarse_ref, mix_ref, cot_t_ref, mix_t_ref, grad_hbm, grad_ref, sem):
    copies = []
    for c in range(mix_ref.shape[0]):
        at = (slice(None), pl.ds(16 * c, 16), slice(None))
        _, grad = mixed(coarse_ref[at].reshape(-1, 256), mix_ref[c], cot_t_ref[c])
        part = dot(mix_t_ref[c], grad, 1, 0).astype(BF16)
        grad_ref[at] = part.reshape(-1, 16, 256)
        copies.append(pltpu.make_async_copy(grad_ref.at[at], grad_hbm.at[at], sem.at[c]))
        copies[-1].start()
    for copy in copies:
        copy.wait()


def mix_grad_kernel(scale, me_ref, coarse_ref, mix_ref, cot_t_ref, mid_ref, *more_refs):
    *share_refs, total_ref = more_refs
    coarse = coarse_ref[...].reshape(-1, 256)
    mid, grad = mixed(coarse, mix_ref[0], cot_t_ref[0])
    mid_ref[0] = mid.astype(BF16).T
    total_ref[...] = dot(grad, coarse, 1, 1) * scale
    rows = total_ref.shape[0] // (2 * len(share_refs))
    for place in range(2 * len(share_refs)):
        start = pl.multiple_of(jnp.bitwise_xor(me_ref[0], place) * rows, rows)
        at = place % 2 * rows
        share_ref = share_refs[place // 2]
        share_ref[0, at : at + rows, :] = total_ref[pl.ds(start, rows), :].astype(share_ref.dtype)


def fold(value, step):
    lanes = value.shape[-1]
    if lanes == 256:
        value = value[:, :128] + value[:, 128:]
    shift = 64
    while shift >= step:
        value = value + pltpu.roll(value, shift, 1)
        shift //= 2
    return value


def backward_kernel(
    down_scale, conv_scale, cgrad_ref, emb_hbm, slope_hbm, hidden_hbm, pair_ref, pair_t_ref, face_ref, edge_ref,
    out_ref, turn_a, turn_b, turned_pg, emb_in, slope_in, hidden_ref, sem,
):
    copies = [
        pltpu.make_async_copy(slope_hbm, slope_in, sem.at[0]),
        pltpu.make_async_copy(emb_hbm, emb_in, sem.at[1]),
        pltpu.make_async_copy(hidden_hbm, hidden_ref, sem.at[2]),
    ]
    copies[2].start()
    copies[0].start()
    for half in range(2):
        turn_b[half] = cgrad_ref[:, 128 * half : 128 * half + 128].astype(F32)
    for half in range(2):
        for quad in range(4):
            pieces = [turn_b[half, pl.ds(4 * quad + k, 64, stride=16), :] for k in range(4)]
            for k in range(4):
                x2 = 4 * half + k
                turn_a[64 * x2 : 64 * x2 + 64, 128 * quad : 128 * quad + 128] = jnp.concatenate(
                    [p[:, 32 * k : 32 * k + 32] for p in pieces], axis=1
                )
    copies[1].start()
    cg_t = turn_a[...].astype(BF16)
    pairs = [cg_t[128 * pair : 128 * pair + 128, :] for pair in range(4)]
    copies[2].wait()
    down = None
    for pair in range(4):
        part = dot(pairs[pair], pair_rows(hidden_ref, pair), 1, 1)
        down = part if down is None else down + part
    down = jnp.where(iota((64, 256), 1) // 32 % 2 == 0, down[:64], down[64:]) * down_scale
    left = down[:, :128] + pltpu.roll(down[:, :128], 96, 1)
    right = down[:, 128:] + pltpu.roll(down[:, 128:], 32, 1)
    out_ref[0:64, :] = jnp.where(iota((64, 128), 1) // 32 % 2 == 0, left, right)
    copies[0].wait()
    for pair in range(4):
        hgrad = dot(pair_t_ref[...], pairs[pair], 1, 0)
        at = slice(64 * pair, 64 * pair + 64)
        for bc in range(4):
            rows = hgrad[64 * bc : 64 * bc + 64]
            turned_pg[bc, at, :] = (rows * slope_in[bc, at, :]).astype(BF16)
            edge = slice(480 * (bc % 2), 480 * (bc % 2) + 32)
            low = 64 * (bc % 2) + 32 * (bc // 2)
            turned_pg[bc, at, edge] = (rows[:, edge] * edge_ref[at, low : low + 32]).astype(BF16)
    copies[1].wait()
    lane_x = iota((16, 128), 1) // 16
    own = iota((8, 128), 1) // 16 == iota((8, 128), 0)
    for ty in range(3):
        for tz in range(3):
            acc = None
            for bc in range(4):
                b, c = bc // 2, bc % 2
                for half in range(2):
                    rows = cells_of(emb_in, b, c, ty, tz, half)
                    run = RUNS[b][ty]
                    if c + tz == 0 and half == 0:
                        rows = jnp.concatenate([face_ref[0, run : run + 32, :], rows[32:]], axis=0)
                    if c + tz == 3 and half == 1:
                        rows = jnp.concatenate([rows[:224], face_ref[1, run : run + 32, :]], axis=0)
                    part = dot(turned_pg[bc, :, 256 * half : 256 * half + 256], rows, 1, 0)
                    acc = part if acc is None else acc + part
            for tx in range(3):
                total = None
                for side in range(2):
                    half = jnp.zeros((16, 128), F32)
                    for x in range(16):
                        lane = x + tx - 1 - 8 * side
                        if 0 <= lane < 8:
                            part = acc[16 * x : 16 * x + 16, 128 * side : 128 * side + 128]
                            half = jnp.where(lane_x == lane, part, half)
                    total = half if total is None else total + half
                tap = 9 * tx + 3 * ty + tz
                total = fold(total, 16) * conv_scale
                for half in range(2):
                    part = jnp.where(own, total[8 * half : 8 * half + 8], 0.0)
                    line = 64 + 32 * half + tap
                    out_ref[line : line + 1, :] = jnp.sum(part, axis=0, keepdims=True)
    for half in range(2):
        out_ref[91 + 32 * half : 96 + 32 * half, :] = jnp.zeros((5, 128), F32)


def finish_kernel(a_ref, b_ref, c_ref, d_ref, down_ref, conv_ref):
    total = (a_ref[...] + b_ref[...]) + (c_ref[...] + d_ref[...])
    down = total[:64].T
    for a in range(2):
        for bc in range(4):
            at = (2 * (2 * (bc % 2) + bc // 2) + a) * 16
            down_ref[4 * a + bc] = down[at : at + 16, :]
    for half in range(2):
        conv = total[64 + 32 * half : 96 + 32 * half].T
        conv_ref[128 * half : 128 * half + 128, :] = conv[:, :27]


def kept(*values):
    return [pltpu.with_memory_space_constraint(v, pltpu.HBM) for v in values]


def params(mib):
    return pltpu.CompilerParams(vmem_limit_bytes=mib << 20)


def cost(flops, nbytes):
    return pl.CostEstimate(flops=flops, bytes_accessed=nbytes, transcendentals=0)


def shape(dims, dtype):
    return jax.ShapeDtypeStruct(dims, dtype)


def sum_rounds(count_y, count_z):
    in_z = [1 << k for k in range(count_z.bit_length() - 1)]
    in_y = [count_z << k for k in range(count_y.bit_length() - 1)]
    order = in_z[:1] + in_z[1:2] + in_y[:1] + in_z[2:] + in_y[1:]
    rounds, order = ([order[:1]] if len(order) % 2 else []), order[len(order) % 2 :]
    return rounds + [order[k : k + 2] for k in range(0, len(order), 2)]


def exchanged(value, masks, count):
    masks = list(masks) + [masks[0] ^ masks[1]] if len(masks) == 2 else masks
    return [lax.ppermute(value, ("sy", "sz"), [(i, i ^ m) for i in range(count)]) for m in masks]


def per_device(
    labels, wall_dist, material_table, dist_weight, conv_weight, down_weight, mix_weight, cotangent
):
    count_y = lax.axis_size("sy")
    count_z = lax.axis_size("sz")
    mine = 64 // count_z
    width = mix_weight.shape[1]
    features, first, last, *weights = pl.pallas_call(
        feature_kernel,
        out_shape=(
            shape((32, 128, 80), BF16),
            shape((32, 80), BF16),
            shape((32, 80), BF16),
            shape((16, 16, 27), BF16),
            shape((8, 16, 64), BF16),
            shape((4, 16), BF16),
            shape((1, 16), BF16),
        ),
        in_specs=[HBM] * 6,
        out_specs=(VMEM,) * 7,
        scratch_shapes=[
            pltpu.VMEM((512, 64), jnp.int32),
            pltpu.VMEM((512, 64), BF16),
            pltpu.VMEM((512, 64), F32),
            pltpu.VMEM((32, 80), F32),
            pltpu.VMEM((32, 80), F32),
            pltpu.SemaphoreType.DMA((6,)),
        ],
        compiler_params=params(8),
        cost_estimate=cost(32 * 128 * 64 * 80 * 2, 2 << 20),
        name="features",
    )(
        *kept(
            jnp.transpose(labels, (0, 2, 1)).reshape(512, 64),
            jnp.transpose(wall_dist, (0, 2, 1)).reshape(512, 64),
            jnp.transpose(conv_weight, (1, 2, 0)),
            jnp.transpose(down_weight, (0, 2, 1)),
            material_table,
            dist_weight[None],
        )
    )
    up_y = [(i, i + 1) for i in range(count_y - 1)]
    up_z = [(i, i + 1) for i in range(count_z - 1)]
    ylo = lax.ppermute(last, "sy", up_y)
    yhi = lax.ppermute(first, "sy", [(j, i) for i, j in up_y])
    band, pair, pair_t, table = pl.pallas_call(
        weight_kernel,
        out_shape=(
            shape((9, 256, 256), BF16),
            shape((128, 256), BF16),
            shape((256, 128), BF16),
            shape((80, 256), BF16),
        ),
        in_specs=[VMEM] * 4,
        out_specs=(VMEM,) * 4,
        compiler_params=params(8),
        cost_estimate=cost(27 * 256 * 16 * 256 * 2, 3 << 20),
        name="weights",
    )(*weights)
    ylo, yhi, band, pair, pair_t, table = lax.optimization_barrier(
        (ylo, yhi, band, pair, pair_t, table)
    )

    def whole(z):
        row = lax.broadcasted_iota(jnp.int32, (80, 80), 0)
        face = jnp.where(row == 64, ylo[z][None], features[z, :80])
        return jnp.where(row == 65, yhi[z][None], face)

    zlo = lax.ppermute(whole(31), "sz", up_z)
    zhi = lax.ppermute(whole(0), "sz", [(j, i) for i, j in up_z])
    embedded, slope, hidden, edge = pl.pallas_call(
        inner_kernel,
        out_shape=(
            shape((17, 2, 128, 256), BF16),
            pltpu.HBM((4, 256, 512), F32),
            shape((4, 256, 512), BF16),
            shape((2, 2, 256, 32), F32),
        ),
        in_specs=[VMEM] * 5,
        out_specs=(VMEM, HBM, VMEM, VMEM),
        scratch_shapes=[pltpu.VMEM((4, 256, 512), F32), pltpu.SemaphoreType.DMA((8,))],
        compiler_params=params(12),
        cost_estimate=cost(3 << 30, 10 << 20),
        name="inner",
    )(features, ylo, yhi, table, band)
    faces, edge_slope, hidden, coarse = pl.pallas_call(
        outer_kernel,
        out_shape=(
            shape((2, 128, 256), BF16),
            shape((256, 128), F32),
            pltpu.HBM((4, 256, 512), BF16),
            pltpu.HBM((1024, 256), BF16),
        ),
        in_specs=[VMEM] * 7,
        out_specs=(VMEM, VMEM, HBM, HBM),
        scratch_shapes=[
            pltpu.VMEM((512, 512), F32),
            pltpu.VMEM((2, 1024, 128), F32),
            pltpu.VMEM((4, 256, 512), BF16),
            pltpu.VMEM((1024, 256), BF16),
            pltpu.SemaphoreType.DMA((3,)),
        ],
        compiler_params=params(8),
        cost_estimate=cost(1 << 30, 4 << 20),
        name="outer",
    )(zlo, zhi, table, band, pair, edge, hidden)

    mix_weight, cotangent_rows, coarse = lax.optimization_barrier(
        (mix_weight, cotangent.reshape(mine, 256, width), coarse)
    )
    sent = lax.all_to_all(
        coarse.reshape(count_z, mine * 16, 256), "sz", split_axis=0, concat_axis=0, tiled=True
    )
    block = lambda *dims: pl.BlockSpec(dims, lambda c: (c,) + (0,) * (len(dims) - 1))
    shares = count_y // 2
    mix_specs = [
        pl.BlockSpec((count_z, 16, 256), lambda c: (0, c, 0)),
        block(1, width, width),
        block(1, width, 256),
    ]
    mix_t, cotangent_t = pl.pallas_call(
        turn_kernel,
        grid=(mine,),
        out_shape=(shape((mine, width, width), BF16), shape((mine, width, 256), BF16)),
        in_specs=[block(1, width, width), block(1, 256, width)],
        out_specs=(block(1, width, width), block(1, width, 256)),
        compiler_params=params(4),
        cost_estimate=cost(1 << 20, 2 << 20),
        name="turn",
    )(mix_weight, cotangent_rows)
    back = pl.pallas_call(
        mix_kernel,
        out_shape=pltpu.HBM((count_z, mine * 16, 256), BF16),
        in_specs=[VMEM] * 4,
        out_specs=HBM,
        scratch_shapes=[
            pltpu.VMEM((count_z, mine * 16, 256), BF16),
            pltpu.SemaphoreType.DMA((mine,)),
        ],
        compiler_params=params(8),
        cost_estimate=cost(mine * 2 * 2 * 256 * width * width, 2 << 20),
        name="mix",
    )(sent, mix_weight, cotangent_t, mix_t)
    coarse_grad = lax.all_to_all(back, "sz", split_axis=0, concat_axis=0, tiled=True)
    sent, back = lax.optimization_barrier((sent, back))
    mid, *mix_parts = pl.pallas_call(
        lambda *refs: mix_grad_kernel(1.0 / math.sqrt(8 * 32 * count_y), *refs),
        grid=(mine,),
        out_shape=[shape((mine, 256, width), BF16)]
        + [
            pltpu.HBM((mine, width // shares, width), BF16 if k else F32) for k in range(shares)
        ],
        in_specs=[pl.BlockSpec(memory_space=pltpu.SMEM)] + mix_specs,
        out_specs=[block(1, 256, width)] + [block(1, width // shares, width)] * shares,
        scratch_shapes=[pltpu.VMEM((width, width), F32)],
        compiler_params=params(8),
        cost_estimate=cost(mine * 2 * 2 * 256 * width * width, 3 << 20),
        name="mix_grad",
    )(lax.axis_index("sy")[None], sent, mix_weight, cotangent_t)
    mix_sum = mix_parts[0]
    moved = []
    for k, part in enumerate(mix_parts[1:], 1):
        moved.append(lax.ppermute(part, "sy", [(i, i ^ (2 * k)) for i in range(count_y)]))
    cells = 16 * 64 * count_y * 32 * count_z
    sums = pl.pallas_call(
        lambda *refs: backward_kernel(
            1.0 / math.sqrt(cells // 8), 1.0 / math.sqrt(cells), *refs
        ),
        out_shape=shape((128, 128), F32),
        in_specs=[VMEM, HBM, HBM, HBM] + [VMEM] * 4,
        out_specs=VMEM,
        scratch_shapes=[
            pltpu.VMEM((512, 512), F32),
            pltpu.VMEM((2, 1024, 128), F32),
            pltpu.VMEM((4, 256, 512), BF16),
            pltpu.VMEM((17, 2, 128, 256), BF16),
            pltpu.VMEM((4, 256, 512), F32),
            pltpu.VMEM((4, 256, 512), BF16),
            pltpu.SemaphoreType.DMA((3,)),
        ],
        compiler_params=params(12),
        cost_estimate=cost(4 << 30, 8 << 20),
        name="backward",
    )(
        coarse_grad.reshape(1024, 256),
        *kept(embedded, slope, hidden),
        pair,
        pair_t,
        faces,
        edge_slope,
    )
    *moved, sums = lax.optimization_barrier((*moved, sums))
    for part in moved:
        mix_sum = mix_sum + part.astype(F32)
    mine_last, other = jnp.split(mix_sum, 2, axis=1)
    other = lax.ppermute(other.astype(BF16), "sy", [(i, i ^ 1) for i in range(count_y)])
    mix_grad = mine_last + other.astype(F32)

    rounds = sum_rounds(count_y, count_z)
    for masks in rounds[:-1]:
        parts = [sums] + exchanged(sums, masks, count_y * count_z)
        sums = parts[0] + parts[1] if len(parts) == 2 else (parts[0] + parts[1]) + (parts[2] + parts[3])
    down_grad, conv_grad = pl.pallas_call(
        finish_kernel,
        out_shape=(shape((8, 16, 64), F32), shape((256, 27), F32)),
        in_specs=[VMEM] * 4,
        out_specs=(VMEM,) * 2,
        compiler_params=params(8),
        cost_estimate=cost(1 << 20, 1 << 18),
        name="finish",
    )(sums, *exchanged(sums, rounds[-1], count_y * count_z))
    down_grad = jnp.transpose(down_grad, (0, 2, 1))
    conv_grad = jnp.transpose(conv_grad.reshape(16, 16, 27), (2, 0, 1))
    return (mid.reshape(cotangent.shape), mix_grad, down_grad, conv_grad)


def solution(mesh):
    in_specs = (
        P(None, "sy", "sz"),
        P(None, "sy", "sz"),
        P(),
        P(),
        P(),
        P(),
        P("sz", None, None),
        P("sz", None, "sy", None),
    )
    out_specs = (P("sz", None, "sy", None), P("sz", "sy", None), P(), P())
    return jax.shard_map(
        per_device, mesh=mesh, in_specs=in_specs, out_specs=out_specs, check_vma=False
    )
```

```python
import math

import jax
import jax.numpy as jnp
from jax import lax
from jax.experimental import pallas as pl
from jax.experimental.pallas import tpu as pltpu
from jax.sharding import PartitionSpec as P

F32 = jnp.float32
BF16 = jnp.bfloat16
VMEM = pl.BlockSpec(memory_space=pltpu.VMEM)
HBM = pl.BlockSpec(memory_space=pltpu.HBM)
RUNS = ((64, 0, 32), (0, 32, 96))


def dot(a, b, ca, cb):
    return lax.dot_general(a, b, (((ca,), (cb,)), ((), ())), preferred_element_type=F32)


def iota(shape, dim):
    return lax.broadcasted_iota(jnp.int32, shape, dim)


def fetch(sources, targets, sem):
    copies = [pltpu.make_async_copy(a, b, sem.at[k]) for k, (a, b) in enumerate(zip(sources, targets))]
    for copy in copies:
        copy.start()
    return copies


def feature_kernel(
    lab_hbm, wd_hbm, conv_hbm, down_hbm, mat_hbm, dist_hbm,
    out_ref, first_ref, last_ref, conv_ref, down_ref, mat_ref, dist_ref,
    lab_s, wd_b, wd_s, first_s, last_s, sem,
):
    copies = fetch(
        (lab_hbm, wd_hbm, conv_hbm, down_hbm, mat_hbm, dist_hbm),
        (lab_s, wd_b, conv_ref, down_ref, mat_ref, dist_ref),
        sem,
    )
    row = iota((128, 64), 0)
    run, r = row // 32, row % 32
    y = jnp.where(run == 0, 2 * r, jnp.where(run == 1, 2 * r + 1, jnp.where(run == 2, 2 * r - 1, 2 * r + 2)))
    pick = (y == iota((128, 64), 1)).astype(BF16)
    copies[0].wait()
    copies[1].wait()
    wd_s[...] = wd_b[...].astype(F32)
    for z in range(out_ref.shape[0]):
        lab = lab_s[pl.ds(z, 16, stride=32), :]
        parts = [(lab == m).astype(F32).astype(BF16) for m in range(4)]
        parts.append(wd_s[pl.ds(z, 16, stride=32), :].astype(BF16))
        rows = dot(pick, jnp.concatenate(parts, axis=0), 1, 1)
        out_ref[z] = rows.astype(BF16)
        first_s[z : z + 1, :] = rows[0:1, :]
        last_s[z : z + 1, :] = rows[63:64, :]
    first_ref[...] = first_s[...].astype(BF16)
    last_ref[...] = last_s[...].astype(BF16)
    for copy in copies[2:]:
        copy.wait()


def weight_kernel(
    conv_ref, down_ref, mat_ref, dist_ref, band_ref, pair_ref, pair_t_ref, table_ref
):
    spread = (iota((256, 16), 0) % 16 == iota((256, 16), 1)).astype(BF16)
    taps = conv_ref[...].reshape(256, 27)
    repeat = (iota((27, 432), 0) == iota((27, 432), 1) // 16).astype(BF16)
    own = iota((256, 432), 0) % 16 == iota((256, 432), 1) % 16
    apart = jnp.where(own, dot(taps, repeat, 1, 0), 0.0).astype(BF16)
    gather = (iota((256, 256), 0) % 16 == iota((256, 256), 1) // 16).astype(BF16)
    wide = dot(gather, apart, 1, 0).astype(BF16)
    offset = iota((256, 256), 1) // 16 - iota((256, 256), 0) // 16 + 1
    for t in range(9):
        total = jnp.zeros((256, 256), F32)
        for tx in range(3):
            at = (tx * 9 + t) * 16
            tile = dot(wide[:, at : at + 16], spread, 1, 1)
            total = jnp.where(offset == tx, tile, total)
        band_ref[t] = total.astype(BF16)
    for bc in range(4):
        for x2 in range(2):
            for a in range(2):
                tap = down_ref[4 * a + bc]
                none = jnp.zeros_like(tap)
                at = 64 * bc + 32 * x2 + 16 * a
                pair_t_ref[at : at + 16, :] = jnp.concatenate([none, tap] if x2 else [tap, none], axis=1)
    pair_ref[...] = pair_t_ref[...].T
    lane_e = iota((16, 256), 1) // 16
    row_e = iota((16, 256), 0)
    mat = dot(mat_ref[...], spread, 1, 1)
    dist = dot(dist_ref[...], spread, 1, 1)
    for m in range(5):
        line = jnp.broadcast_to(mat[m : m + 1, :] if m < 4 else dist, (16, 256))
        table_ref[16 * m : 16 * m + 16, :] = jnp.where(lane_e == row_e, line, 0.0).astype(BF16)


def activate(acc):
    sigma = jax.nn.sigmoid(acc)
    return (acc * sigma).astype(BF16), sigma * (1.0 + acc * (1.0 - sigma))


def cells_of(emb_ref, b, c, ty, tz, half):
    run = RUNS[b][ty]
    q = (c + tz) // 2 + 8 * half
    return emb_ref[q : q + 8, (c + tz) % 2, run : run + 32, :].reshape(256, 256)


def inner_kernel(
    feat_ref, ylo_ref, yhi_ref, table_ref, band_ref, emb_ref, slope_hbm, hidden_ref, edge_ref,
    slope_ref, sem,
):
    table = table_ref[...]
    row = iota((128, 80), 0)
    emb_ref[0, 0] = jnp.zeros((128, 256), BF16)
    emb_ref[16, 1] = jnp.zeros((128, 256), BF16)
    ylo = ylo_ref[...].astype(F32)
    yhi = yhi_ref[...].astype(F32)
    for z in range(32):
        f = feat_ref[z].astype(F32)
        f = jnp.where(row == 64, ylo[z : z + 1, :], f)
        f = jnp.where(row == 127, yhi[z : z + 1, :], f)
        emb_ref[(z + 1) // 2, (z + 1) % 2] = dot(f.astype(BF16), table, 1, 0).astype(BF16)
    copies = []
    for bc in range(4):
        b, c = bc // 2, bc % 2
        for half in range(2):
            acc = None
            for ty in range(3):
                for tz in range(3):
                    part = dot(band_ref[3 * ty + tz], cells_of(emb_ref, b, c, ty, tz, half), 1, 1)
                    acc = part if acc is None else acc + part
            if half == 0 and c == 0:
                edge_ref[0, b] = acc[:, :32]
            if half == 1 and c == 1:
                edge_ref[1, b] = acc[:, 224:]
            at = slice(256 * half, 256 * half + 256)
            hidden_ref[bc, :, at], slope_ref[bc, :, at] = activate(acc)
            part = (bc, slice(None), pl.ds(256 * half, 256))
            copies.append(pltpu.make_async_copy(slope_ref.at[part], slope_hbm.at[part], sem.at[len(copies)]))
            copies[-1].start()
    for copy in copies:
        copy.wait()


def pair_rows(hidden_ref, pair):
    return jnp.concatenate([hidden_ref[bc, 64 * pair : 64 * pair + 64, :] for bc in range(4)], axis=0)


def outer_kernel(
    zlo_ref, zhi_ref, table_ref, band_ref, pair_ref, edge_ref, inner_ref,
    emb_ref, slope_ref, hidden_hbm, coarse_hbm, turn_a, turn_b, hidden_ref, coarse_ref, sem,
):
    table = table_ref[...]
    hidden_ref[...] = inner_ref[...]
    for side, face in enumerate((zlo_ref, zhi_ref)):
        f = face[...].astype(F32)
        runs = [f[:64], f[64:65], f[32:63], f[1:32], f[65:66]]
        plane = dot(jnp.concatenate(runs, axis=0).astype(BF16), table, 1, 0).astype(BF16)
        emb_ref[side] = plane
        for b in range(2):
            acc = edge_ref[side, b]
            for ty in range(3):
                run = RUNS[b][ty]
                acc = acc + dot(band_ref[3 * ty + 2 * side], plane[run : run + 32], 1, 1)
            at = slice(480 * side, 480 * side + 32)
            hidden_ref[2 * b + side, :, at], slope_ref[:, 64 * side + 32 * b : 64 * side + 32 * b + 32] = activate(acc)
    copies = [pltpu.make_async_copy(hidden_ref, hidden_hbm, sem.at[0])]
    copies[0].start()
    for pair in range(4):
        turn_a[128 * pair : 128 * pair + 128, :] = dot(pair_ref[...], pair_rows(hidden_ref, pair), 1, 0)
    for half in range(2):
        for z2 in range(16):
            pieces = [
                turn_a[64 * x2 : 64 * x2 + 64, 32 * z2 : 32 * z2 + 32]
                for x2 in range(4 * half, 4 * half + 4)
            ]
            turn_b[half, pl.ds(z2, 64, stride=16), :] = jnp.concatenate(pieces, axis=1)
        at = (slice(None), pl.ds(128 * half, 128))
        coarse_ref[at] = turn_b[half].astype(BF16)
        copies.append(pltpu.make_async_copy(coarse_ref.at[at], coarse_hbm.at[at], sem.at[1 + half]))
        copies[-1].start()
    for copy in copies:
        copy.wait()


def turn_kernel(mix_ref, cot_ref, mix_t_ref, cot_t_ref):
    mix_t_ref[0] = mix_ref[0].T
    cot_t_ref[0] = cot_ref[0].T


def mixed(coarse, mix, cot_t):
    pre = dot(mix, coarse, 1, 0)
    sigma = jax.nn.sigmoid(pre)
    grad = cot_t.astype(F32) * (sigma * (1.0 + pre * (1.0 - sigma)))
    return pre * sigma, grad.astype(BF16)


def mix_kernel(coarse_ref, mix_ref, cot_t_ref, mix_t_ref, grad_hbm, grad_ref, sem):
    copies = []
    for c in range(mix_ref.shape[0]):
        at = (slice(None), pl.ds(16 * c, 16), slice(None))
        _, grad = mixed(coarse_ref[at].reshape(-1, 256), mix_ref[c], cot_t_ref[c])
        part = dot(mix_t_ref[c], grad, 1, 0).astype(BF16)
        grad_ref[at] = part.reshape(-1, 16, 256)
        copies.append(pltpu.make_async_copy(grad_ref.at[at], grad_hbm.at[at], sem.at[c]))
        copies[-1].start()
    for copy in copies:
        copy.wait()


def mix_grad_kernel(scale, me_ref, coarse_ref, mix_ref, cot_t_ref, mid_ref, *more_refs):
    *share_refs, total_ref = more_refs
    coarse = coarse_ref[...].reshape(-1, 256)
    mid, grad = mixed(coarse, mix_ref[0], cot_t_ref[0])
    mid_ref[0] = mid.astype(BF16).T
    total_ref[...] = dot(grad, coarse, 1, 1) * scale
    rows = total_ref.shape[0] // (2 * len(share_refs))
    for place in range(2 * len(share_refs)):
        start = pl.multiple_of(jnp.bitwise_xor(me_ref[0], place) * rows, rows)
        at = place % 2 * rows
        share_ref = share_refs[place // 2]
        share_ref[0, at : at + rows, :] = total_ref[pl.ds(start, rows), :].astype(share_ref.dtype)


def fold(value, step):
    lanes = value.shape[-1]
    if lanes == 256:
        value = value[:, :128] + value[:, 128:]
    shift = 64
    while shift >= step:
        value = value + pltpu.roll(value, shift, 1)
        shift //= 2
    return value


def backward_kernel(
    down_scale, conv_scale, cgrad_ref, emb_hbm, slope_hbm, hidden_hbm, pair_ref, pair_t_ref, face_ref, edge_ref,
    out_ref, turn_a, turn_b, turned_pg, emb_in, slope_in, hidden_ref, sem,
):
    copies = []
    for source, target in ((hidden_hbm, hidden_ref), (slope_hbm, slope_in)):
        for bc in range(4):
            copies.append(pltpu.make_async_copy(source.at[bc], target.at[bc], sem.at[len(copies)]))
    for q in range(0, 17, 4):
        part = pl.ds(q, min(4, 17 - q))
        copies.append(pltpu.make_async_copy(emb_hbm.at[part], emb_in.at[part], sem.at[len(copies)]))
    for copy in copies:
        copy.start()
    for half in range(2):
        turn_b[half] = cgrad_ref[:, 128 * half : 128 * half + 128].astype(F32)
    for half in range(2):
        for quad in range(4):
            pieces = [turn_b[half, pl.ds(4 * quad + k, 64, stride=16), :] for k in range(4)]
            for k in range(4):
                x2 = 4 * half + k
                turn_a[64 * x2 : 64 * x2 + 64, 128 * quad : 128 * quad + 128] = jnp.concatenate(
                    [p[:, 32 * k : 32 * k + 32] for p in pieces], axis=1
                )
    cg_t = turn_a[...].astype(BF16)
    pairs = [cg_t[128 * pair : 128 * pair + 128, :] for pair in range(4)]
    for copy in copies[:4]:
        copy.wait()
    down = None
    for pair in range(4):
        part = dot(pairs[pair], pair_rows(hidden_ref, pair), 1, 1)
        down = part if down is None else down + part
    down = jnp.where(iota((64, 256), 1) // 32 % 2 == 0, down[:64], down[64:]) * down_scale
    left = down[:, :128] + pltpu.roll(down[:, :128], 96, 1)
    right = down[:, 128:] + pltpu.roll(down[:, 128:], 32, 1)
    out_ref[0:64, :] = jnp.where(iota((64, 128), 1) // 32 % 2 == 0, left, right)
    for copy in copies[4:8]:
        copy.wait()
    for pair in range(4):
        hgrad = dot(pair_t_ref[...], pairs[pair], 1, 0)
        at = slice(64 * pair, 64 * pair + 64)
        for bc in range(4):
            rows = hgrad[64 * bc : 64 * bc + 64]
            turned_pg[bc, at, :] = (rows * slope_in[bc, at, :]).astype(BF16)
            edge = slice(480 * (bc % 2), 480 * (bc % 2) + 32)
            low = 64 * (bc % 2) + 32 * (bc // 2)
            turned_pg[bc, at, edge] = (rows[:, edge] * edge_ref[at, low : low + 32]).astype(BF16)
    for copy in copies[8:]:
        copy.wait()
    lane_x = iota((16, 128), 1) // 16
    own = iota((8, 128), 1) // 16 == iota((8, 128), 0)
    for ty in range(3):
        for tz in range(3):
            acc = None
            for bc in range(4):
                b, c = bc // 2, bc % 2
                for half in range(2):
                    rows = cells_of(emb_in, b, c, ty, tz, half)
                    run = RUNS[b][ty]
                    if c + tz == 0 and half == 0:
                        rows = jnp.concatenate([face_ref[0, run : run + 32, :], rows[32:]], axis=0)
                    if c + tz == 3 and half == 1:
                        rows = jnp.concatenate([rows[:224], face_ref[1, run : run + 32, :]], axis=0)
                    part = dot(turned_pg[bc, :, 256 * half : 256 * half + 256], rows, 1, 0)
                    acc = part if acc is None else acc + part
            for tx in range(3):
                total = None
                for side in range(2):
                    half = jnp.zeros((16, 128), F32)
                    for x in range(16):
                        lane = x + tx - 1 - 8 * side
                        if 0 <= lane < 8:
                            part = acc[16 * x : 16 * x + 16, 128 * side : 128 * side + 128]
                            half = jnp.where(lane_x == lane, part, half)
                    total = half if total is None else total + half
                tap = 9 * tx + 3 * ty + tz
                total = fold(total, 16) * conv_scale
                for half in range(2):
                    part = jnp.where(own, total[8 * half : 8 * half + 8], 0.0)
                    line = 64 + 32 * half + tap
                    out_ref[line : line + 1, :] = jnp.sum(part, axis=0, keepdims=True)
    for half in range(2):
        out_ref[91 + 32 * half : 96 + 32 * half, :] = jnp.zeros((5, 128), F32)


def finish_kernel(a_ref, b_ref, c_ref, d_ref, down_ref, conv_ref):
    total = (a_ref[...] + b_ref[...]) + (c_ref[...] + d_ref[...])
    down = total[:64].T
    for a in range(2):
        for bc in range(4):
            at = (2 * (2 * (bc % 2) + bc // 2) + a) * 16
            down_ref[4 * a + bc] = down[at : at + 16, :]
    for half in range(2):
        conv = total[64 + 32 * half : 96 + 32 * half].T
        conv_ref[128 * half : 128 * half + 128, :] = conv[:, :27]


def kept(*values):
    return [pltpu.with_memory_space_constraint(v, pltpu.HBM) for v in values]


def params(mib):
    return pltpu.CompilerParams(vmem_limit_bytes=mib << 20)


def cost(flops, nbytes):
    return pl.CostEstimate(flops=flops, bytes_accessed=nbytes, transcendentals=0)


def shape(dims, dtype):
    return jax.ShapeDtypeStruct(dims, dtype)


def sum_rounds(count_y, count_z):
    in_z = [1 << k for k in range(count_z.bit_length() - 1)]
    in_y = [count_z << k for k in range(count_y.bit_length() - 1)]
    order = in_z[:1] + in_z[1:2] + in_y[:1] + in_z[2:] + in_y[1:]
    rounds, order = ([order[:1]] if len(order) % 2 else []), order[len(order) % 2 :]
    return rounds + [order[k : k + 2] for k in range(0, len(order), 2)]


def exchanged(value, masks, count):
    masks = list(masks) + [masks[0] ^ masks[1]] if len(masks) == 2 else masks
    return [lax.ppermute(value, ("sy", "sz"), [(i, i ^ m) for i in range(count)]) for m in masks]


def per_device(
    labels, wall_dist, material_table, dist_weight, conv_weight, down_weight, mix_weight, cotangent
):
    count_y = lax.axis_size("sy")
    count_z = lax.axis_size("sz")
    mine = 64 // count_z
    width = mix_weight.shape[1]
    features, first, last, *weights = pl.pallas_call(
        feature_kernel,
        out_shape=(
            shape((32, 128, 80), BF16),
            shape((32, 80), BF16),
            shape((32, 80), BF16),
            shape((16, 16, 27), BF16),
            shape((8, 16, 64), BF16),
            shape((4, 16), BF16),
            shape((1, 16), BF16),
        ),
        in_specs=[HBM] * 6,
        out_specs=(VMEM,) * 7,
        scratch_shapes=[
            pltpu.VMEM((512, 64), jnp.int32),
            pltpu.VMEM((512, 64), BF16),
            pltpu.VMEM((512, 64), F32),
            pltpu.VMEM((32, 80), F32),
            pltpu.VMEM((32, 80), F32),
            pltpu.SemaphoreType.DMA((6,)),
        ],
        compiler_params=params(8),
        cost_estimate=cost(32 * 128 * 64 * 80 * 2, 2 << 20),
        name="features",
    )(
        *kept(
            jnp.transpose(labels, (0, 2, 1)).reshape(512, 64),
            jnp.transpose(wall_dist, (0, 2, 1)).reshape(512, 64),
            jnp.transpose(conv_weight, (1, 2, 0)),
            jnp.transpose(down_weight, (0, 2, 1)),
            material_table,
            dist_weight[None],
        )
    )
    up_y = [(i, i + 1) for i in range(count_y - 1)]
    up_z = [(i, i + 1) for i in range(count_z - 1)]
    ylo = lax.ppermute(last, "sy", up_y)
    yhi = lax.ppermute(first, "sy", [(j, i) for i, j in up_y])
    band, pair, pair_t, table = pl.pallas_call(
        weight_kernel,
        out_shape=(
            shape((9, 256, 256), BF16),
            shape((128, 256), BF16),
            shape((256, 128), BF16),
            shape((80, 256), BF16),
        ),
        in_specs=[VMEM] * 4,
        out_specs=(VMEM,) * 4,
        compiler_params=params(8),
        cost_estimate=cost(27 * 256 * 16 * 256 * 2, 3 << 20),
        name="weights",
    )(*weights)
    ylo, yhi, band, pair, pair_t, table = lax.optimization_barrier(
        (ylo, yhi, band, pair, pair_t, table)
    )

    def whole(z):
        row = lax.broadcasted_iota(jnp.int32, (80, 80), 0)
        face = jnp.where(row == 64, ylo[z][None], features[z, :80])
        return jnp.where(row == 65, yhi[z][None], face)

    zlo = lax.ppermute(whole(31), "sz", up_z)
    zhi = lax.ppermute(whole(0), "sz", [(j, i) for i, j in up_z])
    embedded, slope, hidden, edge = pl.pallas_call(
        inner_kernel,
        out_shape=(
            shape((17, 2, 128, 256), BF16),
            pltpu.HBM((4, 256, 512), F32),
            shape((4, 256, 512), BF16),
            shape((2, 2, 256, 32), F32),
        ),
        in_specs=[VMEM] * 5,
        out_specs=(VMEM, HBM, VMEM, VMEM),
        scratch_shapes=[pltpu.VMEM((4, 256, 512), F32), pltpu.SemaphoreType.DMA((8,))],
        compiler_params=params(12),
        cost_estimate=cost(3 << 30, 10 << 20),
        name="inner",
    )(features, ylo, yhi, table, band)
    faces, edge_slope, hidden, coarse = pl.pallas_call(
        outer_kernel,
        out_shape=(
            shape((2, 128, 256), BF16),
            shape((256, 128), F32),
            pltpu.HBM((4, 256, 512), BF16),
            pltpu.HBM((1024, 256), BF16),
        ),
        in_specs=[VMEM] * 7,
        out_specs=(VMEM, VMEM, HBM, HBM),
        scratch_shapes=[
            pltpu.VMEM((512, 512), F32),
            pltpu.VMEM((2, 1024, 128), F32),
            pltpu.VMEM((4, 256, 512), BF16),
            pltpu.VMEM((1024, 256), BF16),
            pltpu.SemaphoreType.DMA((3,)),
        ],
        compiler_params=params(8),
        cost_estimate=cost(1 << 30, 4 << 20),
        name="outer",
    )(zlo, zhi, table, band, pair, edge, hidden)

    mix_weight, cotangent_rows, coarse = lax.optimization_barrier(
        (mix_weight, cotangent.reshape(mine, 256, width), coarse)
    )
    sent = lax.all_to_all(
        coarse.reshape(count_z, mine * 16, 256), "sz", split_axis=0, concat_axis=0, tiled=True
    )
    block = lambda *dims: pl.BlockSpec(dims, lambda c: (c,) + (0,) * (len(dims) - 1))
    shares = count_y // 2
    mix_specs = [
        pl.BlockSpec((count_z, 16, 256), lambda c: (0, c, 0)),
        block(1, width, width),
        block(1, width, 256),
    ]
    mix_t, cotangent_t = pl.pallas_call(
        turn_kernel,
        grid=(mine,),
        out_shape=(shape((mine, width, width), BF16), shape((mine, width, 256), BF16)),
        in_specs=[block(1, width, width), block(1, 256, width)],
        out_specs=(block(1, width, width), block(1, width, 256)),
        compiler_params=params(4),
        cost_estimate=cost(1 << 20, 2 << 20),
        name="turn",
    )(mix_weight, cotangent_rows)
    back = pl.pallas_call(
        mix_kernel,
        out_shape=pltpu.HBM((count_z, mine * 16, 256), BF16),
        in_specs=[VMEM] * 4,
        out_specs=HBM,
        scratch_shapes=[
            pltpu.VMEM((count_z, mine * 16, 256), BF16),
            pltpu.SemaphoreType.DMA((mine,)),
        ],
        compiler_params=params(8),
        cost_estimate=cost(mine * 2 * 2 * 256 * width * width, 2 << 20),
        name="mix",
    )(sent, mix_weight, cotangent_t, mix_t)
    coarse_grad = lax.all_to_all(back, "sz", split_axis=0, concat_axis=0, tiled=True)
    sent, back = lax.optimization_barrier((sent, back))
    mid, *mix_parts = pl.pallas_call(
        lambda *refs: mix_grad_kernel(1.0 / math.sqrt(8 * 32 * count_y), *refs),
        grid=(mine,),
        out_shape=[shape((mine, 256, width), BF16)]
        + [
            pltpu.HBM((mine, width // shares, width), BF16 if k else F32) for k in range(shares)
        ],
        in_specs=[pl.BlockSpec(memory_space=pltpu.SMEM)] + mix_specs,
        out_specs=[block(1, 256, width)] + [block(1, width // shares, width)] * shares,
        scratch_shapes=[pltpu.VMEM((width, width), F32)],
        compiler_params=params(8),
        cost_estimate=cost(mine * 2 * 2 * 256 * width * width, 3 << 20),
        name="mix_grad",
    )(lax.axis_index("sy")[None], sent, mix_weight, cotangent_t)
    mix_sum = mix_parts[0]
    moved = []
    for k, part in enumerate(mix_parts[1:], 1):
        moved.append(lax.ppermute(part, "sy", [(i, i ^ (2 * k)) for i in range(count_y)]))
    cells = 16 * 64 * count_y * 32 * count_z
    sums = pl.pallas_call(
        lambda *refs: backward_kernel(
            1.0 / math.sqrt(cells // 8), 1.0 / math.sqrt(cells), *refs
        ),
        out_shape=shape((128, 128), F32),
        in_specs=[VMEM, HBM, HBM, HBM] + [VMEM] * 4,
        out_specs=VMEM,
        scratch_shapes=[
            pltpu.VMEM((512, 512), F32),
            pltpu.VMEM((2, 1024, 128), F32),
            pltpu.VMEM((4, 256, 512), BF16),
            pltpu.VMEM((17, 2, 128, 256), BF16),
            pltpu.VMEM((4, 256, 512), F32),
            pltpu.VMEM((4, 256, 512), BF16),
            pltpu.SemaphoreType.DMA((13,)),
        ],
        compiler_params=params(12),
        cost_estimate=cost(4 << 30, 8 << 20),
        name="backward",
    )(
        coarse_grad.reshape(1024, 256),
        *kept(embedded, slope, hidden),
        pair,
        pair_t,
        faces,
        edge_slope,
    )
    *moved, sums = lax.optimization_barrier((*moved, sums))
    for part in moved:
        mix_sum = mix_sum + part.astype(F32)
    mine_last, other = jnp.split(mix_sum, 2, axis=1)
    other = lax.ppermute(other.astype(BF16), "sy", [(i, i ^ 1) for i in range(count_y)])
    mix_grad = mine_last + other.astype(F32)

    rounds = sum_rounds(count_y, count_z)
    for masks in rounds[:-1]:
        parts = [sums] + exchanged(sums, masks, count_y * count_z)
        sums = parts[0] + parts[1] if len(parts) == 2 else (parts[0] + parts[1]) + (parts[2] + parts[3])
    down_grad, conv_grad = pl.pallas_call(
        finish_kernel,
        out_shape=(shape((8, 16, 64), F32), shape((256, 27), F32)),
        in_specs=[VMEM] * 4,
        out_specs=(VMEM,) * 2,
        compiler_params=params(8),
        cost_estimate=cost(1 << 20, 1 << 18),
        name="finish",
    )(sums, *exchanged(sums, rounds[-1], count_y * count_z))
    down_grad = jnp.transpose(down_grad, (0, 2, 1))
    conv_grad = jnp.transpose(conv_grad.reshape(16, 16, 27), (2, 0, 1))
    return (mid.reshape(cotangent.shape), mix_grad, down_grad, conv_grad)


def solution(mesh):
    in_specs = (
        P(None, "sy", "sz"),
        P(None, "sy", "sz"),
        P(),
        P(),
        P(),
        P(),
        P("sz", None, None),
        P("sz", None, "sy", None),
    )
    out_specs = (P("sz", None, "sy", None), P("sz", "sy", None), P(), P())
    return jax.shard_map(
        per_device, mesh=mesh, in_specs=in_specs, out_specs=out_specs, check_vma=False
    )
```

```python
import math

import jax
import jax.numpy as jnp
from jax import lax
from jax.experimental import pallas as pl
from jax.experimental.pallas import tpu as pltpu
from jax.sharding import PartitionSpec as P

F32 = jnp.float32
BF16 = jnp.bfloat16
VMEM = pl.BlockSpec(memory_space=pltpu.VMEM)
HBM = pl.BlockSpec(memory_space=pltpu.HBM)
RUNS = ((64, 0, 32), (0, 32, 96))


def dot(a, b, ca, cb):
    return lax.dot_general(a, b, (((ca,), (cb,)), ((), ())), preferred_element_type=F32)


def iota(shape, dim):
    return lax.broadcasted_iota(jnp.int32, shape, dim)


def fetch(sources, targets, sem):
    copies = [pltpu.make_async_copy(a, b, sem.at[k]) for k, (a, b) in enumerate(zip(sources, targets))]
    for copy in copies:
        copy.start()
    return copies


def feature_kernel(
    lab_hbm, wd_hbm, conv_hbm, down_hbm, mat_hbm, dist_hbm,
    out_ref, first_ref, last_ref, conv_ref, down_ref, mat_ref, dist_ref,
    lab_s, wd_b, wd_s, first_s, last_s, sem,
):
    copies = fetch(
        (lab_hbm, wd_hbm, conv_hbm, down_hbm, mat_hbm, dist_hbm),
        (lab_s, wd_b, conv_ref, down_ref, mat_ref, dist_ref),
        sem,
    )
    row = iota((128, 64), 0)
    run, r = row // 32, row % 32
    y = jnp.where(run == 0, 2 * r, jnp.where(run == 1, 2 * r + 1, jnp.where(run == 2, 2 * r - 1, 2 * r + 2)))
    pick = (y == iota((128, 64), 1)).astype(BF16)
    copies[0].wait()
    copies[1].wait()
    wd_s[...] = wd_b[...].astype(F32)
    for z in range(out_ref.shape[0]):
        lab = lab_s[pl.ds(z, 16, stride=32), :]
        parts = [(lab == m).astype(F32).astype(BF16) for m in range(4)]
        parts.append(wd_s[pl.ds(z, 16, stride=32), :].astype(BF16))
        rows = dot(pick, jnp.concatenate(parts, axis=0), 1, 1)
        out_ref[z] = rows.astype(BF16)
        first_s[z : z + 1, :] = rows[0:1, :]
        last_s[z : z + 1, :] = rows[63:64, :]
    first_ref[...] = first_s[...].astype(BF16)
    last_ref[...] = last_s[...].astype(BF16)
    for copy in copies[2:]:
        copy.wait()


def weight_kernel(
    conv_ref, down_ref, mat_ref, dist_ref, band_ref, pair_ref, pair_t_ref, table_ref
):
    spread = (iota((256, 16), 0) % 16 == iota((256, 16), 1)).astype(BF16)
    taps = conv_ref[...].reshape(256, 27)
    repeat = (iota((27, 432), 0) == iota((27, 432), 1) // 16).astype(BF16)
    own = iota((256, 432), 0) % 16 == iota((256, 432), 1) % 16
    apart = jnp.where(own, dot(taps, repeat, 1, 0), 0.0).astype(BF16)
    gather = (iota((256, 256), 0) % 16 == iota((256, 256), 1) // 16).astype(BF16)
    wide = dot(gather, apart, 1, 0).astype(BF16)
    offset = iota((256, 256), 1) // 16 - iota((256, 256), 0) // 16 + 1
    for t in range(9):
        total = jnp.zeros((256, 256), F32)
        for tx in range(3):
            at = (tx * 9 + t) * 16
            tile = dot(wide[:, at : at + 16], spread, 1, 1)
            total = jnp.where(offset == tx, tile, total)
        band_ref[t] = total.astype(BF16)
    for bc in range(4):
        for x2 in range(2):
            for a in range(2):
                tap = down_ref[4 * a + bc]
                none = jnp.zeros_like(tap)
                at = 64 * bc + 32 * x2 + 16 * a
                pair_t_ref[at : at + 16, :] = jnp.concatenate([none, tap] if x2 else [tap, none], axis=1)
    pair_ref[...] = pair_t_ref[...].T
    lane_e = iota((16, 256), 1) // 16
    row_e = iota((16, 256), 0)
    mat = dot(mat_ref[...], spread, 1, 1)
    dist = dot(dist_ref[...], spread, 1, 1)
    for m in range(5):
        line = jnp.broadcast_to(mat[m : m + 1, :] if m < 4 else dist, (16, 256))
        table_ref[16 * m : 16 * m + 16, :] = jnp.where(lane_e == row_e, line, 0.0).astype(BF16)


def activate(acc):
    sigma = jax.nn.sigmoid(acc)
    return (acc * sigma).astype(BF16), sigma * (1.0 + acc * (1.0 - sigma))


def cells_of(emb_ref, b, c, ty, tz, half):
    run = RUNS[b][ty]
    q = (c + tz) // 2 + 8 * half
    return emb_ref[q : q + 8, (c + tz) % 2, run : run + 32, :].reshape(256, 256)


def inner_kernel(
    feat_ref, ylo_ref, yhi_ref, table_ref, band_ref, emb_ref, slope_hbm, hidden_ref, edge_ref,
    slope_ref, sem,
):
    table = table_ref[...]
    row = iota((128, 80), 0)
    emb_ref[0, 0] = jnp.zeros((128, 256), BF16)
    emb_ref[16, 1] = jnp.zeros((128, 256), BF16)
    ylo = ylo_ref[...].astype(F32)
    yhi = yhi_ref[...].astype(F32)
    for z in range(32):
        f = feat_ref[z].astype(F32)
        f = jnp.where(row == 64, ylo[z : z + 1, :], f)
        f = jnp.where(row == 127, yhi[z : z + 1, :], f)
        emb_ref[(z + 1) // 2, (z + 1) % 2] = dot(f.astype(BF16), table, 1, 0).astype(BF16)
    copies = []
    for bc in range(4):
        b, c = bc // 2, bc % 2
        for half in range(2):
            acc = None
            for ty in range(3):
                for tz in range(3):
                    part = dot(band_ref[3 * ty + tz], cells_of(emb_ref, b, c, ty, tz, half), 1, 1)
                    acc = part if acc is None else acc + part
            if half == 0 and c == 0:
                edge_ref[0, b] = acc[:, :32]
            if half == 1 and c == 1:
                edge_ref[1, b] = acc[:, 224:]
            at = slice(256 * half, 256 * half + 256)
            hidden_ref[bc, :, at], slope_ref[bc, :, at] = activate(acc)
            part = (bc, slice(None), pl.ds(256 * half, 256))
            copies.append(pltpu.make_async_copy(slope_ref.at[part], slope_hbm.at[part], sem.at[len(copies)]))
            copies[-1].start()
    for copy in copies:
        copy.wait()


def pair_rows(hidden_ref, pair):
    return jnp.concatenate([hidden_ref[bc, 64 * pair : 64 * pair + 64, :] for bc in range(4)], axis=0)


def outer_kernel(
    zlo_ref, zhi_ref, table_ref, band_ref, pair_ref, edge_ref, inner_ref,
    emb_ref, slope_ref, hidden_hbm, coarse_hbm, turn_a, turn_b, hidden_ref, coarse_ref, sem,
):
    table = table_ref[...]
    hidden_ref[...] = inner_ref[...]
    for side, face in enumerate((zlo_ref, zhi_ref)):
        f = face[...].astype(F32)
        runs = [f[:64], f[64:65], f[32:63], f[1:32], f[65:66]]
        plane = dot(jnp.concatenate(runs, axis=0).astype(BF16), table, 1, 0).astype(BF16)
        emb_ref[side] = plane
        for b in range(2):
            acc = edge_ref[side, b]
            for ty in range(3):
                run = RUNS[b][ty]
                acc = acc + dot(band_ref[3 * ty + 2 * side], plane[run : run + 32], 1, 1)
            at = slice(480 * side, 480 * side + 32)
            hidden_ref[2 * b + side, :, at], slope_ref[:, 64 * side + 32 * b : 64 * side + 32 * b + 32] = activate(acc)
    copies = [pltpu.make_async_copy(hidden_ref, hidden_hbm, sem.at[0])]
    copies[0].start()
    for pair in range(4):
        turn_a[128 * pair : 128 * pair + 128, :] = dot(pair_ref[...], pair_rows(hidden_ref, pair), 1, 0)
    for half in range(2):
        for z2 in range(16):
            pieces = [
                turn_a[64 * x2 : 64 * x2 + 64, 32 * z2 : 32 * z2 + 32]
                for x2 in range(4 * half, 4 * half + 4)
            ]
            turn_b[half, pl.ds(z2, 64, stride=16), :] = jnp.concatenate(pieces, axis=1)
        at = (slice(None), pl.ds(128 * half, 128))
        coarse_ref[at] = turn_b[half].astype(BF16)
        copies.append(pltpu.make_async_copy(coarse_ref.at[at], coarse_hbm.at[at], sem.at[1 + half]))
        copies[-1].start()
    for copy in copies:
        copy.wait()


def turn_kernel(mix_ref, cot_ref, mix_t_ref, cot_t_ref):
    mix_t_ref[0] = mix_ref[0].T
    cot_t_ref[0] = cot_ref[0].T


def mixed(coarse, mix, cot_t):
    pre = dot(mix, coarse, 1, 0)
    sigma = jax.nn.sigmoid(pre)
    grad = cot_t.astype(F32) * (sigma * (1.0 + pre * (1.0 - sigma)))
    return pre * sigma, grad.astype(BF16)


def mix_kernel(coarse_ref, mix_ref, cot_t_ref, mix_t_ref, grad_hbm, grad_ref, sem):
    copies = []
    for c in range(mix_ref.shape[0]):
        at = (slice(None), pl.ds(16 * c, 16), slice(None))
        _, grad = mixed(coarse_ref[at].reshape(-1, 256), mix_ref[c], cot_t_ref[c])
        part = dot(mix_t_ref[c], grad, 1, 0).astype(BF16)
        grad_ref[at] = part.reshape(-1, 16, 256)
        copies.append(pltpu.make_async_copy(grad_ref.at[at], grad_hbm.at[at], sem.at[c]))
        copies[-1].start()
    for copy in copies:
        copy.wait()


def mix_grad_kernel(scale, me_ref, coarse_ref, mix_ref, cot_t_ref, mid_ref, *more_refs):
    *share_refs, total_ref = more_refs
    coarse = coarse_ref[...].reshape(-1, 256)
    mid, grad = mixed(coarse, mix_ref[0], cot_t_ref[0])
    mid_ref[0] = mid.astype(BF16).T
    total_ref[...] = dot(grad, coarse, 1, 1) * scale
    rows = total_ref.shape[0] // (2 * len(share_refs))
    for place in range(2 * len(share_refs)):
        start = pl.multiple_of(jnp.bitwise_xor(me_ref[0], place) * rows, rows)
        at = place % 2 * rows
        share_ref = share_refs[place // 2]
        share_ref[0, at : at + rows, :] = total_ref[pl.ds(start, rows), :].astype(share_ref.dtype)


def fold(value, step):
    lanes = value.shape[-1]
    if lanes == 256:
        value = value[:, :128] + value[:, 128:]
    shift = 64
    while shift >= step:
        value = value + pltpu.roll(value, shift, 1)
        shift //= 2
    return value


def backward_kernel(
    down_scale, conv_scale, cgrad_ref, emb_hbm, slope_hbm, hidden_hbm, pair_ref, pair_t_ref, face_ref, edge_ref,
    out_ref, turn_a, turn_b, turned_pg, emb_in, slope_in, hidden_ref, sem,
):
    copies = [
        pltpu.make_async_copy(slope_hbm, slope_in, sem.at[0]),
        pltpu.make_async_copy(emb_hbm, emb_in, sem.at[1]),
        pltpu.make_async_copy(hidden_hbm, hidden_ref, sem.at[2]),
    ]
    copies[2].start()
    copies[0].start()
    for half in range(2):
        turn_b[half] = cgrad_ref[:, 128 * half : 128 * half + 128].astype(F32)
    for half in range(2):
        for quad in range(4):
            pieces = [turn_b[half, pl.ds(4 * quad + k, 64, stride=16), :] for k in range(4)]
            for k in range(4):
                x2 = 4 * half + k
                turn_a[64 * x2 : 64 * x2 + 64, 128 * quad : 128 * quad + 128] = jnp.concatenate(
                    [p[:, 32 * k : 32 * k + 32] for p in pieces], axis=1
                )
    copies[1].start()
    cg_t = turn_a[...].astype(BF16)
    pairs = [cg_t[128 * pair : 128 * pair + 128, :] for pair in range(4)]
    copies[2].wait()
    down = None
    for pair in range(4):
        part = dot(pairs[pair], pair_rows(hidden_ref, pair), 1, 1)
        down = part if down is None else down + part
    down = jnp.where(iota((64, 256), 1) // 32 % 2 == 0, down[:64], down[64:]) * down_scale
    left = down[:, :128] + pltpu.roll(down[:, :128], 96, 1)
    right = down[:, 128:] + pltpu.roll(down[:, 128:], 32, 1)
    out_ref[0:64, :] = jnp.where(iota((64, 128), 1) // 32 % 2 == 0, left, right)
    copies[0].wait()
    for pair in range(4):
        hgrad = dot(pair_t_ref[...], pairs[pair], 1, 0)
        at = slice(64 * pair, 64 * pair + 64)
        for bc in range(4):
            rows = hgrad[64 * bc : 64 * bc + 64]
            turned_pg[at, 512 * bc : 512 * bc + 512] = (rows * slope_in[bc, at, :]).astype(BF16)
            first = 480 * (bc % 2)
            low = 64 * (bc % 2) + 32 * (bc // 2)
            turned_pg[at, 512 * bc + first : 512 * bc + first + 32] = (rows[:, first : first + 32] * edge_ref[at, low : low + 32]).astype(BF16)
    copies[1].wait()
    lane_x = iota((16, 128), 1) // 16
    own = iota((8, 128), 1) // 16 == iota((8, 128), 0)
    for ty in range(3):
        for tz in range(3):
            pieces = []
            for bc in range(4):
                b, c = bc // 2, bc % 2
                run = RUNS[b][ty]
                for half in range(2):
                    rows = cells_of(emb_in, b, c, ty, tz, half)
                    if c + tz == 0 and half == 0:
                        rows = jnp.concatenate([face_ref[0, run : run + 32, :], rows[32:]], axis=0)
                    if c + tz == 3 and half == 1:
                        rows = jnp.concatenate([rows[:224], face_ref[1, run : run + 32, :]], axis=0)
                    pieces.append(rows)
            acc = dot(turned_pg[...], jnp.concatenate(pieces, axis=0), 1, 0)
            for tx in range(3):
                total = None
                for side in range(2):
                    half = jnp.zeros((16, 128), F32)
                    for x in range(16):
                        lane = x + tx - 1 - 8 * side
                        if 0 <= lane < 8:
                            part = acc[16 * x : 16 * x + 16, 128 * side : 128 * side + 128]
                            half = jnp.where(lane_x == lane, part, half)
                    total = half if total is None else total + half
                tap = 9 * tx + 3 * ty + tz
                total = fold(total, 16) * conv_scale
                for half in range(2):
                    part = jnp.where(own, total[8 * half : 8 * half + 8], 0.0)
                    line = 64 + 32 * half + tap
                    out_ref[line : line + 1, :] = jnp.sum(part, axis=0, keepdims=True)
    for half in range(2):
        out_ref[91 + 32 * half : 96 + 32 * half, :] = jnp.zeros((5, 128), F32)


def finish_kernel(a_ref, b_ref, c_ref, d_ref, down_ref, conv_ref):
    total = (a_ref[...] + b_ref[...]) + (c_ref[...] + d_ref[...])
    down = total[:64].T
    for a in range(2):
        for bc in range(4):
            at = (2 * (2 * (bc % 2) + bc // 2) + a) * 16
            down_ref[4 * a + bc] = down[at : at + 16, :]
    for half in range(2):
        conv = total[64 + 32 * half : 96 + 32 * half].T
        conv_ref[128 * half : 128 * half + 128, :] = conv[:, :27]


def kept(*values):
    return [pltpu.with_memory_space_constraint(v, pltpu.HBM) for v in values]


def params(mib):
    return pltpu.CompilerParams(vmem_limit_bytes=mib << 20)


def cost(flops, nbytes):
    return pl.CostEstimate(flops=flops, bytes_accessed=nbytes, transcendentals=0)


def shape(dims, dtype):
    return jax.ShapeDtypeStruct(dims, dtype)


def sum_rounds(count_y, count_z):
    in_z = [1 << k for k in range(count_z.bit_length() - 1)]
    in_y = [count_z << k for k in range(count_y.bit_length() - 1)]
    order = in_z[:1] + in_z[1:2] + in_y[:1] + in_z[2:] + in_y[1:]
    rounds, order = ([order[:1]] if len(order) % 2 else []), order[len(order) % 2 :]
    return rounds + [order[k : k + 2] for k in range(0, len(order), 2)]


def exchanged(value, masks, count):
    masks = list(masks) + [masks[0] ^ masks[1]] if len(masks) == 2 else masks
    return [lax.ppermute(value, ("sy", "sz"), [(i, i ^ m) for i in range(count)]) for m in masks]


def per_device(
    labels, wall_dist, material_table, dist_weight, conv_weight, down_weight, mix_weight, cotangent
):
    count_y = lax.axis_size("sy")
    count_z = lax.axis_size("sz")
    mine = 64 // count_z
    width = mix_weight.shape[1]
    features, first, last, *weights = pl.pallas_call(
        feature_kernel,
        out_shape=(
            shape((32, 128, 80), BF16),
            shape((32, 80), BF16),
            shape((32, 80), BF16),
            shape((16, 16, 27), BF16),
            shape((8, 16, 64), BF16),
            shape((4, 16), BF16),
            shape((1, 16), BF16),
        ),
        in_specs=[HBM] * 6,
        out_specs=(VMEM,) * 7,
        scratch_shapes=[
            pltpu.VMEM((512, 64), jnp.int32),
            pltpu.VMEM((512, 64), BF16),
            pltpu.VMEM((512, 64), F32),
            pltpu.VMEM((32, 80), F32),
            pltpu.VMEM((32, 80), F32),
            pltpu.SemaphoreType.DMA((6,)),
        ],
        compiler_params=params(8),
        cost_estimate=cost(32 * 128 * 64 * 80 * 2, 2 << 20),
        name="features",
    )(
        *kept(
            jnp.transpose(labels, (0, 2, 1)).reshape(512, 64),
            jnp.transpose(wall_dist, (0, 2, 1)).reshape(512, 64),
            jnp.transpose(conv_weight, (1, 2, 0)),
            jnp.transpose(down_weight, (0, 2, 1)),
            material_table,
            dist_weight[None],
        )
    )
    up_y = [(i, i + 1) for i in range(count_y - 1)]
    up_z = [(i, i + 1) for i in range(count_z - 1)]
    ylo = lax.ppermute(last, "sy", up_y)
    yhi = lax.ppermute(first, "sy", [(j, i) for i, j in up_y])
    band, pair, pair_t, table = pl.pallas_call(
        weight_kernel,
        out_shape=(
            shape((9, 256, 256), BF16),
            shape((128, 256), BF16),
            shape((256, 128), BF16),
            shape((80, 256), BF16),
        ),
        in_specs=[VMEM] * 4,
        out_specs=(VMEM,) * 4,
        compiler_params=params(8),
        cost_estimate=cost(27 * 256 * 16 * 256 * 2, 3 << 20),
        name="weights",
    )(*weights)
    ylo, yhi, band, pair, pair_t, table = lax.optimization_barrier(
        (ylo, yhi, band, pair, pair_t, table)
    )

    def whole(z):
        row = lax.broadcasted_iota(jnp.int32, (80, 80), 0)
        face = jnp.where(row == 64, ylo[z][None], features[z, :80])
        return jnp.where(row == 65, yhi[z][None], face)

    zlo = lax.ppermute(whole(31), "sz", up_z)
    zhi = lax.ppermute(whole(0), "sz", [(j, i) for i, j in up_z])
    embedded, slope, hidden, edge = pl.pallas_call(
        inner_kernel,
        out_shape=(
            shape((17, 2, 128, 256), BF16),
            pltpu.HBM((4, 256, 512), F32),
            shape((4, 256, 512), BF16),
            shape((2, 2, 256, 32), F32),
        ),
        in_specs=[VMEM] * 5,
        out_specs=(VMEM, HBM, VMEM, VMEM),
        scratch_shapes=[pltpu.VMEM((4, 256, 512), F32), pltpu.SemaphoreType.DMA((8,))],
        compiler_params=params(12),
        cost_estimate=cost(3 << 30, 10 << 20),
        name="inner",
    )(features, ylo, yhi, table, band)
    faces, edge_slope, hidden, coarse = pl.pallas_call(
        outer_kernel,
        out_shape=(
            shape((2, 128, 256), BF16),
            shape((256, 128), F32),
            pltpu.HBM((4, 256, 512), BF16),
            pltpu.HBM((1024, 256), BF16),
        ),
        in_specs=[VMEM] * 7,
        out_specs=(VMEM, VMEM, HBM, HBM),
        scratch_shapes=[
            pltpu.VMEM((512, 512), F32),
            pltpu.VMEM((2, 1024, 128), F32),
            pltpu.VMEM((4, 256, 512), BF16),
            pltpu.VMEM((1024, 256), BF16),
            pltpu.SemaphoreType.DMA((3,)),
        ],
        compiler_params=params(8),
        cost_estimate=cost(1 << 30, 4 << 20),
        name="outer",
    )(zlo, zhi, table, band, pair, edge, hidden)

    mix_weight, cotangent_rows, coarse = lax.optimization_barrier(
        (mix_weight, cotangent.reshape(mine, 256, width), coarse)
    )
    sent = lax.all_to_all(
        coarse.reshape(count_z, mine * 16, 256), "sz", split_axis=0, concat_axis=0, tiled=True
    )
    block = lambda *dims: pl.BlockSpec(dims, lambda c: (c,) + (0,) * (len(dims) - 1))
    shares = count_y // 2
    mix_specs = [
        pl.BlockSpec((count_z, 16, 256), lambda c: (0, c, 0)),
        block(1, width, width),
        block(1, width, 256),
    ]
    mix_t, cotangent_t = pl.pallas_call(
        turn_kernel,
        grid=(mine,),
        out_shape=(shape((mine, width, width), BF16), shape((mine, width, 256), BF16)),
        in_specs=[block(1, width, width), block(1, 256, width)],
        out_specs=(block(1, width, width), block(1, width, 256)),
        compiler_params=params(4),
        cost_estimate=cost(1 << 20, 2 << 20),
        name="turn",
    )(mix_weight, cotangent_rows)
    back = pl.pallas_call(
        mix_kernel,
        out_shape=pltpu.HBM((count_z, mine * 16, 256), BF16),
        in_specs=[VMEM] * 4,
        out_specs=HBM,
        scratch_shapes=[
            pltpu.VMEM((count_z, mine * 16, 256), BF16),
            pltpu.SemaphoreType.DMA((mine,)),
        ],
        compiler_params=params(8),
        cost_estimate=cost(mine * 2 * 2 * 256 * width * width, 2 << 20),
        name="mix",
    )(sent, mix_weight, cotangent_t, mix_t)
    coarse_grad = lax.all_to_all(back, "sz", split_axis=0, concat_axis=0, tiled=True)
    sent, back = lax.optimization_barrier((sent, back))
    mid, *mix_parts = pl.pallas_call(
        lambda *refs: mix_grad_kernel(1.0 / math.sqrt(8 * 32 * count_y), *refs),
        grid=(mine,),
        out_shape=[shape((mine, 256, width), BF16)]
        + [
            pltpu.HBM((mine, width // shares, width), BF16 if k else F32) for k in range(shares)
        ],
        in_specs=[pl.BlockSpec(memory_space=pltpu.SMEM)] + mix_specs,
        out_specs=[block(1, 256, width)] + [block(1, width // shares, width)] * shares,
        scratch_shapes=[pltpu.VMEM((width, width), F32)],
        compiler_params=params(8),
        cost_estimate=cost(mine * 2 * 2 * 256 * width * width, 3 << 20),
        name="mix_grad",
    )(lax.axis_index("sy")[None], sent, mix_weight, cotangent_t)
    mix_sum = mix_parts[0]
    moved = []
    for k, part in enumerate(mix_parts[1:], 1):
        moved.append(lax.ppermute(part, "sy", [(i, i ^ (2 * k)) for i in range(count_y)]))
    cells = 16 * 64 * count_y * 32 * count_z
    sums = pl.pallas_call(
        lambda *refs: backward_kernel(
            1.0 / math.sqrt(cells // 8), 1.0 / math.sqrt(cells), *refs
        ),
        out_shape=shape((128, 128), F32),
        in_specs=[VMEM, HBM, HBM, HBM] + [VMEM] * 4,
        out_specs=VMEM,
        scratch_shapes=[
            pltpu.VMEM((512, 512), F32),
            pltpu.VMEM((2, 1024, 128), F32),
            pltpu.VMEM((256, 2048), BF16),
            pltpu.VMEM((17, 2, 128, 256), BF16),
            pltpu.VMEM((4, 256, 512), F32),
            pltpu.VMEM((4, 256, 512), BF16),
            pltpu.SemaphoreType.DMA((3,)),
        ],
        compiler_params=params(12),
        cost_estimate=cost(4 << 30, 8 << 20),
        name="backward",
    )(
        coarse_grad.reshape(1024, 256),
        *kept(embedded, slope, hidden),
        pair,
        pair_t,
        faces,
        edge_slope,
    )
    *moved, sums = lax.optimization_barrier((*moved, sums))
    for part in moved:
        mix_sum = mix_sum + part.astype(F32)
    mine_last, other = jnp.split(mix_sum, 2, axis=1)
    other = lax.ppermute(other.astype(BF16), "sy", [(i, i ^ 1) for i in range(count_y)])
    mix_grad = mine_last + other.astype(F32)

    rounds = sum_rounds(count_y, count_z)
    for masks in rounds[:-1]:
        parts = [sums] + exchanged(sums, masks, count_y * count_z)
        sums = parts[0] + parts[1] if len(parts) == 2 else (parts[0] + parts[1]) + (parts[2] + parts[3])
    down_grad, conv_grad = pl.pallas_call(
        finish_kernel,
        out_shape=(shape((8, 16, 64), F32), shape((256, 27), F32)),
        in_specs=[VMEM] * 4,
        out_specs=(VMEM,) * 2,
        compiler_params=params(8),
        cost_estimate=cost(1 << 20, 1 << 18),
        name="finish",
    )(sums, *exchanged(sums, rounds[-1], count_y * count_z))
    down_grad = jnp.transpose(down_grad, (0, 2, 1))
    conv_grad = jnp.transpose(conv_grad.reshape(16, 16, 27), (2, 0, 1))
    return (mid.reshape(cotangent.shape), mix_grad, down_grad, conv_grad)


def solution(mesh):
    in_specs = (
        P(None, "sy", "sz"),
        P(None, "sy", "sz"),
        P(),
        P(),
        P(),
        P(),
        P("sz", None, None),
        P("sz", None, "sy", None),
    )
    out_specs = (P("sz", None, "sy", None), P("sz", "sy", None), P(), P())
    return jax.shard_map(
        per_device, mesh=mesh, in_specs=in_specs, out_specs=out_specs, check_vma=False
    )
```

```python
import math

import jax
import jax.numpy as jnp
from jax import lax
from jax.experimental import pallas as pl
from jax.experimental.pallas import tpu as pltpu
from jax.sharding import PartitionSpec as P

F32 = jnp.float32
BF16 = jnp.bfloat16
VMEM = pl.BlockSpec(memory_space=pltpu.VMEM)
HBM = pl.BlockSpec(memory_space=pltpu.HBM)
RUNS = ((64, 0, 32), (0, 32, 96))


def dot(a, b, ca, cb):
    return lax.dot_general(a, b, (((ca,), (cb,)), ((), ())), preferred_element_type=F32)


def iota(shape, dim):
    return lax.broadcasted_iota(jnp.int32, shape, dim)


def fetch(sources, targets, sem):
    copies = [pltpu.make_async_copy(a, b, sem.at[k]) for k, (a, b) in enumerate(zip(sources, targets))]
    for copy in copies:
        copy.start()
    return copies


def feature_kernel(
    lab_hbm, wd_hbm, conv_hbm, down_hbm, mat_hbm, dist_hbm,
    out_ref, first_ref, last_ref, conv_ref, down_ref, mat_ref, dist_ref,
    lab_s, wd_b, wd_s, first_s, last_s, sem,
):
    copies = fetch(
        (lab_hbm, wd_hbm, conv_hbm, down_hbm, mat_hbm, dist_hbm),
        (lab_s, wd_b, conv_ref, down_ref, mat_ref, dist_ref),
        sem,
    )
    row = iota((128, 64), 0)
    run, r = row // 32, row % 32
    y = jnp.where(run == 0, 2 * r, jnp.where(run == 1, 2 * r + 1, jnp.where(run == 2, 2 * r - 1, 2 * r + 2)))
    pick = (y == iota((128, 64), 1)).astype(BF16)
    copies[0].wait()
    copies[1].wait()
    wd_s[...] = wd_b[...].astype(F32)
    for z in range(out_ref.shape[0]):
        lab = lab_s[pl.ds(z, 16, stride=32), :]
        parts = [(lab == m).astype(F32).astype(BF16) for m in range(4)]
        parts.append(wd_s[pl.ds(z, 16, stride=32), :].astype(BF16))
        rows = dot(pick, jnp.concatenate(parts, axis=0), 1, 1)
        out_ref[z] = rows.astype(BF16)
        first_s[z : z + 1, :] = rows[0:1, :]
        last_s[z : z + 1, :] = rows[63:64, :]
    first_ref[...] = first_s[...].astype(BF16)
    last_ref[...] = last_s[...].astype(BF16)
    for copy in copies[2:]:
        copy.wait()


def weight_kernel(
    conv_ref, down_ref, mat_ref, dist_ref, band_ref, pair_ref, pair_t_ref, table_ref
):
    spread = (iota((256, 16), 0) % 16 == iota((256, 16), 1)).astype(BF16)
    taps = conv_ref[...].reshape(256, 27)
    repeat = (iota((27, 432), 0) == iota((27, 432), 1) // 16).astype(BF16)
    own = iota((256, 432), 0) % 16 == iota((256, 432), 1) % 16
    apart = jnp.where(own, dot(taps, repeat, 1, 0), 0.0).astype(BF16)
    gather = (iota((256, 256), 0) % 16 == iota((256, 256), 1) // 16).astype(BF16)
    wide = dot(gather, apart, 1, 0).astype(BF16)
    offset = iota((256, 256), 1) // 16 - iota((256, 256), 0) // 16 + 1
    for t in range(9):
        total = jnp.zeros((256, 256), F32)
        for tx in range(3):
            at = (tx * 9 + t) * 16
            tile = dot(wide[:, at : at + 16], spread, 1, 1)
            total = jnp.where(offset == tx, tile, total)
        band_ref[t] = total.astype(BF16)
    for bc in range(4):
        for x2 in range(2):
            for a in range(2):
                tap = down_ref[4 * a + bc]
                none = jnp.zeros_like(tap)
                at = 64 * bc + 32 * x2 + 16 * a
                pair_t_ref[at : at + 16, :] = jnp.concatenate([none, tap] if x2 else [tap, none], axis=1)
    pair_ref[...] = pair_t_ref[...].T
    lane_e = iota((16, 256), 1) // 16
    row_e = iota((16, 256), 0)
    mat = dot(mat_ref[...], spread, 1, 1)
    dist = dot(dist_ref[...], spread, 1, 1)
    for m in range(5):
        line = jnp.broadcast_to(mat[m : m + 1, :] if m < 4 else dist, (16, 256))
        table_ref[16 * m : 16 * m + 16, :] = jnp.where(lane_e == row_e, line, 0.0).astype(BF16)


def activate(acc):
    sigma = jax.nn.sigmoid(acc)
    return (acc * sigma).astype(BF16), sigma * (1.0 + acc * (1.0 - sigma))


def cells_of(emb_ref, b, c, ty, tz, half):
    run = RUNS[b][ty]
    q = (c + tz) // 2 + 8 * half
    return emb_ref[q : q + 8, (c + tz) % 2, run : run + 32, :].reshape(256, 256)


def inner_kernel(
    feat_ref, ylo_ref, yhi_ref, table_ref, band_ref, emb_ref, slope_hbm, hidden_ref, edge_ref,
    slope_ref, sem,
):
    table = table_ref[...]
    row = iota((128, 80), 0)
    emb_ref[0, 0] = jnp.zeros((128, 256), BF16)
    emb_ref[16, 1] = jnp.zeros((128, 256), BF16)
    ylo = ylo_ref[...].astype(F32)
    yhi = yhi_ref[...].astype(F32)
    for z in range(32):
        f = feat_ref[z].astype(F32)
        f = jnp.where(row == 64, ylo[z : z + 1, :], f)
        f = jnp.where(row == 127, yhi[z : z + 1, :], f)
        emb_ref[(z + 1) // 2, (z + 1) % 2] = dot(f.astype(BF16), table, 1, 0).astype(BF16)
    copies = []
    for bc in range(4):
        b, c = bc // 2, bc % 2
        for half in range(2):
            acc = None
            for ty in range(3):
                for tz in range(3):
                    part = dot(band_ref[3 * ty + tz], cells_of(emb_ref, b, c, ty, tz, half), 1, 1)
                    acc = part if acc is None else acc + part
            if half == 0 and c == 0:
                edge_ref[0, b] = acc[:, :32]
            if half == 1 and c == 1:
                edge_ref[1, b] = acc[:, 224:]
            at = slice(256 * half, 256 * half + 256)
            hidden_ref[bc, :, at], slope_ref[bc, :, at] = activate(acc)
            part = (bc, slice(None), pl.ds(256 * half, 256))
            copies.append(pltpu.make_async_copy(slope_ref.at[part], slope_hbm.at[part], sem.at[len(copies)]))
            copies[-1].start()
    for copy in copies:
        copy.wait()


def pair_rows(hidden_ref, pair):
    return jnp.concatenate([hidden_ref[bc, 64 * pair : 64 * pair + 64, :] for bc in range(4)], axis=0)


def outer_kernel(
    zlo_ref, zhi_ref, table_ref, band_ref, pair_ref, edge_ref, inner_ref,
    emb_ref, slope_ref, hidden_hbm, coarse_hbm, turn_a, turn_b, hidden_ref, coarse_ref, sem,
):
    table = table_ref[...]
    hidden_ref[...] = inner_ref[...]
    for side, face in enumerate((zlo_ref, zhi_ref)):
        f = face[...].astype(F32)
        runs = [f[:64], f[64:65], f[32:63], f[1:32], f[65:66]]
        plane = dot(jnp.concatenate(runs, axis=0).astype(BF16), table, 1, 0).astype(BF16)
        emb_ref[side] = plane
        for b in range(2):
            acc = edge_ref[side, b]
            for ty in range(3):
                run = RUNS[b][ty]
                acc = acc + dot(band_ref[3 * ty + 2 * side], plane[run : run + 32], 1, 1)
            at = slice(480 * side, 480 * side + 32)
            hidden_ref[2 * b + side, :, at], slope_ref[:, 64 * side + 32 * b : 64 * side + 32 * b + 32] = activate(acc)
    copies = [pltpu.make_async_copy(hidden_ref, hidden_hbm, sem.at[0])]
    copies[0].start()
    for pair in range(4):
        turn_a[128 * pair : 128 * pair + 128, :] = dot(pair_ref[...], pair_rows(hidden_ref, pair), 1, 0)
    for half in range(2):
        for z2 in range(16):
            pieces = [
                turn_a[64 * x2 : 64 * x2 + 64, 32 * z2 : 32 * z2 + 32]
                for x2 in range(4 * half, 4 * half + 4)
            ]
            turn_b[half, pl.ds(z2, 64, stride=16), :] = jnp.concatenate(pieces, axis=1)
        at = (slice(None), pl.ds(128 * half, 128))
        coarse_ref[at] = turn_b[half].astype(BF16)
        copies.append(pltpu.make_async_copy(coarse_ref.at[at], coarse_hbm.at[at], sem.at[1 + half]))
        copies[-1].start()
    for copy in copies:
        copy.wait()


def turn_kernel(mix_ref, cot_ref, mix_t_ref, cot_t_ref):
    mix_t_ref[0] = mix_ref[0].T
    cot_t_ref[0] = cot_ref[0].T


def mixed(coarse, mix, cot_t):
    pre = dot(mix, coarse, 1, 0)
    sigma = jax.nn.sigmoid(pre)
    grad = cot_t.astype(F32) * (sigma * (1.0 + pre * (1.0 - sigma)))
    return pre * sigma, grad.astype(BF16)


def mix_kernel(coarse_ref, mix_ref, cot_t_ref, mix_t_ref, grad_hbm, grad_ref, sem):
    copies = []
    for c in range(mix_ref.shape[0]):
        at = (slice(None), pl.ds(16 * c, 16), slice(None))
        _, grad = mixed(coarse_ref[at].reshape(-1, 256), mix_ref[c], cot_t_ref[c])
        part = dot(mix_t_ref[c], grad, 1, 0).astype(BF16)
        grad_ref[at] = part.reshape(-1, 16, 256)
        copies.append(pltpu.make_async_copy(grad_ref.at[at], grad_hbm.at[at], sem.at[c]))
        copies[-1].start()
    for copy in copies:
        copy.wait()


def mix_grad_kernel(scale, me_ref, coarse_ref, mix_ref, cot_t_ref, mid_ref, *more_refs):
    *share_refs, total_ref = more_refs
    coarse = coarse_ref[...].reshape(-1, 256)
    mid, grad = mixed(coarse, mix_ref[0], cot_t_ref[0])
    mid_ref[0] = mid.astype(BF16).T
    total_ref[...] = dot(grad, coarse, 1, 1) * scale
    rows = total_ref.shape[0] // (2 * len(share_refs))
    for place in range(2 * len(share_refs)):
        start = pl.multiple_of(jnp.bitwise_xor(me_ref[0], place) * rows, rows)
        at = place % 2 * rows
        share_ref = share_refs[place // 2]
        share_ref[0, at : at + rows, :] = total_ref[pl.ds(start, rows), :].astype(share_ref.dtype)


def fold(value, step):
    lanes = value.shape[-1]
    if lanes == 256:
        value = value[:, :128] + value[:, 128:]
    shift = 64
    while shift >= step:
        value = value + pltpu.roll(value, shift, 1)
        shift //= 2
    return value


def backward_kernel(
    down_scale, conv_scale, cgrad_ref, emb_hbm, slope_hbm, hidden_hbm, pair_ref, pair_t_ref, face_ref, edge_ref,
    out_ref, turn_a, turn_b, turned_pg, taps_ref, emb_in, slope_in, hidden_ref, sem,
):
    copies = [
        pltpu.make_async_copy(slope_hbm, slope_in, sem.at[0]),
        pltpu.make_async_copy(emb_hbm, emb_in, sem.at[1]),
        pltpu.make_async_copy(hidden_hbm, hidden_ref, sem.at[2]),
    ]
    copies[2].start()
    copies[0].start()
    for half in range(2):
        turn_b[half] = cgrad_ref[:, 128 * half : 128 * half + 128].astype(F32)
    for half in range(2):
        for quad in range(4):
            pieces = [turn_b[half, pl.ds(4 * quad + k, 64, stride=16), :] for k in range(4)]
            for k in range(4):
                x2 = 4 * half + k
                turn_a[64 * x2 : 64 * x2 + 64, 128 * quad : 128 * quad + 128] = jnp.concatenate(
                    [p[:, 32 * k : 32 * k + 32] for p in pieces], axis=1
                )
    copies[1].start()
    cg_t = turn_a[...].astype(BF16)
    pairs = [cg_t[128 * pair : 128 * pair + 128, :] for pair in range(4)]
    copies[2].wait()
    down = None
    for pair in range(4):
        part = dot(pairs[pair], pair_rows(hidden_ref, pair), 1, 1)
        down = part if down is None else down + part
    down = jnp.where(iota((64, 256), 1) // 32 % 2 == 0, down[:64], down[64:]) * down_scale
    left = down[:, :128] + pltpu.roll(down[:, :128], 96, 1)
    right = down[:, 128:] + pltpu.roll(down[:, 128:], 32, 1)
    out_ref[0:64, :] = jnp.where(iota((64, 128), 1) // 32 % 2 == 0, left, right)
    copies[0].wait()
    for pair in range(4):
        hgrad = dot(pair_t_ref[...], pairs[pair], 1, 0)
        at = slice(64 * pair, 64 * pair + 64)
        for bc in range(4):
            rows = hgrad[64 * bc : 64 * bc + 64]
            turned_pg[at, 512 * bc : 512 * bc + 512] = (rows * slope_in[bc, at, :]).astype(BF16)
            first = 480 * (bc % 2)
            low = 64 * (bc % 2) + 32 * (bc // 2)
            turned_pg[at, 512 * bc + first : 512 * bc + first + 32] = (rows[:, first : first + 32] * edge_ref[at, low : low + 32]).astype(BF16)
    copies[1].wait()
    lane_x = iota((16, 128), 1) // 16
    own = iota((64, 8, 128), 2) // 16 == iota((64, 8, 128), 1)
    for ty in range(3):
        for tz in range(3):
            pieces = []
            for bc in range(4):
                b, c = bc // 2, bc % 2
                run = RUNS[b][ty]
                for half in range(2):
                    rows = cells_of(emb_in, b, c, ty, tz, half)
                    if c + tz == 0 and half == 0:
                        rows = jnp.concatenate([face_ref[0, run : run + 32, :], rows[32:]], axis=0)
                    if c + tz == 3 and half == 1:
                        rows = jnp.concatenate([rows[:224], face_ref[1, run : run + 32, :]], axis=0)
                    pieces.append(rows)
            acc = dot(turned_pg[...], jnp.concatenate(pieces, axis=0), 1, 0)
            for tx in range(3):
                total = None
                for side in range(2):
                    half = jnp.zeros((16, 128), F32)
                    for x in range(16):
                        lane = x + tx - 1 - 8 * side
                        if 0 <= lane < 8:
                            part = acc[16 * x : 16 * x + 16, 128 * side : 128 * side + 128]
                            half = jnp.where(lane_x == lane, part, half)
                    total = half if total is None else total + half
                tap = 9 * tx + 3 * ty + tz
                for half in range(2):
                    at = 8 * (32 * half + tap)
                    taps_ref[at : at + 8, :] = total[8 * half : 8 * half + 8]
    for half in range(2):
        taps_ref[256 * half + 216 : 256 * half + 256, :] = jnp.zeros((40, 128), F32)
    total = fold(taps_ref[...], 16) * conv_scale
    out_ref[64:128, :] = jnp.sum(jnp.where(own, total.reshape(64, 8, 128), 0.0), axis=1)


def finish_kernel(a_ref, b_ref, c_ref, d_ref, down_ref, conv_ref):
    total = (a_ref[...] + b_ref[...]) + (c_ref[...] + d_ref[...])
    down = total[:64].T
    for a in range(2):
        for bc in range(4):
            at = (2 * (2 * (bc % 2) + bc // 2) + a) * 16
            down_ref[4 * a + bc] = down[at : at + 16, :]
    for half in range(2):
        conv = total[64 + 32 * half : 96 + 32 * half].T
        conv_ref[128 * half : 128 * half + 128, :] = conv[:, :27]


def kept(*values):
    return [pltpu.with_memory_space_constraint(v, pltpu.HBM) for v in values]


def params(mib):
    return pltpu.CompilerParams(vmem_limit_bytes=mib << 20)


def cost(flops, nbytes):
    return pl.CostEstimate(flops=flops, bytes_accessed=nbytes, transcendentals=0)


def shape(dims, dtype):
    return jax.ShapeDtypeStruct(dims, dtype)


def sum_rounds(count_y, count_z):
    in_z = [1 << k for k in range(count_z.bit_length() - 1)]
    in_y = [count_z << k for k in range(count_y.bit_length() - 1)]
    order = in_z[:1] + in_z[1:2] + in_y[:1] + in_z[2:] + in_y[1:]
    rounds, order = ([order[:1]] if len(order) % 2 else []), order[len(order) % 2 :]
    return rounds + [order[k : k + 2] for k in range(0, len(order), 2)]


def exchanged(value, masks, count):
    masks = list(masks) + [masks[0] ^ masks[1]] if len(masks) == 2 else masks
    return [lax.ppermute(value, ("sy", "sz"), [(i, i ^ m) for i in range(count)]) for m in masks]


def per_device(
    labels, wall_dist, material_table, dist_weight, conv_weight, down_weight, mix_weight, cotangent
):
    count_y = lax.axis_size("sy")
    count_z = lax.axis_size("sz")
    mine = 64 // count_z
    width = mix_weight.shape[1]
    features, first, last, *weights = pl.pallas_call(
        feature_kernel,
        out_shape=(
            shape((32, 128, 80), BF16),
            shape((32, 80), BF16),
            shape((32, 80), BF16),
            shape((16, 16, 27), BF16),
            shape((8, 16, 64), BF16),
            shape((4, 16), BF16),
            shape((1, 16), BF16),
        ),
        in_specs=[HBM] * 6,
        out_specs=(VMEM,) * 7,
        scratch_shapes=[
            pltpu.VMEM((512, 64), jnp.int32),
            pltpu.VMEM((512, 64), BF16),
            pltpu.VMEM((512, 64), F32),
            pltpu.VMEM((32, 80), F32),
            pltpu.VMEM((32, 80), F32),
            pltpu.SemaphoreType.DMA((6,)),
        ],
        compiler_params=params(8),
        cost_estimate=cost(32 * 128 * 64 * 80 * 2, 2 << 20),
        name="features",
    )(
        *kept(
            jnp.transpose(labels, (0, 2, 1)).reshape(512, 64),
            jnp.transpose(wall_dist, (0, 2, 1)).reshape(512, 64),
            jnp.transpose(conv_weight, (1, 2, 0)),
            jnp.transpose(down_weight, (0, 2, 1)),
            material_table,
            dist_weight[None],
        )
    )
    up_y = [(i, i + 1) for i in range(count_y - 1)]
    up_z = [(i, i + 1) for i in range(count_z - 1)]
    ylo = lax.ppermute(last, "sy", up_y)
    yhi = lax.ppermute(first, "sy", [(j, i) for i, j in up_y])
    band, pair, pair_t, table = pl.pallas_call(
        weight_kernel,
        out_shape=(
            shape((9, 256, 256), BF16),
            shape((128, 256), BF16),
            shape((256, 128), BF16),
            shape((80, 256), BF16),
        ),
        in_specs=[VMEM] * 4,
        out_specs=(VMEM,) * 4,
        compiler_params=params(8),
        cost_estimate=cost(27 * 256 * 16 * 256 * 2, 3 << 20),
        name="weights",
    )(*weights)
    ylo, yhi, band, pair, pair_t, table = lax.optimization_barrier(
        (ylo, yhi, band, pair, pair_t, table)
    )

    def whole(z):
        row = lax.broadcasted_iota(jnp.int32, (80, 80), 0)
        face = jnp.where(row == 64, ylo[z][None], features[z, :80])
        return jnp.where(row == 65, yhi[z][None], face)

    zlo = lax.ppermute(whole(31), "sz", up_z)
    zhi = lax.ppermute(whole(0), "sz", [(j, i) for i, j in up_z])
    embedded, slope, hidden, edge = pl.pallas_call(
        inner_kernel,
        out_shape=(
            shape((17, 2, 128, 256), BF16),
            pltpu.HBM((4, 256, 512), F32),
            shape((4, 256, 512), BF16),
            shape((2, 2, 256, 32), F32),
        ),
        in_specs=[VMEM] * 5,
        out_specs=(VMEM, HBM, VMEM, VMEM),
        scratch_shapes=[pltpu.VMEM((4, 256, 512), F32), pltpu.SemaphoreType.DMA((8,))],
        compiler_params=params(12),
        cost_estimate=cost(3 << 30, 10 << 20),
        name="inner",
    )(features, ylo, yhi, table, band)
    faces, edge_slope, hidden, coarse = pl.pallas_call(
        outer_kernel,
        out_shape=(
            shape((2, 128, 256), BF16),
            shape((256, 128), F32),
            pltpu.HBM((4, 256, 512), BF16),
            pltpu.HBM((1024, 256), BF16),
        ),
        in_specs=[VMEM] * 7,
        out_specs=(VMEM, VMEM, HBM, HBM),
        scratch_shapes=[
            pltpu.VMEM((512, 512), F32),
            pltpu.VMEM((2, 1024, 128), F32),
            pltpu.VMEM((4, 256, 512), BF16),
            pltpu.VMEM((1024, 256), BF16),
            pltpu.SemaphoreType.DMA((3,)),
        ],
        compiler_params=params(8),
        cost_estimate=cost(1 << 30, 4 << 20),
        name="outer",
    )(zlo, zhi, table, band, pair, edge, hidden)

    mix_weight, cotangent_rows, coarse = lax.optimization_barrier(
        (mix_weight, cotangent.reshape(mine, 256, width), coarse)
    )
    sent = lax.all_to_all(
        coarse.reshape(count_z, mine * 16, 256), "sz", split_axis=0, concat_axis=0, tiled=True
    )
    block = lambda *dims: pl.BlockSpec(dims, lambda c: (c,) + (0,) * (len(dims) - 1))
    shares = count_y // 2
    mix_specs = [
        pl.BlockSpec((count_z, 16, 256), lambda c: (0, c, 0)),
        block(1, width, width),
        block(1, width, 256),
    ]
    mix_t, cotangent_t = pl.pallas_call(
        turn_kernel,
        grid=(mine,),
        out_shape=(shape((mine, width, width), BF16), shape((mine, width, 256), BF16)),
        in_specs=[block(1, width, width), block(1, 256, width)],
        out_specs=(block(1, width, width), block(1, width, 256)),
        compiler_params=params(4),
        cost_estimate=cost(1 << 20, 2 << 20),
        name="turn",
    )(mix_weight, cotangent_rows)
    back = pl.pallas_call(
        mix_kernel,
        out_shape=pltpu.HBM((count_z, mine * 16, 256), BF16),
        in_specs=[VMEM] * 4,
        out_specs=HBM,
        scratch_shapes=[
            pltpu.VMEM((count_z, mine * 16, 256), BF16),
            pltpu.SemaphoreType.DMA((mine,)),
        ],
        compiler_params=params(8),
        cost_estimate=cost(mine * 2 * 2 * 256 * width * width, 2 << 20),
        name="mix",
    )(sent, mix_weight, cotangent_t, mix_t)
    coarse_grad = lax.all_to_all(back, "sz", split_axis=0, concat_axis=0, tiled=True)
    sent, back = lax.optimization_barrier((sent, back))
    mid, *mix_parts = pl.pallas_call(
        lambda *refs: mix_grad_kernel(1.0 / math.sqrt(8 * 32 * count_y), *refs),
        grid=(mine,),
        out_shape=[shape((mine, 256, width), BF16)]
        + [
            pltpu.HBM((mine, width // shares, width), BF16 if k else F32) for k in range(shares)
        ],
        in_specs=[pl.BlockSpec(memory_space=pltpu.SMEM)] + mix_specs,
        out_specs=[block(1, 256, width)] + [block(1, width // shares, width)] * shares,
        scratch_shapes=[pltpu.VMEM((width, width), F32)],
        compiler_params=params(8),
        cost_estimate=cost(mine * 2 * 2 * 256 * width * width, 3 << 20),
        name="mix_grad",
    )(lax.axis_index("sy")[None], sent, mix_weight, cotangent_t)
    mix_sum = mix_parts[0]
    moved = []
    for k, part in enumerate(mix_parts[1:], 1):
        moved.append(lax.ppermute(part, "sy", [(i, i ^ (2 * k)) for i in range(count_y)]))
    cells = 16 * 64 * count_y * 32 * count_z
    sums = pl.pallas_call(
        lambda *refs: backward_kernel(
            1.0 / math.sqrt(cells // 8), 1.0 / math.sqrt(cells), *refs
        ),
        out_shape=shape((128, 128), F32),
        in_specs=[VMEM, HBM, HBM, HBM] + [VMEM] * 4,
        out_specs=VMEM,
        scratch_shapes=[
            pltpu.VMEM((512, 512), F32),
            pltpu.VMEM((2, 1024, 128), F32),
            pltpu.VMEM((256, 2048), BF16),
            pltpu.VMEM((512, 128), F32),
            pltpu.VMEM((17, 2, 128, 256), BF16),
            pltpu.VMEM((4, 256, 512), F32),
            pltpu.VMEM((4, 256, 512), BF16),
            pltpu.SemaphoreType.DMA((3,)),
        ],
        compiler_params=params(12),
        cost_estimate=cost(4 << 30, 8 << 20),
        name="backward",
    )(
        coarse_grad.reshape(1024, 256),
        *kept(embedded, slope, hidden),
        pair,
        pair_t,
        faces,
        edge_slope,
    )
    *moved, sums = lax.optimization_barrier((*moved, sums))
    for part in moved:
        mix_sum = mix_sum + part.astype(F32)
    mine_last, other = jnp.split(mix_sum, 2, axis=1)
    other = lax.ppermute(other.astype(BF16), "sy", [(i, i ^ 1) for i in range(count_y)])
    mix_grad = mine_last + other.astype(F32)

    rounds = sum_rounds(count_y, count_z)
    for masks in rounds[:-1]:
        parts = [sums] + exchanged(sums, masks, count_y * count_z)
        sums = parts[0] + parts[1] if len(parts) == 2 else (parts[0] + parts[1]) + (parts[2] + parts[3])
    down_grad, conv_grad = pl.pallas_call(
        finish_kernel,
        out_shape=(shape((8, 16, 64), F32), shape((256, 27), F32)),
        in_specs=[VMEM] * 4,
        out_specs=(VMEM,) * 2,
        compiler_params=params(8),
        cost_estimate=cost(1 << 20, 1 << 18),
        name="finish",
    )(sums, *exchanged(sums, rounds[-1], count_y * count_z))
    down_grad = jnp.transpose(down_grad, (0, 2, 1))
    conv_grad = jnp.transpose(conv_grad.reshape(16, 16, 27), (2, 0, 1))
    return (mid.reshape(cotangent.shape), mix_grad, down_grad, conv_grad)


def solution(mesh):
    in_specs = (
        P(None, "sy", "sz"),
        P(None, "sy", "sz"),
        P(),
        P(),
        P(),
        P(),
        P("sz", None, None),
        P("sz", None, "sy", None),
    )
    out_specs = (P("sz", None, "sy", None), P("sz", "sy", None), P(), P())
    return jax.shard_map(
        per_device, mesh=mesh, in_specs=in_specs, out_specs=out_specs, check_vma=False
    )
```

```python
import math

import jax
import jax.numpy as jnp
from jax import lax
from jax.experimental import pallas as pl
from jax.experimental.pallas import tpu as pltpu
from jax.sharding import PartitionSpec as P

F32 = jnp.float32
BF16 = jnp.bfloat16
VMEM = pl.BlockSpec(memory_space=pltpu.VMEM)
HBM = pl.BlockSpec(memory_space=pltpu.HBM)
RUNS = ((64, 0, 32), (0, 32, 96))


def dot(a, b, ca, cb):
    return lax.dot_general(a, b, (((ca,), (cb,)), ((), ())), preferred_element_type=F32)


def iota(shape, dim):
    return lax.broadcasted_iota(jnp.int32, shape, dim)


def fetch(sources, targets, sem):
    copies = [pltpu.make_async_copy(a, b, sem.at[k]) for k, (a, b) in enumerate(zip(sources, targets))]
    for copy in copies:
        copy.start()
    return copies


def feature_kernel(
    lab_hbm, wd_hbm, conv_hbm, down_hbm, mat_hbm, dist_hbm,
    out_ref, first_ref, last_ref, conv_ref, down_ref, mat_ref, dist_ref,
    lab_s, wd_b, wd_s, first_s, last_s, sem,
):
    copies = fetch(
        (lab_hbm, wd_hbm, conv_hbm, down_hbm, mat_hbm, dist_hbm),
        (lab_s, wd_b, conv_ref, down_ref, mat_ref, dist_ref),
        sem,
    )
    row = iota((128, 64), 0)
    run, r = row // 32, row % 32
    y = jnp.where(run == 0, 2 * r, jnp.where(run == 1, 2 * r + 1, jnp.where(run == 2, 2 * r - 1, 2 * r + 2)))
    pick = (y == iota((128, 64), 1)).astype(BF16)
    copies[0].wait()
    copies[1].wait()
    wd_s[...] = wd_b[...].astype(F32)
    for z in range(out_ref.shape[0]):
        lab = lab_s[pl.ds(z, 16, stride=32), :]
        parts = [(lab == m).astype(F32).astype(BF16) for m in range(4)]
        parts.append(wd_s[pl.ds(z, 16, stride=32), :].astype(BF16))
        rows = dot(pick, jnp.concatenate(parts, axis=0), 1, 1)
        out_ref[z] = rows.astype(BF16)
        first_s[z : z + 1, :] = rows[0:1, :]
        last_s[z : z + 1, :] = rows[63:64, :]
    first_ref[...] = first_s[...].astype(BF16)
    last_ref[...] = last_s[...].astype(BF16)
    for copy in copies[2:]:
        copy.wait()


def weight_kernel(
    conv_ref, down_ref, mat_ref, dist_ref, band_ref, pair_ref, pair_t_ref, table_ref
):
    spread = (iota((256, 16), 0) % 16 == iota((256, 16), 1)).astype(BF16)
    taps = conv_ref[...].reshape(256, 27)
    repeat = (iota((27, 432), 0) == iota((27, 432), 1) // 16).astype(BF16)
    own = iota((256, 432), 0) % 16 == iota((256, 432), 1) % 16
    apart = jnp.where(own, dot(taps, repeat, 1, 0), 0.0).astype(BF16)
    gather = (iota((256, 256), 0) % 16 == iota((256, 256), 1) // 16).astype(BF16)
    wide = dot(gather, apart, 1, 0).astype(BF16)
    offset = iota((256, 256), 1) // 16 - iota((256, 256), 0) // 16 + 1
    for t in range(9):
        total = jnp.zeros((256, 256), F32)
        for tx in range(3):
            at = (tx * 9 + t) * 16
            tile = dot(wide[:, at : at + 16], spread, 1, 1)
            total = jnp.where(offset == tx, tile, total)
        band_ref[t] = total.astype(BF16)
    for bc in range(4):
        for x2 in range(2):
            for a in range(2):
                tap = down_ref[4 * a + bc]
                none = jnp.zeros_like(tap)
                at = 64 * bc + 32 * x2 + 16 * a
                pair_t_ref[at : at + 16, :] = jnp.concatenate([none, tap] if x2 else [tap, none], axis=1)
    pair_ref[...] = pair_t_ref[...].T
    lane_e = iota((16, 256), 1) // 16
    row_e = iota((16, 256), 0)
    mat = dot(mat_ref[...], spread, 1, 1)
    dist = dot(dist_ref[...], spread, 1, 1)
    for m in range(5):
        line = jnp.broadcast_to(mat[m : m + 1, :] if m < 4 else dist, (16, 256))
        table_ref[16 * m : 16 * m + 16, :] = jnp.where(lane_e == row_e, line, 0.0).astype(BF16)


def activate(acc):
    sigma = jax.nn.sigmoid(acc)
    return (acc * sigma).astype(BF16), sigma * (1.0 + acc * (1.0 - sigma))


def cells_of(emb_ref, b, c, ty, tz, half):
    run = RUNS[b][ty]
    q = (c + tz) // 2 + 8 * half
    return emb_ref[q : q + 8, (c + tz) % 2, run : run + 32, :].reshape(256, 256)


def inner_kernel(
    feat_ref, ylo_ref, yhi_ref, table_ref, band_ref, emb_ref, slope_hbm, hidden_ref, edge_ref,
    slope_ref, sem,
):
    table = table_ref[...]
    row = iota((128, 80), 0)
    emb_ref[0, 0] = jnp.zeros((128, 256), BF16)
    emb_ref[16, 1] = jnp.zeros((128, 256), BF16)
    ylo = ylo_ref[...].astype(F32)
    yhi = yhi_ref[...].astype(F32)
    for z in range(32):
        f = feat_ref[z].astype(F32)
        f = jnp.where(row == 64, ylo[z : z + 1, :], f)
        f = jnp.where(row == 127, yhi[z : z + 1, :], f)
        emb_ref[(z + 1) // 2, (z + 1) % 2] = dot(f.astype(BF16), table, 1, 0).astype(BF16)
    copies = []
    for bc in range(4):
        b, c = bc // 2, bc % 2
        for half in range(2):
            acc = None
            for ty in range(3):
                for tz in range(3):
                    part = dot(band_ref[3 * ty + tz], cells_of(emb_ref, b, c, ty, tz, half), 1, 1)
                    acc = part if acc is None else acc + part
            if half == 0 and c == 0:
                edge_ref[0, b] = acc[:, :32]
            if half == 1 and c == 1:
                edge_ref[1, b] = acc[:, 224:]
            at = slice(256 * half, 256 * half + 256)
            hidden_ref[bc, :, at], slope_ref[bc, :, at] = activate(acc)
            part = (bc, slice(None), pl.ds(256 * half, 256))
            copies.append(pltpu.make_async_copy(slope_ref.at[part], slope_hbm.at[part], sem.at[len(copies)]))
            copies[-1].start()
    for copy in copies:
        copy.wait()


def pair_rows(hidden_ref, pair):
    return jnp.concatenate([hidden_ref[bc, 64 * pair : 64 * pair + 64, :] for bc in range(4)], axis=0)


def outer_kernel(
    zlo_ref, zhi_ref, table_ref, band_ref, pair_ref, edge_ref, inner_ref,
    emb_ref, slope_ref, hidden_hbm, coarse_hbm, turn_a, turn_b, hidden_ref, coarse_ref, sem,
):
    table = table_ref[...]
    hidden_ref[...] = inner_ref[...]
    for side, face in enumerate((zlo_ref, zhi_ref)):
        f = face[...].astype(F32)
        runs = [f[:64], f[64:65], f[32:63], f[1:32], f[65:66]]
        plane = dot(jnp.concatenate(runs, axis=0).astype(BF16), table, 1, 0).astype(BF16)
        emb_ref[side] = plane
        for b in range(2):
            acc = edge_ref[side, b]
            for ty in range(3):
                run = RUNS[b][ty]
                acc = acc + dot(band_ref[3 * ty + 2 * side], plane[run : run + 32], 1, 1)
            at = slice(480 * side, 480 * side + 32)
            hidden_ref[2 * b + side, :, at], slope_ref[:, 64 * side + 32 * b : 64 * side + 32 * b + 32] = activate(acc)
    copies = [pltpu.make_async_copy(hidden_ref, hidden_hbm, sem.at[0])]
    copies[0].start()
    for pair in range(4):
        turn_a[128 * pair : 128 * pair + 128, :] = dot(pair_ref[...], pair_rows(hidden_ref, pair), 1, 0)
    for half in range(2):
        for z2 in range(16):
            pieces = [
                turn_a[64 * x2 : 64 * x2 + 64, 32 * z2 : 32 * z2 + 32]
                for x2 in range(4 * half, 4 * half + 4)
            ]
            turn_b[half, pl.ds(z2, 64, stride=16), :] = jnp.concatenate(pieces, axis=1)
        at = (slice(None), pl.ds(128 * half, 128))
        coarse_ref[at] = turn_b[half].astype(BF16)
        copies.append(pltpu.make_async_copy(coarse_ref.at[at], coarse_hbm.at[at], sem.at[1 + half]))
        copies[-1].start()
    for copy in copies:
        copy.wait()


def turn_kernel(mix_ref, cot_ref, mix_t_ref, cot_t_ref):
    mix_t_ref[0] = mix_ref[0].T
    cot_t_ref[0] = cot_ref[0].T


def mixed(coarse, mix, cot_t):
    pre = dot(mix, coarse, 1, 0)
    sigma = jax.nn.sigmoid(pre)
    grad = cot_t.astype(F32) * (sigma * (1.0 + pre * (1.0 - sigma)))
    return pre * sigma, grad.astype(BF16)


def mix_kernel(coarse_ref, mix_ref, cot_t_ref, mix_t_ref, grad_hbm, grad_ref, sem):
    copies = []
    for c in range(mix_ref.shape[0]):
        at = (slice(None), pl.ds(16 * c, 16), slice(None))
        _, grad = mixed(coarse_ref[at].reshape(-1, 256), mix_ref[c], cot_t_ref[c])
        part = dot(mix_t_ref[c], grad, 1, 0).astype(BF16)
        grad_ref[at] = part.reshape(-1, 16, 256)
        copies.append(pltpu.make_async_copy(grad_ref.at[at], grad_hbm.at[at], sem.at[c]))
        copies[-1].start()
    for copy in copies:
        copy.wait()


def mix_grad_kernel(scale, me_ref, coarse_ref, mix_ref, cot_t_ref, mid_ref, *more_refs):
    *share_refs, total_ref = more_refs
    coarse = coarse_ref[...].reshape(-1, 256)
    mid, grad = mixed(coarse, mix_ref[0], cot_t_ref[0])
    mid_ref[0] = mid.astype(BF16).T
    total_ref[...] = dot(grad, coarse, 1, 1) * scale
    rows = total_ref.shape[0] // (2 * len(share_refs))
    for place in range(2 * len(share_refs)):
        start = pl.multiple_of(jnp.bitwise_xor(me_ref[0], place) * rows, rows)
        at = place % 2 * rows
        share_ref = share_refs[place // 2]
        share_ref[0, at : at + rows, :] = total_ref[pl.ds(start, rows), :].astype(share_ref.dtype)


def fold(value, step):
    lanes = value.shape[-1]
    if lanes == 256:
        value = value[:, :128] + value[:, 128:]
    shift = 64
    while shift >= step:
        value = value + pltpu.roll(value, shift, 1)
        shift //= 2
    return value


def backward_kernel(
    down_scale, conv_scale, cgrad_ref, emb_hbm, slope_hbm, hidden_hbm, pair_ref, pair_t_ref, face_ref, edge_ref,
    out_ref, turn_a, turn_b, turned_pg, taps_ref, emb_in, slope_in, hidden_ref, sem,
):
    copies = [
        pltpu.make_async_copy(slope_hbm, slope_in, sem.at[0]),
        pltpu.make_async_copy(emb_hbm, emb_in, sem.at[1]),
        pltpu.make_async_copy(hidden_hbm, hidden_ref, sem.at[2]),
    ]
    copies[2].start()
    copies[0].start()
    for half in range(2):
        turn_b[half] = cgrad_ref[:, 128 * half : 128 * half + 128].astype(F32)
    for half in range(2):
        for quad in range(4):
            pieces = [turn_b[half, pl.ds(4 * quad + k, 64, stride=16), :] for k in range(4)]
            for k in range(4):
                x2 = 4 * half + k
                turn_a[64 * x2 : 64 * x2 + 64, 128 * quad : 128 * quad + 128] = jnp.concatenate(
                    [p[:, 32 * k : 32 * k + 32] for p in pieces], axis=1
                )
    copies[1].start()
    cg_t = turn_a[...].astype(BF16)
    pairs = [cg_t[128 * pair : 128 * pair + 128, :] for pair in range(4)]
    copies[2].wait()
    down = None
    for pair in range(4):
        part = dot(pairs[pair], pair_rows(hidden_ref, pair), 1, 1)
        down = part if down is None else down + part
    down = jnp.where(iota((64, 256), 1) // 32 % 2 == 0, down[:64], down[64:]) * down_scale
    left = down[:, :128] + pltpu.roll(down[:, :128], 96, 1)
    right = down[:, 128:] + pltpu.roll(down[:, 128:], 32, 1)
    out_ref[0:64, :] = jnp.where(iota((64, 128), 1) // 32 % 2 == 0, left, right)
    copies[0].wait()
    for pair in range(4):
        hgrad = dot(pair_t_ref[...], pairs[pair], 1, 0)
        at = slice(64 * pair, 64 * pair + 64)
        for bc in range(4):
            rows = hgrad[64 * bc : 64 * bc + 64]
            turned_pg[at, 512 * bc : 512 * bc + 512] = (rows * slope_in[bc, at, :]).astype(BF16)
            first = 480 * (bc % 2)
            low = 64 * (bc % 2) + 32 * (bc // 2)
            turned_pg[at, 512 * bc + first : 512 * bc + first + 32] = (rows[:, first : first + 32] * edge_ref[at, low : low + 32]).astype(BF16)
    copies[1].wait()
    lane_x = iota((16, 128), 1) // 16
    own = iota((64, 8, 128), 2) // 16 == iota((64, 8, 128), 1)
    for ty in range(3):
        for tz in range(3):
            pieces = []
            for bc in range(4):
                b, c = bc // 2, bc % 2
                run = RUNS[b][ty]
                for half in range(2):
                    rows = cells_of(emb_in, b, c, ty, tz, half)
                    if c + tz == 0 and half == 0:
                        rows = jnp.concatenate([face_ref[0, run : run + 32, :], rows[32:]], axis=0)
                    if c + tz == 3 and half == 1:
                        rows = jnp.concatenate([rows[:224], face_ref[1, run : run + 32, :]], axis=0)
                    pieces.append(rows)
            acc = dot(turned_pg[...], jnp.concatenate(pieces, axis=0), 1, 0)
            for tx in range(3):
                total = None
                for side in range(2):
                    half = jnp.zeros((16, 128), F32)
                    for x in range(16):
                        lane = x + tx - 1 - 8 * side
                        if 0 <= lane < 8:
                            part = acc[16 * x : 16 * x + 16, 128 * side : 128 * side + 128]
                            half = jnp.where(lane_x == lane, part, half)
                    total = half if total is None else total + half
                tap = 9 * tx + 3 * ty + tz
                for half in range(2):
                    at = 8 * (32 * half + tap)
                    taps_ref[at : at + 8, :] = total[8 * half : 8 * half + 8]
    for half in range(2):
        taps_ref[256 * half + 216 : 256 * half + 256, :] = jnp.zeros((40, 128), F32)
    total = fold(taps_ref[...], 16) * conv_scale
    out_ref[64:128, :] = jnp.sum(jnp.where(own, total.reshape(64, 8, 128), 0.0), axis=1)


def finish_kernel(a_ref, b_ref, c_ref, d_ref, down_ref, conv_ref):
    total = (a_ref[...] + b_ref[...]) + (c_ref[...] + d_ref[...])
    down = total[:64].T
    for a in range(2):
        for bc in range(4):
            at = (2 * (2 * (bc % 2) + bc // 2) + a) * 16
            down_ref[4 * a + bc] = down[at : at + 16, :]
    for half in range(2):
        conv = total[64 + 32 * half : 96 + 32 * half].T
        conv_ref[128 * half : 128 * half + 128, :] = conv[:, :27]


def kept(*values):
    return [pltpu.with_memory_space_constraint(v, pltpu.HBM) for v in values]


def params(mib):
    return pltpu.CompilerParams(vmem_limit_bytes=mib << 20)


def cost(flops, nbytes):
    return pl.CostEstimate(flops=flops, bytes_accessed=nbytes, transcendentals=0)


def shape(dims, dtype):
    return jax.ShapeDtypeStruct(dims, dtype)


def sum_rounds(count_y, count_z):
    in_z = [1 << k for k in range(count_z.bit_length() - 1)]
    in_y = [count_z << k for k in range(count_y.bit_length() - 1)]
    order = in_z[:1] + in_z[2:] + in_y[1:] + in_z[1:2] + in_y[:1]
    rounds, order = ([order[:1]] if len(order) % 2 else []), order[len(order) % 2 :]
    return rounds + [order[k : k + 2] for k in range(0, len(order), 2)]


def exchanged(value, masks, count):
    masks = list(masks) + [masks[0] ^ masks[1]] if len(masks) == 2 else masks
    return [lax.ppermute(value, ("sy", "sz"), [(i, i ^ m) for i in range(count)]) for m in masks]


def per_device(
    labels, wall_dist, material_table, dist_weight, conv_weight, down_weight, mix_weight, cotangent
):
    count_y = lax.axis_size("sy")
    count_z = lax.axis_size("sz")
    mine = 64 // count_z
    width = mix_weight.shape[1]
    features, first, last, *weights = pl.pallas_call(
        feature_kernel,
        out_shape=(
            shape((32, 128, 80), BF16),
            shape((32, 80), BF16),
            shape((32, 80), BF16),
            shape((16, 16, 27), BF16),
            shape((8, 16, 64), BF16),
            shape((4, 16), BF16),
            shape((1, 16), BF16),
        ),
        in_specs=[HBM] * 6,
        out_specs=(VMEM,) * 7,
        scratch_shapes=[
            pltpu.VMEM((512, 64), jnp.int32),
            pltpu.VMEM((512, 64), BF16),
            pltpu.VMEM((512, 64), F32),
            pltpu.VMEM((32, 80), F32),
            pltpu.VMEM((32, 80), F32),
            pltpu.SemaphoreType.DMA((6,)),
        ],
        compiler_params=params(8),
        cost_estimate=cost(32 * 128 * 64 * 80 * 2, 2 << 20),
        name="features",
    )(
        *kept(
            jnp.transpose(labels, (0, 2, 1)).reshape(512, 64),
            jnp.transpose(wall_dist, (0, 2, 1)).reshape(512, 64),
            jnp.transpose(conv_weight, (1, 2, 0)),
            jnp.transpose(down_weight, (0, 2, 1)),
            material_table,
            dist_weight[None],
        )
    )
    up_y = [(i, i + 1) for i in range(count_y - 1)]
    up_z = [(i, i + 1) for i in range(count_z - 1)]
    ylo = lax.ppermute(last, "sy", up_y)
    yhi = lax.ppermute(first, "sy", [(j, i) for i, j in up_y])
    band, pair, pair_t, table = pl.pallas_call(
        weight_kernel,
        out_shape=(
            shape((9, 256, 256), BF16),
            shape((128, 256), BF16),
            shape((256, 128), BF16),
            shape((80, 256), BF16),
        ),
        in_specs=[VMEM] * 4,
        out_specs=(VMEM,) * 4,
        compiler_params=params(8),
        cost_estimate=cost(27 * 256 * 16 * 256 * 2, 3 << 20),
        name="weights",
    )(*weights)
    ylo, yhi, band, pair, pair_t, table = lax.optimization_barrier(
        (ylo, yhi, band, pair, pair_t, table)
    )

    def whole(z):
        row = lax.broadcasted_iota(jnp.int32, (80, 80), 0)
        face = jnp.where(row == 64, ylo[z][None], features[z, :80])
        return jnp.where(row == 65, yhi[z][None], face)

    zlo = lax.ppermute(whole(31), "sz", up_z)
    zhi = lax.ppermute(whole(0), "sz", [(j, i) for i, j in up_z])
    embedded, slope, hidden, edge = pl.pallas_call(
        inner_kernel,
        out_shape=(
            shape((17, 2, 128, 256), BF16),
            pltpu.HBM((4, 256, 512), F32),
            shape((4, 256, 512), BF16),
            shape((2, 2, 256, 32), F32),
        ),
        in_specs=[VMEM] * 5,
        out_specs=(VMEM, HBM, VMEM, VMEM),
        scratch_shapes=[pltpu.VMEM((4, 256, 512), F32), pltpu.SemaphoreType.DMA((8,))],
        compiler_params=params(12),
        cost_estimate=cost(3 << 30, 10 << 20),
        name="inner",
    )(features, ylo, yhi, table, band)
    faces, edge_slope, hidden, coarse = pl.pallas_call(
        outer_kernel,
        out_shape=(
            shape((2, 128, 256), BF16),
            shape((256, 128), F32),
            pltpu.HBM((4, 256, 512), BF16),
            pltpu.HBM((1024, 256), BF16),
        ),
        in_specs=[VMEM] * 7,
        out_specs=(VMEM, VMEM, HBM, HBM),
        scratch_shapes=[
            pltpu.VMEM((512, 512), F32),
            pltpu.VMEM((2, 1024, 128), F32),
            pltpu.VMEM((4, 256, 512), BF16),
            pltpu.VMEM((1024, 256), BF16),
            pltpu.SemaphoreType.DMA((3,)),
        ],
        compiler_params=params(8),
        cost_estimate=cost(1 << 30, 4 << 20),
        name="outer",
    )(zlo, zhi, table, band, pair, edge, hidden)

    mix_weight, cotangent_rows, coarse = lax.optimization_barrier(
        (mix_weight, cotangent.reshape(mine, 256, width), coarse)
    )
    sent = lax.all_to_all(
        coarse.reshape(count_z, mine * 16, 256), "sz", split_axis=0, concat_axis=0, tiled=True
    )
    block = lambda *dims: pl.BlockSpec(dims, lambda c: (c,) + (0,) * (len(dims) - 1))
    shares = count_y // 2
    mix_specs = [
        pl.BlockSpec((count_z, 16, 256), lambda c: (0, c, 0)),
        block(1, width, width),
        block(1, width, 256),
    ]
    mix_t, cotangent_t = pl.pallas_call(
        turn_kernel,
        grid=(mine,),
        out_shape=(shape((mine, width, width), BF16), shape((mine, width, 256), BF16)),
        in_specs=[block(1, width, width), block(1, 256, width)],
        out_specs=(block(1, width, width), block(1, width, 256)),
        compiler_params=params(4),
        cost_estimate=cost(1 << 20, 2 << 20),
        name="turn",
    )(mix_weight, cotangent_rows)
    back = pl.pallas_call(
        mix_kernel,
        out_shape=pltpu.HBM((count_z, mine * 16, 256), BF16),
        in_specs=[VMEM] * 4,
        out_specs=HBM,
        scratch_shapes=[
            pltpu.VMEM((count_z, mine * 16, 256), BF16),
            pltpu.SemaphoreType.DMA((mine,)),
        ],
        compiler_params=params(8),
        cost_estimate=cost(mine * 2 * 2 * 256 * width * width, 2 << 20),
        name="mix",
    )(sent, mix_weight, cotangent_t, mix_t)
    coarse_grad = lax.all_to_all(back, "sz", split_axis=0, concat_axis=0, tiled=True)
    sent, back = lax.optimization_barrier((sent, back))
    mid, *mix_parts = pl.pallas_call(
        lambda *refs: mix_grad_kernel(1.0 / math.sqrt(8 * 32 * count_y), *refs),
        grid=(mine,),
        out_shape=[shape((mine, 256, width), BF16)]
        + [
            pltpu.HBM((mine, width // shares, width), BF16 if k else F32) for k in range(shares)
        ],
        in_specs=[pl.BlockSpec(memory_space=pltpu.SMEM)] + mix_specs,
        out_specs=[block(1, 256, width)] + [block(1, width // shares, width)] * shares,
        scratch_shapes=[pltpu.VMEM((width, width), F32)],
        compiler_params=params(8),
        cost_estimate=cost(mine * 2 * 2 * 256 * width * width, 3 << 20),
        name="mix_grad",
    )(lax.axis_index("sy")[None], sent, mix_weight, cotangent_t)
    mix_sum = mix_parts[0]
    moved = []
    for k, part in enumerate(mix_parts[1:], 1):
        moved.append(lax.ppermute(part, "sy", [(i, i ^ (2 * k)) for i in range(count_y)]))
    cells = 16 * 64 * count_y * 32 * count_z
    sums = pl.pallas_call(
        lambda *refs: backward_kernel(
            1.0 / math.sqrt(cells // 8), 1.0 / math.sqrt(cells), *refs
        ),
        out_shape=shape((128, 128), F32),
        in_specs=[VMEM, HBM, HBM, HBM] + [VMEM] * 4,
        out_specs=VMEM,
        scratch_shapes=[
            pltpu.VMEM((512, 512), F32),
            pltpu.VMEM((2, 1024, 128), F32),
            pltpu.VMEM((256, 2048), BF16),
            pltpu.VMEM((512, 128), F32),
            pltpu.VMEM((17, 2, 128, 256), BF16),
            pltpu.VMEM((4, 256, 512), F32),
            pltpu.VMEM((4, 256, 512), BF16),
            pltpu.SemaphoreType.DMA((3,)),
        ],
        compiler_params=params(12),
        cost_estimate=cost(4 << 30, 8 << 20),
        name="backward",
    )(
        coarse_grad.reshape(1024, 256),
        *kept(embedded, slope, hidden),
        pair,
        pair_t,
        faces,
        edge_slope,
    )
    *moved, sums = lax.optimization_barrier((*moved, sums))
    for part in moved:
        mix_sum = mix_sum + part.astype(F32)
    mine_last, other = jnp.split(mix_sum, 2, axis=1)
    other = lax.ppermute(other.astype(BF16), "sy", [(i, i ^ 1) for i in range(count_y)])
    mix_grad = mine_last + other.astype(F32)

    rounds = sum_rounds(count_y, count_z)
    for masks in rounds[:-1]:
        parts = [sums] + exchanged(sums, masks, count_y * count_z)
        sums = parts[0] + parts[1] if len(parts) == 2 else (parts[0] + parts[1]) + (parts[2] + parts[3])
    down_grad, conv_grad = pl.pallas_call(
        finish_kernel,
        out_shape=(shape((8, 16, 64), F32), shape((256, 27), F32)),
        in_specs=[VMEM] * 4,
        out_specs=(VMEM,) * 2,
        compiler_params=params(8),
        cost_estimate=cost(1 << 20, 1 << 18),
        name="finish",
    )(sums, *exchanged(sums, rounds[-1], count_y * count_z))
    down_grad = jnp.transpose(down_grad, (0, 2, 1))
    conv_grad = jnp.transpose(conv_grad.reshape(16, 16, 27), (2, 0, 1))
    return (mid.reshape(cotangent.shape), mix_grad, down_grad, conv_grad)


def solution(mesh):
    in_specs = (
        P(None, "sy", "sz"),
        P(None, "sy", "sz"),
        P(),
        P(),
        P(),
        P(),
        P("sz", None, None),
        P("sz", None, "sy", None),
    )
    out_specs = (P("sz", None, "sy", None), P("sz", "sy", None), P(), P())
    return jax.shard_map(
        per_device, mesh=mesh, in_specs=in_specs, out_specs=out_specs, check_vma=False
    )
```
